32 devices in a mesh: shard: 4 (over z), tensor: 4 (over x, core), dp: 2 (over y).
Axes of the slice: x: 2, y: 2, z: 4, core: 2. Of those that a mesh axis runs over, the one named last changes fastest.
Arguments:
- gradient: bfloat16 [1, 8192, 8192], P(None, 'shard', ('tensor', 'dp')), may hold values from -16 to 16
- momentum: float32 [1, 8192, 8192], P(None, 'shard', ('tensor', 'dp')), may hold values from -16 to 16
- prior_right_factor: float32 [1, 8192, 128], P(None, ('tensor', 'dp')), may hold values from -8 to 8
Outputs:
- momentum_next: float32 [1, 8192, 8192], P(None, 'shard', ('tensor', 'dp'))
- following_right_factor: float32 [1, 8192, 128], P(None, ('tensor', 'dp'))
- direction: bfloat16 [1, 8192, 8192], P(None, 'shard', ('tensor', 'dp'))
The draws below stay inside these ranges and needn't reach their ends.
All inputs are finite; a program needn't handle non-finite values.
Results may differ from the reference program's by a relative error of at most 0.0029.
Values sent between devices are 32-bit elements; how exact they have to be, the bound alone decides.
A program may use at most 64 MiB of HBM per device.

```python
import math
import jax
import jax.numpy as jnp
from jax import lax

M = 8192
N = 8192
R = 128
LAYERS = 1


def orthonormal_columns(seed_key, row_count, col_count):
    gaussian = jax.random.normal(seed_key, (LAYERS, row_count, col_count), jnp.float32)

    def orthonormalize(matrix):
        q_matrix, r_matrix = jnp.linalg.qr(matrix)
        return q_matrix
    return jax.vmap(orthonormalize)(gaussian)


def shared_factors(key):
    left_vectors = jax.random.normal(jax.random.fold_in(key, 11), (LAYERS, M, R), jnp.float32) / math.sqrt(M)
    joint_columns = orthonormal_columns(jax.random.fold_in(key, 12), N, 2 * R)
    mixing = orthonormal_columns(jax.random.fold_in(key, 13), R, R)
    positions = jnp.arange(R, dtype=jnp.float32) / max(R - 1, 1)
    jitter = jax.random.uniform(jax.random.fold_in(key, 14), (LAYERS, R), jnp.float32, 0.9, 1.1)
    strengths = jnp.power(2000.0, -positions)[None, :] * jitter
    strengths = strengths * (0.95 * math.sqrt(M * N) / jnp.sqrt(jnp.sum(strengths * strengths, axis=1, keepdims=True)))
    momentum_share = jax.random.uniform(jax.random.fold_in(key, 15), (LAYERS, R), jnp.float32, 0.55, 0.9)
    row_scales = jnp.ones((LAYERS, M), jnp.float32)
    return (left_vectors, joint_columns, mixing, strengths, momentum_share, row_scales)


def blended_piece(key, stream_tag, use_share, tail_scale):
    left_vectors, joint_columns, mixing, strengths, momentum_share, row_scales = shared_factors(key)
    singular_vectors = joint_columns[:, :, :R]
    if use_share:
        weights = momentum_share
    else:
        weights = 1.0 - momentum_share
    rescaled_update = left_vectors * (strengths * weights)[:, None, :]
    rank_limited = jnp.einsum('fwd,fad->fwa', rescaled_update, singular_vectors, precision=lax.Precision.HIGHEST)
    noise_key = jax.random.fold_in(key, stream_tag)
    random_perturbation = jax.random.normal(noise_key, (LAYERS, M, N), jnp.float32)
    basis_component = jnp.einsum('aph,aht->apt', random_perturbation, joint_columns, precision=lax.Precision.HIGHEST)
    residual_portion = random_perturbation - jnp.einsum('fwd,fad->fwa', basis_component, joint_columns, precision=lax.Precision.HIGHEST)
    return row_scales[:, :, None] * (rank_limited + tail_scale * residual_portion)


def draw_momentum(key, part):
    return jnp.clip(blended_piece(key, 21, True, 0.08), -16.0, 16.0)


def draw_gradient(key, part):
    return jnp.clip(blended_piece(key, 22, False, 0.06), -16.0, 16.0).astype(jnp.bfloat16)


def draw_prior_right_factor(key, part):
    left_vectors, joint_columns, mixing, strengths, momentum_share, row_scales = shared_factors(key)
    singular_vectors = joint_columns[:, :, :R]
    other_vectors = joint_columns[:, :, R:]
    aligned = jnp.einsum('lnr,lrs->lns', singular_vectors, mixing, precision=lax.Precision.HIGHEST)
    tilt = math.sqrt(0.5)
    factor = math.sqrt(N) * (tilt * aligned + tilt * other_vectors)
    return jnp.clip(factor, -8.0, 8.0)


def setup_inputs(seed: int = 0) -> dict:
    keys = jax.random.split(jax.random.key(seed), 4)
    return {
        "gradient": draw_gradient(jax.random.fold_in(keys[3], 71), 0),
        "momentum": draw_momentum(jax.random.fold_in(keys[3], 71), 0),
        "prior_right_factor": draw_prior_right_factor(jax.random.fold_in(keys[3], 71), 0),
    }


decay_rate = 0.95
epsilon = 1e-06

def one_layer(operands):
    gradient, momentum, prior_right_factor = operands
    mixed_update = momentum + gradient.astype(jnp.float32)
    left = jnp.dot(mixed_update, prior_right_factor, precision=lax.Precision.HIGHEST)
    q_matrix, r_matrix = jnp.linalg.qr(left)
    column_basis = q_matrix * jnp.sign(jnp.diagonal(r_matrix))[None, :]
    fresh_right_factor = jnp.dot(mixed_update.T, column_basis, precision=lax.Precision.HIGHEST)
    momentum_next = mixed_update - (1.0 - decay_rate) * jnp.dot(column_basis, fresh_right_factor.T, precision=lax.Precision.HIGHEST)
    scales = jnp.sqrt(lax.optimization_barrier(jnp.mean(fresh_right_factor * fresh_right_factor, axis=0)) + epsilon)
    following_right_factor = fresh_right_factor / scales[None, :]
    direction = (jnp.sqrt(M / R) * jnp.dot(column_basis, following_right_factor.T, precision=lax.Precision.HIGHEST)).astype(jnp.bfloat16)
    return (momentum_next, following_right_factor, direction)

def reference(gradient, momentum, prior_right_factor):
    momentum_next, following_right_factor, direction = lax.map(one_layer, (gradient, momentum, prior_right_factor))
    return (momentum_next, following_right_factor, direction)
```

```python
import functools

import jax
import jax.numpy as jnp
from jax import lax
from jax.experimental import pallas as pl
from jax.experimental.pallas import tpu as pltpu
from jax.sharding import PartitionSpec as P

MESH = pl.DeviceIdType.MESH
HIGHEST = lax.Precision.HIGHEST
decay_rate = 0.95
epsilon = 1e-06
CHUNKS = 8
STEPS = 8


def dot(a, b, dims, precision=HIGHEST):
    return lax.dot_general(
        a, b, (dims, ((), ())), precision=precision, preferred_element_type=jnp.float32
    )


def split(value):
    high = value.astype(jnp.bfloat16)
    low = (value - high.astype(jnp.float32)).astype(jnp.bfloat16)
    return high, low


def product(lhs, rhs):
    high, low = split(lhs)
    pair = jnp.concatenate(split(rhs), axis=1)
    both = dot(high, pair, ((1,), (0,)), None) + dot(low, pair, ((1,), (0,)), None)
    width = rhs.shape[1]
    return both[:, :width] + both[:, width:]


def inverse_factor(gram):
    size = gram.shape[0]
    sub = lax.broadcasted_iota(jnp.int32, (8, size), 0)
    lane = lax.broadcasted_iota(jnp.int32, (8, size), 1)
    rows = lax.broadcasted_iota(jnp.int32, (size, size), 0)
    lanes = lax.broadcasted_iota(jnp.int32, (size, size), 1)

    def row(value, index):
        return jnp.broadcast_to(value[index : index + 1], value.shape)

    def block(step, a):
        top = a[:8]
        columns = [jnp.broadcast_to(top[:, c : c + 1], (8, size)) for c in range(8)]
        panel = jnp.where(lane < 8, jnp.where(lane == sub, 1.0, 0.0), top)
        scale = jnp.zeros((8, size), jnp.float32)
        for c in range(8):
            inverse_root = lax.rsqrt(row(columns[c], c))
            scale = jnp.where(sub == c, inverse_root, scale)
            factor = jnp.where(sub > c, columns[c] * (inverse_root * inverse_root), 0.0)
            panel = panel - factor * row(panel, c)
            for j in range(c + 1, 8):
                columns[j] = columns[j] - factor * row(columns[j], c)
        square = scale * scale
        solved = panel * square
        for c in range(7, 0, -1):
            solved = solved - jnp.where(sub < c, columns[c] * square, 0.0) * row(solved, c)
        active = rows < size - 8 * step
        source = jnp.where(active, a, 0.0)[8:]
        rest = jnp.where(active & (lanes < 8), 0.0, a)[8:]
        for c in range(8):
            rest = rest - jnp.broadcast_to(source[:, c : c + 1], rest.shape) * jnp.broadcast_to(
                solved[c : c + 1], rest.shape
            )
        return pltpu.roll(jnp.concatenate([rest, panel * scale], axis=0), size - 8, 1)

    return jnp.where(rows >= lanes, lax.fori_loop(0, size // 8, block, gram), 0.0)


class Group:
    def __init__(self, count, me, where):
        self.count, self.me, self.where = count, me, where

    def peer(self, k):
        other = lax.rem(self.me + k, self.count)
        return other, self.where(other)


def groups(shape):
    s, t, d = lax.axis_index("shard"), lax.axis_index("tensor"), lax.axis_index("dp")
    tensor, dp = shape["tensor"], shape["dp"]
    cores = 2 if tensor % 2 == 0 else 1
    core, x = lax.rem(t, cores), lax.div(t, cores)
    return {
        "core": Group(cores, core, lambda j: {"tensor": x * cores + j}),
        "x": Group(tensor // cores, x, lambda j: {"tensor": j * cores + core}),
        "y": Group(dp, d, lambda j: {"dp": j}),
        "z": Group(shape["shard"], s, lambda j: {"shard": j}),
        "plane": Group(
            tensor * dp, t * dp + d, lambda j: {"tensor": lax.div(j, dp), "dp": lax.rem(j, dp)}
        ),
    }


def stage_plan(shape, rows):
    cores = 2 if shape["tensor"] % 2 == 0 else 1
    sizes = {"core": cores, "x": shape["tensor"] // cores, "y": shape["dp"]}
    members = shape["tensor"] * shape["dp"]
    halves = 2 if rows % (16 * members) == 0 else 1
    orders = (("core", "x", "y"), ("core", "y", "x"))[:halves]
    return sizes, halves, orders


def factors(shape, momentum_ref, gradient_ref, prior_ref, mixed, basis_ref, right_ref, following_ref, *scratch):
    (raw, left, whole, local, pieces, piece_in, piece_z, piece_all, shares, share_in, squares, load_sem,
     gram_send, gram_recv, share_send,
     share_recv, full_send, full_recv, square_send, square_recv, prior_vmem,
     prior_sem, *stages) = scratch
    rows, cols = mixed.shape
    rank = prior_ref.shape[1]
    where = groups(shape)
    sizes, halves, orders = stage_plan(shape, rows)
    part = rows // CHUNKS

    def load(i):
        at = pl.ds(pl.multiple_of(i * part, 8), part)
        return (
            pltpu.make_async_copy(momentum_ref.at[at], mixed.at[at], load_sem.at[0, i]),
            pltpu.make_async_copy(gradient_ref.at[at], raw.at[at], load_sem.at[1, i]),
        )

    prior_copy = pltpu.make_async_copy(prior_ref, prior_vmem, prior_sem)
    prior_copy.start()
    for i in range(CHUNKS):
        for copy in load(i):
            copy.start()

    barrier = pltpu.get_barrier_semaphore()
    peers = 0
    for name in ("plane", "z"):
        for k in range(1, where[name].count):
            pl.semaphore_signal(barrier, inc=1, device_id=where[name].peer(k)[1], device_id_type=MESH)
            peers += 1
    pl.semaphore_wait(barrier, peers)

    plane, z = where["plane"], where["z"]
    piece = rank // plane.count

    def summed(slots, count):
        total = slots[0]
        for i in range(1, count):
            total = total + slots[i]
        return total

    def sends(group, turn, stage, source, target):
        copies = []
        for k in range(1, group.count):
            other, device = group.peer(k)
            copy = pltpu.make_async_remote_copy(
                src_ref=source(other),
                dst_ref=target,
                send_sem=gram_send.at[turn, stage, k - 1],
                recv_sem=gram_recv.at[turn, stage, k - 1],
                device_id=device,
                device_id_type=MESH,
            )
            copy.start()
            copies.append(copy)
        return copies

    def gram_steps(turn, values):
        gram = sum(dot(value, value, ((0,), (0,))) for value in values)
        for i in range(plane.count):
            pieces[turn, i] = gram[i * piece : (i + 1) * piece]
        piece_in[turn, plane.me] = pieces[turn, plane.me]
        copies = sends(plane, turn, 0, lambda i: pieces.at[turn, i], piece_in.at[turn, plane.me])
        yield
        for copy in copies:
            copy.wait()
        piece_z[turn, z.me] = summed(piece_in.at[turn], plane.count)
        own = piece_z.at[turn, z.me]
        copies = sends(z, turn, 1, lambda i: own, own)
        yield
        for copy in copies:
            copy.wait()
        piece_all[turn, plane.me] = summed(piece_z.at[turn], z.count)
        own = piece_all.at[turn, plane.me]
        copies = sends(plane, turn, 2, lambda i: own, own)
        yield
        for copy in copies:
            copy.wait()
        yield jnp.concatenate([piece_all[turn, i] for i in range(plane.count)], axis=0)

    prior_copy.wait()
    prior = prior_vmem[...]

    def first(i, carry):
        for copy in load(i):
            copy.wait()
        at = pl.ds(pl.multiple_of(i * part, 8), part)
        value = mixed[at, :] + raw[at, :].astype(jnp.float32)
        mixed[at, :] = value
        left[at, :] = product(value, prior)
        return carry

    lax.fori_loop(0, CHUNKS, first, 0)

    starts = [h * (rows // halves) for h in range(halves)]
    sizes_now = [rows // halves] * halves
    trail = []
    for level in range(3):
        pending = []
        for h in range(halves):
            name = orders[h][level]
            group = where[name]
            buffer, send_sem, recv_sem = stages[level * 6 + h * 3 : level * 6 + h * 3 + 3] if halves == 2 else stages[level * 3 : level * 3 + 3]
            if group.count == 1:
                continue
            size = sizes_now[h] // group.count
            copies = []
            for k in range(1, group.count):
                other, device = group.peer(k)
                copy = pltpu.make_async_remote_copy(
                    src_ref=left.at[pl.ds(pl.multiple_of(starts[h] + other * size, 8), size)],
                    dst_ref=buffer.at[k - 1],
                    send_sem=send_sem.at[k - 1],
                    recv_sem=recv_sem.at[k - 1],
                    device_id=device,
                    device_id_type=MESH,
                )
                copy.start()
                copies.append(copy)
            pending.append((h, group, size, copies, buffer))
        for h, group, size, copies, buffer in pending:
            for copy in copies:
                copy.wait()
            own = pl.multiple_of(starts[h] + group.me * size, 8)
            total = left[pl.ds(own, size), :]
            for k in range(group.count - 1):
                total = total + buffer[k]
            left[pl.ds(own, size), :] = total
            starts[h], sizes_now[h] = own, size
            trail.append((level, h, group, own, size))
    for h in range(halves):
        own = pl.ds(starts[h], sizes_now[h])
        whole[own, :] = left[own, :]
    for level in (2, 1, 0):
        copies = []
        for stage, h, group, own, size in trail:
            if stage != level:
                continue
            index = (level * 2 + h) if halves == 2 else level
            for k in range(1, group.count):
                other, device = group.peer(k)
                at = pl.ds(own, size)
                copy = pltpu.make_async_remote_copy(
                    src_ref=whole.at[at],
                    dst_ref=whole.at[at],
                    send_sem=full_send.at[index, k - 1],
                    recv_sem=full_recv.at[index, k - 1],
                    device_id=device,
                    device_id_type=MESH,
                )
                copy.start()
                copies.append(copy)
        if level == 2:
            steps = gram_steps(0, [left[pl.ds(starts[h], sizes_now[h]), :] for h in range(halves)])
            next(steps)
        elif level == 1:
            next(steps)
        else:
            next(steps)
            inverse = inverse_factor(next(steps))
            owned = [
                dot(left[pl.ds(starts[h], sizes_now[h]), :], inverse, ((1,), (1,))) for h in range(halves)
            ]
            steps = gram_steps(1, owned)
            next(steps)
        for copy in copies:
            copy.wait()

    def exchange(slots, group, send_sem, recv_sem):
        copies = []
        for k in range(1, group.count):
            copy = pltpu.make_async_remote_copy(
                src_ref=slots.at[group.me],
                dst_ref=slots.at[group.me],
                send_sem=send_sem.at[k - 1],
                recv_sem=recv_sem.at[k - 1],
                device_id=group.peer(k)[1],
                device_id_type=MESH,
            )
            copy.start()
            copies.append(copy)
        return copies

    value = dot(whole[...], inverse, ((1,), (1,)))
    basis_ref[...] = value
    next(steps)
    high, low = split(value)
    half = cols // 2
    for c in range(2):
        wide_high, wide_low = split(mixed[:, c * half : (c + 1) * half])
        both = dot(jnp.concatenate([high, low], axis=1), wide_high, ((0,), (0,)), None)
        local[:, c * half : (c + 1) * half] = (
            both[:rank] + both[rank:] + dot(high, wide_low, ((0,), (0,)), None)
        )
        if c == 0:
            next(steps)
    share = rank // z.count
    share_copies = []
    for k in range(1, z.count):
        other, device = z.peer(k)
        copy = pltpu.make_async_remote_copy(
            src_ref=local.at[pl.ds(pl.multiple_of(other * share, 8), share)],
            dst_ref=share_in.at[k - 1],
            send_sem=share_send.at[k - 1],
            recv_sem=share_recv.at[k - 1],
            device_id=device,
            device_id_type=MESH,
        )
        copy.start()
        share_copies.append(copy)
    inverse = inverse_factor(next(steps))
    for copy in share_copies:
        copy.wait()
    total = local[pl.ds(pl.multiple_of(z.me * share, 8), share), :]
    for k in range(z.count - 1):
        total = total + share_in[k]
    shares[z.me] = total
    full = exchange(shares, z, full_send.at[full_send.shape[0] - 1], full_recv.at[full_recv.shape[0] - 1])
    basis_ref[...] = dot(basis_ref[...], inverse, ((1,), (1,)))
    for copy in full:
        copy.wait()
    stacked = jnp.concatenate([shares[i] for i in range(z.count)], axis=0)
    right = dot(stacked, inverse, ((0,), (1,)))
    right_ref[...] = right
    squares[plane.me] = jnp.broadcast_to(jnp.sum(right * right, axis=0, keepdims=True), (8, rank))
    for copy in exchange(squares, plane, square_send, square_recv):
        copy.wait()
    mean = summed(squares, plane.count)[:1] / (cols * plane.count)
    following_ref[...] = right / jnp.sqrt(mean + epsilon)


def finish(scale, mixed_ref, basis_ref, right_ref, following_ref, next_ref, direction_ref, out_ref,
           next_vmem, direction_vmem, sems):
    rows = mixed_ref.shape[0]
    block = rows // STEPS
    out = pltpu.make_async_copy(following_ref, out_ref, sems.at[2, 0])
    out.start()
    right = (right_ref[...] * (decay_rate - 1.0)).astype(jnp.bfloat16)
    follow = (following_ref[...] * scale).astype(jnp.bfloat16)
    follow = jnp.concatenate([follow, follow], axis=1)
    dims = ((1,), (1,))
    copies = [out]
    for i in range(STEPS):
        at = pl.ds(i * block, block)
        high, low = split(basis_ref[at, :])
        next_vmem[at, :] = mixed_ref[at, :] + dot(high, right, dims, None)
        copy = pltpu.make_async_copy(next_vmem.at[at], next_ref.at[at], sems.at[0, i])
        copy.start()
        copies.append(copy)
        pair = jnp.concatenate([high, low], axis=1)
        direction_vmem[at, :] = dot(pair, follow, dims, None).astype(jnp.bfloat16)
        copy = pltpu.make_async_copy(direction_vmem.at[at], direction_ref.at[at], sems.at[1, i])
        copy.start()
        copies.append(copy)
    for copy in copies:
        copy.wait()


def shards(shape, gradient, momentum, prior_right_factor):
    gradient, momentum, prior = gradient[0], momentum[0], prior_right_factor[0]
    rows, cols = momentum.shape
    rank = prior.shape[1]
    sizes, halves, orders = stage_plan(shape, rows)
    stages = []
    now = [rows // halves] * halves
    widest = max(max(sizes.values()), shape["shard"], 2) - 1
    for level in range(3):
        for h in range(halves):
            count = sizes[orders[h][level]]
            now[h] //= count
            stages += [
                pltpu.VMEM((max(count - 1, 1), now[h], rank), jnp.float32),
                pltpu.SemaphoreType.DMA((max(count - 1, 1),)),
                pltpu.SemaphoreType.DMA((max(count - 1, 1),)),
            ]
    z = shape["shard"]
    plane = shape["tensor"] * shape["dp"]
    dma = pltpu.SemaphoreType.DMA
    vmem = pl.BlockSpec(memory_space=pltpu.VMEM)
    hbm = pl.BlockSpec(memory_space=pltpu.HBM)
    f32 = jnp.float32
    mixed, basis, right, following = pl.pallas_call(
        functools.partial(factors, shape),
        out_shape=[
            pltpu.VMEM((rows, cols), f32),
            pltpu.VMEM((rows, rank), f32),
            pltpu.VMEM((cols, rank), f32),
            pltpu.VMEM((cols, rank), f32),
        ],
        in_specs=[hbm, hbm, hbm],
        out_specs=[vmem, vmem, vmem, vmem],
        scratch_shapes=[
            pltpu.VMEM((rows, cols), jnp.bfloat16),
            pltpu.VMEM((rows, rank), f32),
            pltpu.VMEM((rows, rank), f32),
            pltpu.VMEM((rank, cols), f32),
            pltpu.VMEM((2, plane, rank // plane, rank), f32),
            pltpu.VMEM((2, plane, rank // plane, rank), f32),
            pltpu.VMEM((2, z, rank // plane, rank), f32),
            pltpu.VMEM((2, plane, rank // plane, rank), f32),
            pltpu.VMEM((z, rank // z, cols), f32),
            pltpu.VMEM((max(z - 1, 1), rank // z, cols), f32),
            pltpu.VMEM((plane, 8, rank), f32),
            dma((2, CHUNKS)),
            dma((2, 3, max(plane, z))),
            dma((2, 3, max(plane, z))),
            dma((max(z - 1, 1),)),
            dma((max(z - 1, 1),)),
            dma((3 * halves + 1, widest)),
            dma((3 * halves + 1, widest)),
            dma((max(plane - 1, 1),)),
            dma((max(plane - 1, 1),)),
            pltpu.VMEM((cols, rank), f32),
            dma,
            *stages,
        ],
        compiler_params=pltpu.CompilerParams(
            collective_id=0, has_side_effects=True, vmem_limit_bytes=40 * 1024 * 1024
        ),
        name="factors",
    )(*(pltpu.with_memory_space_constraint(x, pltpu.HBM) for x in (momentum, gradient, prior)))

    scale = float((rows * z / rank) ** 0.5)
    momentum_next, direction, following = pl.pallas_call(
        functools.partial(finish, scale),
        out_shape=[
            jax.ShapeDtypeStruct((rows, cols), f32),
            jax.ShapeDtypeStruct((rows, cols), jnp.bfloat16),
            jax.ShapeDtypeStruct((cols, rank), f32),
        ],
        in_specs=[vmem, vmem, vmem, vmem],
        out_specs=[hbm, hbm, hbm],
        scratch_shapes=[
            pltpu.VMEM((rows, cols), f32),
            pltpu.VMEM((rows, cols), jnp.bfloat16),
            dma((3, STEPS)),
        ],
        compiler_params=pltpu.CompilerParams(vmem_limit_bytes=32 * 1024 * 1024),
        name="finish",
    )(mixed, basis, right, following)
    return momentum_next[None], following[None], direction[None]


def solution(mesh):
    return jax.shard_map(
        functools.partial(shards, dict(mesh.shape)),
        mesh=mesh,
        in_specs=(
            P(None, "shard", ("tensor", "dp")),
            P(None, "shard", ("tensor", "dp")),
            P(None, ("tensor", "dp"), None),
        ),
        out_specs=(
            P(None, "shard", ("tensor", "dp")),
            P(None, ("tensor", "dp"), None),
            P(None, "shard", ("tensor", "dp")),
        ),
        check_vma=False,
    )
```

```python
import functools

import jax
import jax.numpy as jnp
from jax import lax
from jax.experimental import pallas as pl
from jax.experimental.pallas import tpu as pltpu
from jax.sharding import PartitionSpec as P

MESH = pl.DeviceIdType.MESH
HIGHEST = lax.Precision.HIGHEST
decay_rate = 0.95
epsilon = 1e-06
STEPS = 8
MiB = 1024 * 1024
ROWS, NORMAL, TURNED = ((0,), (0,)), ((1,), (0,)), ((1,), (1,))


def dot(a, b, dims, precision=None):
    return lax.dot_general(
        a, b, (dims, ((), ())), precision=precision, preferred_element_type=jnp.float32
    )


def split(value):
    high = value.astype(jnp.bfloat16)
    low = (value - high.astype(jnp.float32)).astype(jnp.bfloat16)
    return high, low


def split3(value):
    high = value.astype(jnp.bfloat16)
    rest = value - high.astype(jnp.float32)
    middle = rest.astype(jnp.bfloat16)
    return high, middle, (rest - middle.astype(jnp.float32)).astype(jnp.bfloat16)


def inverse_steps(a, start, stop):
    size = a.shape[0]
    sub = lax.broadcasted_iota(jnp.int32, (8, size), 0)
    lane = lax.broadcasted_iota(jnp.int32, (8, size), 1)
    rows = lax.broadcasted_iota(jnp.int32, (size, size), 0)
    lanes = lax.broadcasted_iota(jnp.int32, (size, size), 1)

    def row(value, index):
        return jnp.broadcast_to(value[index : index + 1], value.shape)

    def block(step, a):
        top = a[:8]
        columns = [jnp.broadcast_to(top[:, c : c + 1], (8, size)) for c in range(8)]
        panel = jnp.where(lane < 8, jnp.where(lane == sub, 1.0, 0.0), top)
        scale = jnp.zeros((8, size), jnp.float32)
        for c in range(8):
            inverse_root = lax.rsqrt(row(columns[c], c))
            scale = jnp.where(sub == c, inverse_root, scale)
            factor = jnp.where(sub > c, columns[c] * (inverse_root * inverse_root), 0.0)
            panel = panel - factor * row(panel, c)
            for j in range(c + 1, 8):
                columns[j] = columns[j] - factor * row(columns[j], c)
        square = scale * scale
        solved = panel * square
        for c in range(7, 0, -1):
            solved = solved - jnp.where(sub < c, columns[c] * square, 0.0) * row(solved, c)
        active = rows < size - 8 * step
        source = jnp.where(active, a, 0.0)[8:]
        rest = jnp.where(active & (lanes < 8), 0.0, a)[8:]
        for c in range(8):
            rest = rest - jnp.broadcast_to(source[:, c : c + 1], rest.shape) * jnp.broadcast_to(
                solved[c : c + 1], rest.shape
            )
        return pltpu.roll(jnp.concatenate([rest, panel * scale], axis=0), size - 8, 1)

    return lax.fori_loop(start, stop, block, a)


def lower(a):
    rows = lax.broadcasted_iota(jnp.int32, a.shape, 0)
    lanes = lax.broadcasted_iota(jnp.int32, a.shape, 1)
    return jnp.where(rows >= lanes, a, 0.0)


def remote(src, dst, send_sem, recv_sem, device):
    return pltpu.make_async_remote_copy(
        src_ref=src, dst_ref=dst, send_sem=send_sem, recv_sem=recv_sem, device_id=device, device_id_type=MESH
    )


def widths(cols):
    group = 256 if cols % 256 == 0 else cols
    chunk = 128 if group % 128 == 0 else group
    return group, chunk


def factors(shape, momentum_ref, gradient_ref, prior_ref, mixed, pair_ref, right_ref, following_ref,
            raw, wide_high, wide_low, prior_vmem, left, core_in, plane_in, whole, turned, value_t, sums, totals,
            arrive, pieces, piece_in, piece_z, piece_all, squares, load_sem, prior_sem, core_send, core_recv,
            plane_send, plane_recv, ag_send, ag_recv, half_sem, gram_send, gram_recv, chain_send, chain_recv,
            square_send, square_recv):
    rows, cols = mixed.shape
    rank = prior_ref.shape[1]
    depth, dp = shape["shard"], shape["dp"]
    cores = 2 if shape["tensor"] % 2 == 0 else 1
    nx = shape["tensor"] // cores
    chips = nx * dp
    plane = chips * cores
    own = rows // plane
    s, t, y = lax.axis_index("shard"), lax.axis_index("tensor"), lax.axis_index("dp")
    core, x = lax.rem(t, cores), lax.div(t, cores)
    me = t * dp + y

    def chip(offset):
        px = lax.rem(x + lax.div(offset, dp), nx)
        py = lax.rem(y + lax.rem(offset, dp), dp)
        return px * dp + py, {"tensor": px * cores + core, "dp": py}

    def place(half, index):
        return pl.ds(pl.multiple_of((half * chips + index) * own, 8), own)

    def peer(k):
        other = lax.rem(me + k, plane)
        return other, {"tensor": lax.div(other, dp), "dp": lax.rem(other, dp)}

    def across(k):
        other = lax.rem(s + k, depth)
        return other, {"shard": other}

    partner = {"tensor": x * cores + cores - 1 - core}
    halves = (core,) if cores == 1 else (1 - core, core)

    def load(slot, at):
        return (
            pltpu.make_async_copy(momentum_ref.at[at], mixed.at[at], load_sem.at[0, slot]),
            pltpu.make_async_copy(gradient_ref.at[at], raw.at[at], load_sem.at[1, slot]),
        )

    prior_copy = pltpu.make_async_copy(prior_ref, prior_vmem, prior_sem)
    prior_copy.start()
    for h, half in enumerate(halves):
        for i in range(chips):
            for copy in load(h * chips + i, place(half, chip(chips - 1 - i)[0])):
                copy.start()

    barrier = pltpu.get_barrier_semaphore()
    for k in range(1, plane):
        pl.semaphore_signal(barrier, inc=1, device_id=peer(k)[1], device_id_type=MESH)
    for k in range(1, depth):
        pl.semaphore_signal(barrier, inc=1, device_id=across(k)[1], device_id_type=MESH)

    half_depth = max(depth // 2, 1)
    first = s < half_depth
    level = jnp.where(first, s, depth - 1 - s)
    outer = level > 0
    middle = level == half_depth - 1
    step_in = jnp.where(first, 1, -1)
    group, chunk = widths(cols)
    count = cols // chunk

    prior_copy.wait()
    prior_pair = jnp.concatenate(split(prior_vmem[...]), axis=1)
    pl.semaphore_wait(barrier, plane + depth - 2)

    def product(slot, at):
        for copy in load(slot, at):
            copy.wait()
        value = mixed[at, :] + raw[at, :].astype(jnp.float32)
        mixed[at, :] = value
        high, low = split(value)
        wide_high[at, :] = high
        wide_low[at, :] = low
        both = dot(high, prior_pair, NORMAL) + dot(low, prior_pair, NORMAL)
        return both[:, :rank] + both[:, rank:]

    def core_copy(i):
        at = place(cores - 1 - core, chip(chips - 1 - i)[0])
        return remote(left.at[at], core_in.at[i], core_send.at[i], core_recv.at[i], partner)

    def plane_copy(offset):
        index, device = chip(offset)
        slot = offset - 1
        return remote(left.at[place(core, index)], plane_in.at[slot], plane_send.at[slot], plane_recv.at[slot], device)

    if cores == 2:

        def outgoing(i, carry):
            at = place(1 - core, chip(chips - 1 - i)[0])
            left[at, :] = product(i, at)
            core_copy(i).start()
            return carry

        with jax.named_scope("p1_other"):
            lax.fori_loop(0, chips, outgoing, 0)

    def kept(i, carry):
        offset = chips - 1 - i
        at = place(core, chip(offset)[0])
        value = product((cores - 1) * chips + i, at)
        if cores == 2:
            core_copy(i).wait_recv()
            value = value + core_in[i]
        left[at, :] = value

        @pl.when(offset > 0)
        def _():
            plane_copy(offset).start()

        return carry

    with jax.named_scope("p2_own"):
        lax.fori_loop(0, chips, kept, 0)

    mine = place(core, x * dp + y)
    with jax.named_scope("p3_rswait"):
        total = left[mine, :]
        for offset in range(1, chips):
            plane_copy(offset).wait_recv()
            total = total + plane_in[offset - 1]
        whole[mine, :] = total

    piece = rank // plane

    def summed(slots, n):
        value = slots[0]
        for i in range(1, n):
            value = value + slots[i]
        return value

    def gram_sends(turn, stage, n, find, source, target):
        copies = []
        for k in range(1, n):
            other, device = find(k)
            copy = remote(source(other), target, gram_send.at[turn, stage, k - 1],
                          gram_recv.at[turn, stage, k - 1], device)
            copy.start()
            copies.append(copy)
        return copies

    def gram_steps(turn, gram):
        for i in range(plane):
            pieces[turn, i] = gram[i * piece : (i + 1) * piece]
        piece_in[turn, me] = pieces[turn, me]
        copies = gram_sends(turn, 0, plane, peer, lambda i: pieces.at[turn, i], piece_in.at[turn, me])
        yield
        for copy in copies:
            copy.wait()
        piece_z[turn, s] = summed(piece_in.at[turn], plane)
        mine_z = piece_z.at[turn, s]
        copies = gram_sends(turn, 1, depth, across, lambda i: mine_z, mine_z)
        yield
        for copy in copies:
            copy.wait()
        piece_all[turn, me] = summed(piece_z.at[turn], depth)
        mine_all = piece_all.at[turn, me]
        copies = gram_sends(turn, 2, plane, peer, lambda i: mine_all, mine_all)
        yield
        for copy in copies:
            copy.wait()
        yield jnp.concatenate([piece_all[turn, i] for i in range(plane)], axis=0)

    with jax.named_scope("p4_gram"):
        steps = gram_steps(0, dot(total, total, ROWS, HIGHEST))
        next(steps)
    spread = []
    for offset in range(1, chips):
        copy = remote(whole.at[mine], whole.at[mine], ag_send.at[offset - 1], ag_recv.at[offset - 1], chip(offset)[1])
        copy.start()
        spread.append(copy)
    with jax.named_scope("p5_gram1"):
        next(steps)
    with jax.named_scope("p6_gram2"):
        next(steps)
    with jax.named_scope("p7_agwait"):
        for offset in range(1, chips):
            plane_copy(offset).wait_send()
        for copy in spread:
            copy.wait()
        if cores == 2:
            for i in range(chips):
                core_copy(i).wait_send()
            at = pl.ds(pl.multiple_of(core * (rows // 2), 8), rows // 2)
            half_copy = remote(whole.at[at], whole.at[at], half_sem.at[0], half_sem.at[1], partner)
            half_copy.start()
    with jax.named_scope("p8_gram3"):
        gram = next(steps)
    with jax.named_scope("p9_inv1"):
        inverse = lower(inverse_steps(gram, 0, rank // 8))
    with jax.named_scope("q0_value"):
        if cores == 2:
            half_copy.wait()
        w_high, w_middle, w_low = split3(inverse)
        ends = jnp.concatenate(
            [jnp.concatenate([w_high, w_middle], axis=1), jnp.concatenate([w_middle, w_high], axis=1)], axis=0
        )
        tail = jnp.concatenate([w_low, w_high], axis=1)
        for i in range(STEPS):
            block = rows // STEPS
            at = slice(i * block, (i + 1) * block)
            high, middle_part, low = split3(whole[at, :])
            both = dot(ends, jnp.concatenate([high, middle_part], axis=1), TURNED)
            value = both[:rank] + (both[rank:] + dot(tail, jnp.concatenate([high, low], axis=1), TURNED))
            value_t[:, at] = value
            high, low = split(value)
            turned[:rank, at] = high
            turned[rank:, at] = low
    with jax.named_scope("q1_gram"):
        begin = pl.multiple_of((core * chips + x * dp + y) * own, 128 if own % 128 == 0 else 8)
        if own % 128 == 0:
            part = value_t[:, pl.ds(begin, own)]
            gram = dot(part, part, TURNED, HIGHEST)
        else:
            part = dot(whole[mine, :], inverse, TURNED, HIGHEST)
            gram = dot(part, part, ROWS, HIGHEST)
        steps = gram_steps(1, gram)
        next(steps)

    def inward(c):
        slot = jnp.where(middle, 1, 0)
        return remote(sums.at[c], arrive.at[slot, c], chain_send.at[0, c], chain_recv.at[slot, c],
                      {"shard": s + step_in})

    def outward(c):
        return remote(totals.at[c], arrive.at[1, c], chain_send.at[1, c], chain_recv.at[1, c],
                      {"shard": s - step_in})

    def landed(slot, c):
        return remote(sums.at[c], arrive.at[slot, c], chain_send.at[0, c], chain_recv.at[slot, c],
                      {"shard": s + step_in})

    def near(c):
        if depth > 1:

            @pl.when(outer)
            def _():
                landed(0, c).wait_recv()
                sums[c] = sums[c] + arrive[0, c]
                inward(c).start()

    def far(c):
        if depth > 1:
            landed(1, c).wait_recv()
            totals[c] = jnp.where(middle, sums[c] + arrive[1, c], arrive[1, c])

            @pl.when(outer)
            def _():
                outward(c).start()
        else:
            totals[c] = sums[c]

    per = group // chunk
    groups = cols // group
    with jax.named_scope("q2_right"):
        for g in range(groups):
            at = slice(g * group, (g + 1) * group)
            both = dot(turned[...], wide_high[:, at], NORMAL)
            value = both[:rank] + both[rank:] + dot(turned[:rank], wide_low[:, at], NORMAL)
            for i in range(per):
                c = g * per + i
                sums[c] = value[:, i * chunk : (i + 1) * chunk]
                if depth > 1:

                    @pl.when(jnp.logical_not(outer))
                    def _():
                        inward(c).start()

            if g == min(1, groups - 1):
                with jax.named_scope("q2_gram1"):
                    next(steps)

    blocks = rank // 8
    state = {}

    def gram_second():
        with jax.named_scope("q4_gram2"):
            next(steps)

    def gram_third():
        with jax.named_scope("q4_gram3"):
            state["a"] = next(steps)
            state["at"] = 0

    def invert(share):
        with jax.named_scope("q5_inv2"):
            stop = min(state["at"] + share, blocks)
            state["a"] = inverse_steps(state["a"], state["at"], stop)
            state["at"] = stop

    def correct(c):
        with jax.named_scope("q7_right"):
            value = dot(totals[c], state["inverse"], ((0,), (1,)), HIGHEST)
            right_ref[c * chunk : (c + 1) * chunk, :] = value
            state["squares"] = state.get("squares", 0.0) + jnp.sum(value * value, axis=0, keepdims=True)

    def basis():
        with jax.named_scope("q6_basis"):
            inverse = state["inverse"]
            high, low = split(inverse)
            left_pair = jnp.concatenate([high, low], axis=1)
            for i in range(STEPS):
                block = rows // STEPS
                at = slice(i * block, (i + 1) * block)
                value = dot(
                    left_pair, jnp.concatenate([turned[:rank, at], turned[:rank, at]], axis=0), NORMAL
                ) + dot(high, turned[rank:, at], NORMAL)
                high_t, low_t = split(value.T)
                pair_ref[at, :rank] = high_t
                pair_ref[at, rank:] = low_t

    lag = min(3, count - 1)
    with jax.named_scope("q3_near"):
        for c in range(lag):
            near(c)
    gram_second()
    with jax.named_scope("q3_chain"):
        done = 0
        for c in range(count):
            if c + lag < count:
                near(c + lag)
            if c == min(3, count - 1):
                gram_third()
            if "a" in state and state["at"] < blocks:
                invert(-(-blocks // min(4, count)) if c < count - 1 else blocks)
                if state["at"] == blocks and "inverse" not in state:
                    state["inverse"] = lower(state["a"])
                    basis()
            far(c)
            if "inverse" in state:
                while done <= c:
                    correct(done)
                    done += 1
    with jax.named_scope("q8_squares"):
        squares[me] = jnp.broadcast_to(state["squares"], (8, rank))
        copies = []
        for k in range(1, plane):
            copy = remote(squares.at[me], squares.at[me], square_send.at[k - 1], square_recv.at[k - 1], peer(k)[1])
            copy.start()
            copies.append(copy)
    with jax.named_scope("q9_momentum"):
        scaled = (right_ref[...] * (decay_rate - 1.0)).astype(jnp.bfloat16)

        def update(i, carry):
            block = rows // STEPS
            at = pl.ds(pl.multiple_of(i * block, 8), block)
            mixed[at, :] = mixed[at, :] + dot(pair_ref[at, :rank], scaled, TURNED)
            return carry

        lax.fori_loop(0, STEPS, update, 0)
    with jax.named_scope("r0_follow"):
        for copy in copies:
            copy.wait()
        mean = summed(squares, plane)[:1] / (cols * plane)
        following_ref[...] = right_ref[...] / jnp.sqrt(mean + epsilon)
        if depth > 1:
            for c in range(count):
                inward(c).wait_send()

            @pl.when(outer)
            def _():
                for c in range(count):
                    outward(c).wait_send()


def finish(scale, mixed_ref, pair_ref, following_ref, next_ref, direction_ref, out_ref, direction_vmem, sems):
    rows = mixed_ref.shape[0]
    rank = following_ref.shape[1]
    block = rows // STEPS
    copies = [pltpu.make_async_copy(following_ref, out_ref, sems.at[2, 0])]
    for i in range(STEPS):
        at = pl.ds(i * block, block)
        copies.append(pltpu.make_async_copy(mixed_ref.at[at], next_ref.at[at], sems.at[0, i]))
    for copy in copies:
        copy.start()
    high, low = split(following_ref[...] * scale)
    follow = jnp.concatenate([high, high], axis=1)
    for i in range(STEPS):
        at = pl.ds(i * block, block)
        value = dot(pair_ref[at, :], follow, TURNED) + dot(pair_ref[at, :rank], low, TURNED)
        direction_vmem[at, :] = value.astype(jnp.bfloat16)
        copy = pltpu.make_async_copy(direction_vmem.at[at], direction_ref.at[at], sems.at[1, i])
        copy.start()
        copies.append(copy)
    for copy in copies:
        copy.wait()


def shards(shape, gradient, momentum, prior_right_factor):
    gradient, momentum, prior = gradient[0], momentum[0], prior_right_factor[0]
    rows, cols = momentum.shape
    rank = prior.shape[1]
    z = shape["shard"]
    plane = shape["tensor"] * shape["dp"]
    cores = 2 if shape["tensor"] % 2 == 0 else 1
    chips = plane // cores
    own = rows // plane
    group, chunk = widths(cols)
    count = cols // chunk
    dma = pltpu.SemaphoreType.DMA
    vmem = pl.BlockSpec(memory_space=pltpu.VMEM)
    hbm = pl.BlockSpec(memory_space=pltpu.HBM)
    f32, bf16 = jnp.float32, jnp.bfloat16
    others = max(chips - 1, 1)
    most = max(plane, z)
    mixed, pair, right, following = pl.pallas_call(
        functools.partial(factors, shape),
        out_shape=[
            pltpu.VMEM((rows, cols), f32),
            pltpu.VMEM((rows, 2 * rank), bf16),
            pltpu.VMEM((cols, rank), f32),
            pltpu.VMEM((cols, rank), f32),
        ],
        in_specs=[hbm, hbm, hbm],
        out_specs=[vmem, vmem, vmem, vmem],
        scratch_shapes=[
            pltpu.VMEM((rows, cols), bf16),
            pltpu.VMEM((rows, cols), bf16),
            pltpu.VMEM((rows, cols), bf16),
            pltpu.VMEM((cols, rank), f32),
            pltpu.VMEM((rows, rank), f32),
            pltpu.VMEM((chips, own, rank), f32),
            pltpu.VMEM((others, own, rank), f32),
            pltpu.VMEM((rows, rank), f32),
            pltpu.VMEM((2 * rank, rows), bf16),
            pltpu.VMEM((rank, rows), f32),
            pltpu.VMEM((count, rank, chunk), f32),
            pltpu.VMEM((count, rank, chunk), f32),
            pltpu.VMEM((2, count, rank, chunk), f32),
            pltpu.VMEM((2, plane, rank // plane, rank), f32),
            pltpu.VMEM((2, plane, rank // plane, rank), f32),
            pltpu.VMEM((2, z, rank // plane, rank), f32),
            pltpu.VMEM((2, plane, rank // plane, rank), f32),
            pltpu.VMEM((plane, 8, rank), f32),
            dma((2, plane)),
            dma,
            dma((chips,)),
            dma((chips,)),
            dma((others,)),
            dma((others,)),
            dma((others,)),
            dma((others,)),
            dma((2,)),
            dma((2, 3, most)),
            dma((2, 3, most)),
            dma((2, count)),
            dma((2, count)),
            dma((most,)),
            dma((most,)),
        ],
        compiler_params=pltpu.CompilerParams(
            collective_id=0, has_side_effects=True, vmem_limit_bytes=36 * MiB
        ),
        name="factors",
    )(*(pltpu.with_memory_space_constraint(x, pltpu.HBM) for x in (momentum, gradient, prior)))

    scale = float((rows * z / rank) ** 0.5)
    momentum_next, direction, following = pl.pallas_call(
        functools.partial(finish, scale),
        out_shape=[
            jax.ShapeDtypeStruct((rows, cols), f32),
            jax.ShapeDtypeStruct((rows, cols), bf16),
            jax.ShapeDtypeStruct((cols, rank), f32),
        ],
        in_specs=[vmem, vmem, vmem],
        out_specs=[hbm, hbm, hbm],
        scratch_shapes=[pltpu.VMEM((rows, cols), bf16), dma((3, STEPS))],
        compiler_params=pltpu.CompilerParams(vmem_limit_bytes=24 * MiB),
        name="finish",
    )(mixed, pair, following)
    return momentum_next[None], following[None], direction[None]


def solution(mesh):
    return jax.shard_map(
        functools.partial(shards, dict(mesh.shape)),
        mesh=mesh,
        in_specs=(
            P(None, "shard", ("tensor", "dp")),
            P(None, "shard", ("tensor", "dp")),
            P(None, ("tensor", "dp"), None),
        ),
        out_specs=(
            P(None, "shard", ("tensor", "dp")),
            P(None, ("tensor", "dp"), None),
            P(None, "shard", ("tensor", "dp")),
        ),
        check_vma=False,
    )
```

```python
import functools

import jax
import jax.numpy as jnp
from jax import lax
from jax.experimental import pallas as pl
from jax.experimental.pallas import tpu as pltpu
from jax.sharding import PartitionSpec as P

MESH = pl.DeviceIdType.MESH
HIGHEST = lax.Precision.HIGHEST
decay_rate = 0.95
epsilon = 1e-06
STEPS = 8
AHEAD = 3
LAG = 5
THIRD = 4
SHARE = 1
MiB = 1024 * 1024
ROWS, NORMAL, TURNED = ((0,), (0,)), ((1,), (0,)), ((1,), (1,))


def dot(a, b, dims, precision=None):
    return lax.dot_general(
        a, b, (dims, ((), ())), precision=precision, preferred_element_type=jnp.float32
    )


def split(value):
    high = value.astype(jnp.bfloat16)
    low = (value - high.astype(jnp.float32)).astype(jnp.bfloat16)
    return high, low


def split3(value):
    high = value.astype(jnp.bfloat16)
    rest = value - high.astype(jnp.float32)
    middle = rest.astype(jnp.bfloat16)
    return high, middle, (rest - middle.astype(jnp.float32)).astype(jnp.bfloat16)


def inverse_steps(a, start, stop):
    size = a.shape[0]
    sub = lax.broadcasted_iota(jnp.int32, (8, size), 0)
    lane = lax.broadcasted_iota(jnp.int32, (8, size), 1)
    rows = lax.broadcasted_iota(jnp.int32, (size, size), 0)
    lanes = lax.broadcasted_iota(jnp.int32, (size, size), 1)

    def row(value, index):
        return jnp.broadcast_to(value[index : index + 1], value.shape)

    def block(step, a):
        top = a[:8]
        columns = [jnp.broadcast_to(top[:, c : c + 1], (8, size)) for c in range(8)]
        panel = jnp.where(lane < 8, jnp.where(lane == sub, 1.0, 0.0), top)
        scale = jnp.zeros((8, size), jnp.float32)
        for c in range(8):
            inverse_root = lax.rsqrt(row(columns[c], c))
            scale = jnp.where(sub == c, inverse_root, scale)
            factor = jnp.where(sub > c, columns[c] * (inverse_root * inverse_root), 0.0)
            panel = panel - factor * row(panel, c)
            for j in range(c + 1, 8):
                columns[j] = columns[j] - factor * row(columns[j], c)
        square = scale * scale
        solved = panel * square
        for c in range(7, 0, -1):
            solved = solved - jnp.where(sub < c, columns[c] * square, 0.0) * row(solved, c)
        active = rows < size - 8 * step
        source = jnp.where(active, a, 0.0)[8:]
        rest = jnp.where(active & (lanes < 8), 0.0, a)[8:]
        for c in range(8):
            rest = rest - jnp.broadcast_to(source[:, c : c + 1], rest.shape) * jnp.broadcast_to(
                solved[c : c + 1], rest.shape
            )
        return pltpu.roll(jnp.concatenate([rest, panel * scale], axis=0), size - 8, 1)

    return lax.fori_loop(start, stop, block, a)


def lower(a):
    rows = lax.broadcasted_iota(jnp.int32, a.shape, 0)
    lanes = lax.broadcasted_iota(jnp.int32, a.shape, 1)
    return jnp.where(rows >= lanes, a, 0.0)


def remote(src, dst, send_sem, recv_sem, device):
    return pltpu.make_async_remote_copy(
        src_ref=src, dst_ref=dst, send_sem=send_sem, recv_sem=recv_sem, device_id=device, device_id_type=MESH
    )


def widths(cols):
    group = 256 if cols % 256 == 0 else cols
    chunk = 128 if group % 128 == 0 else group
    return group, chunk


def factors(shape, momentum_ref, gradient_ref, prior_ref, mixed, pair_ref, right_ref, following_ref,
            raw, wide_high, wide_low, prior_vmem, prior_pair, left, core_in, plane_in, whole, turned, value_t, sums, totals,
            arrive, pieces, piece_in, piece_z, piece_all, squares, work, load_sem, prior_sem, core_send, core_recv,
            plane_send, plane_recv, ag_send, ag_recv, half_sem, gram_send, gram_recv, chain_send, chain_recv,
            square_send, square_recv):
    rows, cols = mixed.shape
    rank = prior_ref.shape[1]
    depth, dp = shape["shard"], shape["dp"]
    cores = 2 if shape["tensor"] % 2 == 0 else 1
    nx = shape["tensor"] // cores
    chips = nx * dp
    plane = chips * cores
    own = rows // plane
    s, t, y = lax.axis_index("shard"), lax.axis_index("tensor"), lax.axis_index("dp")
    core, x = lax.rem(t, cores), lax.div(t, cores)
    me = t * dp + y

    def chip(offset):
        px = lax.rem(x + lax.div(offset, dp), nx)
        py = lax.rem(y + lax.rem(offset, dp), dp)
        return px * dp + py, {"tensor": px * cores + core, "dp": py}

    def place(half, index):
        return pl.ds(pl.multiple_of((half * chips + index) * own, 8), own)

    def peer(k):
        other = lax.rem(me + k, plane)
        return other, {"tensor": lax.div(other, dp), "dp": lax.rem(other, dp)}

    def across(k):
        other = lax.rem(s + k, depth)
        return other, {"shard": other}

    partner = {"tensor": x * cores + cores - 1 - core}

    def load(slot, at):
        return (
            pltpu.make_async_copy(momentum_ref.at[at], mixed.at[at], load_sem.at[0, slot]),
            pltpu.make_async_copy(gradient_ref.at[at], raw.at[at], load_sem.at[1, slot]),
        )

    loads = chips * cores

    def spot(slot):
        i = lax.div(slot, cores)
        half = lax.rem(core + 1 + lax.rem(slot, cores), cores)
        return place(half, chip(chips - 1 - i)[0])

    prior_copy = pltpu.make_async_copy(prior_ref, prior_vmem, prior_sem)
    prior_copy.start()
    for slot in range(min(AHEAD, loads)):
        for copy in load(slot, spot(slot)):
            copy.start()

    barrier = pltpu.get_barrier_semaphore()
    for k in range(1, plane):
        pl.semaphore_signal(barrier, inc=1, device_id=peer(k)[1], device_id_type=MESH)
    for k in range(1, depth):
        pl.semaphore_signal(barrier, inc=1, device_id=across(k)[1], device_id_type=MESH)

    half_depth = max(depth // 2, 1)
    first = s < half_depth
    level = jnp.where(first, s, depth - 1 - s)
    outer = level > 0
    middle = level == half_depth - 1
    step_in = jnp.where(first, 1, -1)
    group, chunk = widths(cols)
    count = cols // chunk

    prior_copy.wait()
    high, low = split(prior_vmem[...])
    prior_pair[:, :rank] = high
    prior_pair[:, rank:] = low
    pl.semaphore_wait(barrier, plane + depth - 2)

    def product(slot, at):
        for copy in load(slot, at):
            copy.wait()
        ahead = slot + AHEAD

        @pl.when(ahead < loads)
        def _():
            for copy in load(ahead, spot(ahead)):
                copy.start()

        value = mixed[at, :] + raw[at, :].astype(jnp.float32)
        mixed[at, :] = value
        high, low = split(value)
        wide_high[at, :] = high
        wide_low[at, :] = low
        both = dot(high, prior_pair[...], NORMAL) + dot(low, prior_pair[...], NORMAL)
        return both[:, :rank] + both[:, rank:]

    def core_copy(i):
        at = place(cores - 1 - core, chip(chips - 1 - i)[0])
        return remote(left.at[at], core_in.at[i], core_send.at[i], core_recv.at[i], partner)

    def plane_copy(offset):
        index, device = chip(offset)
        slot = offset - 1
        return remote(left.at[place(core, index)], plane_in.at[slot], plane_send.at[slot], plane_recv.at[slot], device)

    def settle(i):
        offset = chips - 1 - i
        at = place(core, chip(offset)[0])
        if cores == 2:
            core_copy(i).wait_recv()
            left[at, :] = left[at, :] + core_in[i]
        return offset

    def partial(slot, carry):
        i = lax.div(slot, cores)
        at = spot(slot)
        left[at, :] = product(slot, at)
        if cores == 2:

            @pl.when(lax.rem(slot, cores) == 0)
            def _():
                core_copy(i).start()

        @pl.when(jnp.logical_and(lax.rem(slot, cores) == 0, slot > 0))
        def _():
            plane_copy(settle(i - 1)).start()

        return carry

    with jax.named_scope("p1_left"):
        lax.fori_loop(0, loads, partial, 0)

    mine = place(core, x * dp + y)
    with jax.named_scope("p3_rswait"):
        settle(chips - 1)
        total = left[mine, :]
        for offset in range(1, chips):
            plane_copy(offset).wait_recv()
            total = total + plane_in[offset - 1]
        whole[mine, :] = total

    piece = rank // plane

    def summed(slots, n):
        value = slots[0]
        for i in range(1, n):
            value = value + slots[i]
        return value

    def gram_sends(turn, stage, n, find, source, target):
        copies = []
        for k in range(1, n):
            other, device = find(k)
            copy = remote(source(other), target, gram_send.at[turn, stage, k - 1],
                          gram_recv.at[turn, stage, k - 1], device)
            copy.start()
            copies.append(copy)
        return copies

    def gram_steps(turn, gram):
        for i in range(plane):
            pieces[turn, i] = gram[i * piece : (i + 1) * piece]
        piece_in[turn, me] = pieces[turn, me]
        copies = gram_sends(turn, 0, plane, peer, lambda i: pieces.at[turn, i], piece_in.at[turn, me])
        yield
        for copy in copies:
            copy.wait()
        piece_z[turn, s] = summed(piece_in.at[turn], plane)
        mine_z = piece_z.at[turn, s]
        copies = gram_sends(turn, 1, depth, across, lambda i: mine_z, mine_z)
        yield
        for copy in copies:
            copy.wait()
        piece_all[turn, me] = summed(piece_z.at[turn], depth)
        mine_all = piece_all.at[turn, me]
        copies = gram_sends(turn, 2, plane, peer, lambda i: mine_all, mine_all)
        yield copies

    def gram_whole(turn, copies):
        for copy in copies:
            copy.wait()
        return jnp.concatenate([piece_all[turn, i] for i in range(plane)], axis=0)

    with jax.named_scope("p4_gram"):
        steps = gram_steps(0, dot(total, total, ROWS, HIGHEST))
        next(steps)
    spread = []
    for offset in range(1, chips):
        copy = remote(whole.at[mine], whole.at[mine], ag_send.at[offset - 1], ag_recv.at[offset - 1], chip(offset)[1])
        copy.start()
        spread.append(copy)
    with jax.named_scope("p5_gram1"):
        next(steps)
    with jax.named_scope("p6_gram2"):
        last = next(steps)
    with jax.named_scope("p7_agwait"):
        for offset in range(1, chips):
            plane_copy(offset).wait_send()
        for copy in spread:
            copy.wait()
        if cores == 2:
            for i in range(chips):
                core_copy(i).wait_send()
            at = pl.ds(pl.multiple_of(core * (rows // 2), 8), rows // 2)
            half_copy = remote(whole.at[at], whole.at[at], half_sem.at[0], half_sem.at[1], partner)
            half_copy.start()
    with jax.named_scope("p8_gram3"):
        gram = gram_whole(0, last)
    with jax.named_scope("p9_inv1"):
        inverse = lower(inverse_steps(gram, 0, rank // 8))
    with jax.named_scope("q0_value"):
        if cores == 2:
            half_copy.wait()
        w_high, w_middle, w_low = split3(inverse)
        ends = jnp.concatenate(
            [jnp.concatenate([w_high, w_middle], axis=1), jnp.concatenate([w_middle, w_high], axis=1)], axis=0
        )
        tail = jnp.concatenate([w_low, w_high], axis=1)
        for i in range(STEPS):
            block = rows // STEPS
            at = slice(i * block, (i + 1) * block)
            high, middle_part, low = split3(whole[at, :])
            both = dot(ends, jnp.concatenate([high, middle_part], axis=1), TURNED)
            value = both[:rank] + (both[rank:] + dot(tail, jnp.concatenate([high, low], axis=1), TURNED))
            value_t[:, at] = value
            high, low = split(value)
            turned[:rank, at] = high
            turned[rank:, at] = low
    with jax.named_scope("q1_gram"):
        begin = pl.multiple_of((core * chips + x * dp + y) * own, 128 if own % 128 == 0 else 8)
        if own % 128 == 0:
            part = value_t[:, pl.ds(begin, own)]
            gram = dot(part, part, TURNED, HIGHEST)
        else:
            part = dot(whole[mine, :], inverse, TURNED, HIGHEST)
            gram = dot(part, part, ROWS, HIGHEST)
        steps = gram_steps(1, gram)
        next(steps)

    parts = 2 if rank % 16 == 0 else 1
    tall = rank // parts
    units = count * parts

    def unit(ref, u):
        return ref.at[u // parts, pl.ds((u % parts) * tall, tall)]

    def inward(u):
        slot = jnp.where(middle, 1, 0)
        return remote(unit(sums, u), unit(arrive.at[slot], u), chain_send.at[0, u], chain_recv.at[slot, u],
                      {"shard": s + step_in})

    def outward(u):
        return remote(unit(totals, u), unit(arrive.at[1], u), chain_send.at[1, u], chain_recv.at[1, u],
                      {"shard": s - step_in})

    def landed(slot, u):
        remote(unit(sums, u), unit(arrive.at[slot], u), chain_send.at[0, u], chain_recv.at[slot, u],
               {"shard": s + step_in}).wait_recv()

    def near(u):
        if depth > 1:

            @pl.when(outer)
            def _():
                landed(0, u)
                unit(sums, u)[...] = unit(sums, u)[...] + unit(arrive.at[0], u)[...]
                inward(u).start()

    def far(u):
        if depth > 1:
            landed(1, u)
            got = unit(arrive.at[1], u)[...]
            unit(totals, u)[...] = jnp.where(middle, unit(sums, u)[...] + got, got)

            @pl.when(outer)
            def _():
                outward(u).start()
        else:
            unit(totals, u)[...] = unit(sums, u)[...]

    per = group // chunk
    groups = cols // group
    with jax.named_scope("q2_right"):
        for g in range(groups):
            at = slice(g * group, (g + 1) * group)
            both = dot(turned[...], wide_high[:, at], NORMAL)
            value = both[:rank] + both[rank:] + dot(turned[:rank], wide_low[:, at], NORMAL)
            for i in range(per):
                sums[g * per + i] = value[:, i * chunk : (i + 1) * chunk]
            if g == min(1, groups - 1):
                with jax.named_scope("q2_gram1"):
                    next(steps)
            if depth > 1:

                @pl.when(jnp.logical_not(outer))
                def _():
                    for u in range(g * per * parts, (g + 1) * per * parts):
                        inward(u).start()

    lag = min(LAG, units)
    last = None
    for u in range(lag):
        if u == max(lag - 2, 0):
            with jax.named_scope("q4_gram2"):
                last = next(steps)
        with jax.named_scope("q3_near"):
            near(u)

    blocks = rank // 8

    def invert(start, stop):
        with jax.named_scope("q5_inv2"):
            work[...] = inverse_steps(work[...], start, stop)

    def basis():
        with jax.named_scope("q6_basis"):
            work[...] = lower(work[...])
            high, low = split(work[...])
            left_pair = jnp.concatenate([high, low], axis=1)
            for i in range(STEPS):
                block = rows // STEPS
                at = slice(i * block, (i + 1) * block)
                value = dot(
                    left_pair, jnp.concatenate([turned[:rank, at], turned[:rank, at]], axis=0), NORMAL
                ) + dot(high, turned[rank:, at], NORMAL)
                high_t, low_t = split(value.T)
                pair_ref[at, :rank] = high_t
                pair_ref[at, rank:] = low_t

    def correct(c):
        with jax.named_scope("q7_right"):
            value = dot(totals[c], work[...], ((0,), (1,)), HIGHEST)
            right_ref[c * chunk : (c + 1) * chunk, :] = value
            column = jnp.sum(value * value, axis=0, keepdims=True)
            squares[me] = squares[me] + jnp.broadcast_to(column, (8, rank))

    squares[me] = jnp.zeros((8, rank), jnp.float32)

    @pl.when(outer)
    def _():
        third = min(THIRD, units - 1)
        at = 0
        for u in range(units):
            with jax.named_scope("q3_far"):
                far(u)
            if u + lag < units:
                with jax.named_scope("q3_near2"):
                    near(u + lag)
            if u == third:
                with jax.named_scope("q4_gram3"):
                    work[...] = gram_whole(1, last)
            if u >= third and at < blocks:
                stop = blocks if u == units - 1 else min(at + SHARE, blocks)
                invert(at, stop)
                at = stop
        basis()
        for c in range(count):
            correct(c)

    @pl.when(jnp.logical_not(outer))
    def _():
        with jax.named_scope("q4_gram3"):
            work[...] = gram_whole(1, last)
        invert(0, blocks)
        basis()
        for u in range(units):
            with jax.named_scope(f"q3_end{u}"):
                far(u)
            if (u + 1) % parts == 0:
                correct(u // parts)

    with jax.named_scope("q8_squares"):
        copies = []
        for k in range(1, plane):
            copy = remote(squares.at[me], squares.at[me], square_send.at[k - 1], square_recv.at[k - 1], peer(k)[1])
            copy.start()
            copies.append(copy)
    with jax.named_scope("q9_momentum"):
        scaled = (right_ref[...] * (decay_rate - 1.0)).astype(jnp.bfloat16)

        def update(i, carry):
            block = rows // STEPS
            at = pl.ds(pl.multiple_of(i * block, 8), block)
            mixed[at, :] = mixed[at, :] + dot(pair_ref[at, :rank], scaled, TURNED)
            return carry

        lax.fori_loop(0, STEPS, update, 0)
    with jax.named_scope("r0_follow"):
        for copy in copies:
            copy.wait()
        mean = summed(squares, plane)[:1] / (cols * plane)
        following_ref[...] = right_ref[...] / jnp.sqrt(mean + epsilon)
        if depth > 1:
            for u in range(units):
                inward(u).wait_send()

            @pl.when(outer)
            def _():
                for u in range(units):
                    outward(u).wait_send()


def finish(scale, mixed_ref, pair_ref, following_ref, next_ref, direction_ref, out_ref, direction_vmem, sems):
    rows = mixed_ref.shape[0]
    rank = following_ref.shape[1]
    block = rows // STEPS
    copies = [pltpu.make_async_copy(following_ref, out_ref, sems.at[2, 0])]
    for i in range(STEPS):
        at = pl.ds(i * block, block)
        copies.append(pltpu.make_async_copy(mixed_ref.at[at], next_ref.at[at], sems.at[0, i]))
    for copy in copies:
        copy.start()
    high, low = split(following_ref[...] * scale)
    follow = jnp.concatenate([high, high], axis=1)
    for i in range(STEPS):
        at = pl.ds(i * block, block)
        value = dot(pair_ref[at, :], follow, TURNED) + dot(pair_ref[at, :rank], low, TURNED)
        direction_vmem[at, :] = value.astype(jnp.bfloat16)
        copy = pltpu.make_async_copy(direction_vmem.at[at], direction_ref.at[at], sems.at[1, i])
        copy.start()
        copies.append(copy)
    for copy in copies:
        copy.wait()


def shards(shape, gradient, momentum, prior_right_factor):
    gradient, momentum, prior = gradient[0], momentum[0], prior_right_factor[0]
    rows, cols = momentum.shape
    rank = prior.shape[1]
    z = shape["shard"]
    plane = shape["tensor"] * shape["dp"]
    cores = 2 if shape["tensor"] % 2 == 0 else 1
    chips = plane // cores
    own = rows // plane
    group, chunk = widths(cols)
    count = cols // chunk
    dma = pltpu.SemaphoreType.DMA
    vmem = pl.BlockSpec(memory_space=pltpu.VMEM)
    hbm = pl.BlockSpec(memory_space=pltpu.HBM)
    f32, bf16 = jnp.float32, jnp.bfloat16
    others = max(chips - 1, 1)
    most = max(plane, z)
    mixed, pair, right, following = pl.pallas_call(
        functools.partial(factors, shape),
        out_shape=[
            pltpu.VMEM((rows, cols), f32),
            pltpu.VMEM((rows, 2 * rank), bf16),
            pltpu.VMEM((cols, rank), f32),
            pltpu.VMEM((cols, rank), f32),
        ],
        in_specs=[hbm, hbm, hbm],
        out_specs=[vmem, vmem, vmem, vmem],
        scratch_shapes=[
            pltpu.VMEM((rows, cols), bf16),
            pltpu.VMEM((rows, cols), bf16),
            pltpu.VMEM((rows, cols), bf16),
            pltpu.VMEM((cols, rank), f32),
            pltpu.VMEM((cols, 2 * rank), bf16),
            pltpu.VMEM((rows, rank), f32),
            pltpu.VMEM((chips, own, rank), f32),
            pltpu.VMEM((others, own, rank), f32),
            pltpu.VMEM((rows, rank), f32),
            pltpu.VMEM((2 * rank, rows), bf16),
            pltpu.VMEM((rank, rows), f32),
            pltpu.VMEM((count, rank, chunk), f32),
            pltpu.VMEM((count, rank, chunk), f32),
            pltpu.VMEM((2, count, rank, chunk), f32),
            pltpu.VMEM((2, plane, rank // plane, rank), f32),
            pltpu.VMEM((2, plane, rank // plane, rank), f32),
            pltpu.VMEM((2, z, rank // plane, rank), f32),
            pltpu.VMEM((2, plane, rank // plane, rank), f32),
            pltpu.VMEM((plane, 8, rank), f32),
            pltpu.VMEM((rank, rank), f32),
            dma((2, plane)),
            dma,
            dma((chips,)),
            dma((chips,)),
            dma((others,)),
            dma((others,)),
            dma((others,)),
            dma((others,)),
            dma((2,)),
            dma((2, 3, most)),
            dma((2, 3, most)),
            dma((2, 2 * count)),
            dma((2, 2 * count)),
            dma((most,)),
            dma((most,)),
        ],
        compiler_params=pltpu.CompilerParams(
            collective_id=0, has_side_effects=True, vmem_limit_bytes=36 * MiB
        ),
        name="factors",
    )(*(pltpu.with_memory_space_constraint(x, pltpu.HBM) for x in (momentum, gradient, prior)))

    scale = float((rows * z / rank) ** 0.5)
    momentum_next, direction, following = pl.pallas_call(
        functools.partial(finish, scale),
        out_shape=[
            jax.ShapeDtypeStruct((rows, cols), f32),
            jax.ShapeDtypeStruct((rows, cols), bf16),
            jax.ShapeDtypeStruct((cols, rank), f32),
        ],
        in_specs=[vmem, vmem, vmem],
        out_specs=[hbm, hbm, hbm],
        scratch_shapes=[pltpu.VMEM((rows, cols), bf16), dma((3, STEPS))],
        compiler_params=pltpu.CompilerParams(vmem_limit_bytes=24 * MiB),
        name="finish",
    )(mixed, pair, following)
    return momentum_next[None], following[None], direction[None]


def solution(mesh):
    return jax.shard_map(
        functools.partial(shards, dict(mesh.shape)),
        mesh=mesh,
        in_specs=(
            P(None, "shard", ("tensor", "dp")),
            P(None, "shard", ("tensor", "dp")),
            P(None, ("tensor", "dp"), None),
        ),
        out_specs=(
            P(None, "shard", ("tensor", "dp")),
            P(None, ("tensor", "dp"), None),
            P(None, "shard", ("tensor", "dp")),
        ),
        check_vma=False,
    )
```

```python
import functools

import jax
import jax.numpy as jnp
from jax import lax
from jax.experimental import pallas as pl
from jax.experimental.pallas import tpu as pltpu
from jax.sharding import PartitionSpec as P

MESH = pl.DeviceIdType.MESH
HIGHEST = lax.Precision.HIGHEST
decay_rate = 0.95
epsilon = 1e-06
STEPS = 8
AHEAD = 3
LAG = 5
THIRD = 4
SHARE = 1
MiB = 1024 * 1024
ROWS, NORMAL, TURNED = ((0,), (0,)), ((1,), (0,)), ((1,), (1,))


def dot(a, b, dims, precision=None):
    return lax.dot_general(
        a, b, (dims, ((), ())), precision=precision, preferred_element_type=jnp.float32
    )


def split(value):
    high = value.astype(jnp.bfloat16)
    low = (value - high.astype(jnp.float32)).astype(jnp.bfloat16)
    return high, low


def split3(value):
    high = value.astype(jnp.bfloat16)
    rest = value - high.astype(jnp.float32)
    middle = rest.astype(jnp.bfloat16)
    return high, middle, (rest - middle.astype(jnp.float32)).astype(jnp.bfloat16)


def inverse_steps(a, start, stop):
    size = a.shape[0]
    sub = lax.broadcasted_iota(jnp.int32, (8, size), 0)
    lane = lax.broadcasted_iota(jnp.int32, (8, size), 1)
    rows = lax.broadcasted_iota(jnp.int32, (size, size), 0)
    lanes = lax.broadcasted_iota(jnp.int32, (size, size), 1)

    def row(value, index):
        return jnp.broadcast_to(value[index : index + 1], value.shape)

    def block(step, a):
        top = a[:8]
        columns = [jnp.broadcast_to(top[:, c : c + 1], (8, size)) for c in range(8)]
        panel = jnp.where(lane < 8, jnp.where(lane == sub, 1.0, 0.0), top)
        scale = jnp.zeros((8, size), jnp.float32)
        for c in range(8):
            inverse_root = lax.rsqrt(row(columns[c], c))
            scale = jnp.where(sub == c, inverse_root, scale)
            factor = jnp.where(sub > c, columns[c] * (inverse_root * inverse_root), 0.0)
            panel = panel - factor * row(panel, c)
            for j in range(c + 1, 8):
                columns[j] = columns[j] - factor * row(columns[j], c)
        square = scale * scale
        solved = panel * square
        for c in range(7, 0, -1):
            solved = solved - jnp.where(sub < c, columns[c] * square, 0.0) * row(solved, c)
        active = rows < size - 8 * step
        source = jnp.where(active, a, 0.0)[8:]
        rest = jnp.where(active & (lanes < 8), 0.0, a)[8:]
        for c in range(8):
            rest = rest - jnp.broadcast_to(source[:, c : c + 1], rest.shape) * jnp.broadcast_to(
                solved[c : c + 1], rest.shape
            )
        return pltpu.roll(jnp.concatenate([rest, panel * scale], axis=0), size - 8, 1)

    return lax.fori_loop(start, stop, block, a)


def lower(a):
    rows = lax.broadcasted_iota(jnp.int32, a.shape, 0)
    lanes = lax.broadcasted_iota(jnp.int32, a.shape, 1)
    return jnp.where(rows >= lanes, a, 0.0)


def remote(src, dst, send_sem, recv_sem, device):
    return pltpu.make_async_remote_copy(
        src_ref=src, dst_ref=dst, send_sem=send_sem, recv_sem=recv_sem, device_id=device, device_id_type=MESH
    )


def widths(cols):
    group = 256 if cols % 256 == 0 else cols
    chunk = 128 if group % 128 == 0 else group
    return group, chunk


def factors(shape, momentum_ref, gradient_ref, prior_ref, mixed, pair_ref, right_ref, following_ref,
            raw, wide_high, wide_low, prior_vmem, prior_pair, left, core_in, plane_in, whole, turned, value_t, sums, totals,
            arrive, pieces, piece_in, piece_z, piece_all, squares, work, load_sem, prior_sem, core_recv, once,
            gram_send, gram_recv, chain_send, chain_recv):
    rows, cols = mixed.shape
    rank = prior_ref.shape[1]
    depth, dp = shape["shard"], shape["dp"]
    cores = 2 if shape["tensor"] % 2 == 0 else 1
    nx = shape["tensor"] // cores
    chips = nx * dp
    plane = chips * cores
    own = rows // plane
    s, t, y = lax.axis_index("shard"), lax.axis_index("tensor"), lax.axis_index("dp")
    core, x = lax.rem(t, cores), lax.div(t, cores)
    me = t * dp + y

    def chip(offset):
        px = lax.rem(x + lax.div(offset, dp), nx)
        py = lax.rem(y + lax.rem(offset, dp), dp)
        return px * dp + py, {"tensor": px * cores + core, "dp": py}

    def place(half, index):
        return pl.ds(pl.multiple_of((half * chips + index) * own, 8), own)

    def peer(k):
        other = lax.rem(me + k, plane)
        return other, {"tensor": lax.div(other, dp), "dp": lax.rem(other, dp)}

    def across(k):
        other = lax.rem(s + k, depth)
        return other, {"shard": other}

    partner = {"tensor": x * cores + cores - 1 - core}

    def load(slot, at):
        return (
            pltpu.make_async_copy(momentum_ref.at[at], mixed.at[at], load_sem.at[0, lax.rem(slot, AHEAD)]),
            pltpu.make_async_copy(gradient_ref.at[at], raw.at[at], load_sem.at[1, lax.rem(slot, AHEAD)]),
        )

    loads = chips * cores

    def spot(slot):
        i = lax.div(slot, cores)
        half = lax.rem(core + 1 + lax.rem(slot, cores), cores)
        return place(half, chip(chips - 1 - i)[0])

    prior_copy = pltpu.make_async_copy(prior_ref, prior_vmem, prior_sem)
    prior_copy.start()
    for slot in range(min(AHEAD, loads)):
        for copy in load(slot, spot(slot)):
            copy.start()

    barrier = pltpu.get_barrier_semaphore()
    for k in range(1, plane):
        pl.semaphore_signal(barrier, inc=1, device_id=peer(k)[1], device_id_type=MESH)
    for k in range(1, depth):
        pl.semaphore_signal(barrier, inc=1, device_id=across(k)[1], device_id_type=MESH)

    half_depth = max(depth // 2, 1)
    first = s < half_depth
    level = jnp.where(first, s, depth - 1 - s)
    outer = level > 0
    middle = level == half_depth - 1
    step_in = jnp.where(first, 1, -1)
    group, chunk = widths(cols)
    count = cols // chunk

    prior_copy.wait()
    high, low = split(prior_vmem[...])
    prior_pair[:, :rank] = high
    prior_pair[:, rank:] = low
    pl.semaphore_wait(barrier, plane + depth - 2)

    def product(slot, at):
        for copy in load(slot, at):
            copy.wait()
        ahead = slot + AHEAD

        @pl.when(ahead < loads)
        def _():
            for copy in load(ahead, spot(ahead)):
                copy.start()

        value = mixed[at, :] + raw[at, :].astype(jnp.float32)
        mixed[at, :] = value
        high, low = split(value)
        wide_high[at, :] = high
        wide_low[at, :] = low
        both = dot(high, prior_pair[...], NORMAL) + dot(low, prior_pair[...], NORMAL)
        return both[:, :rank] + both[:, rank:]

    def core_copy(i):
        at = place(cores - 1 - core, chip(chips - 1 - i)[0])
        return remote(left.at[at], core_in.at[i], once.at[0], core_recv.at[i], partner)

    def plane_copy(offset):
        index, device = chip(offset)
        slot = offset - 1
        return remote(left.at[place(core, index)], plane_in.at[slot], once.at[1], once.at[2], device)

    def bulk(first):
        return remote(plane_in, plane_in, once.at[first], once.at[first + 1], chip(1)[1])

    def settle(i):
        offset = chips - 1 - i
        at = place(core, chip(offset)[0])
        if cores == 2:
            core_copy(i).wait_recv()
            left[at, :] = left[at, :] + core_in[i]
        return offset

    def partial(slot, carry):
        i = lax.div(slot, cores)
        at = spot(slot)
        left[at, :] = product(slot, at)
        if cores == 2:

            @pl.when(lax.rem(slot, cores) == 0)
            def _():
                core_copy(i).start()

        @pl.when(jnp.logical_and(lax.rem(slot, cores) == 0, slot > 0))
        def _():
            plane_copy(settle(i - 1)).start()

        return carry

    with jax.named_scope("p1_left"):
        lax.fori_loop(0, loads, partial, 0)

    mine = place(core, x * dp + y)
    with jax.named_scope("p3_rswait"):
        settle(chips - 1)
        total = left[mine, :]
        if chips > 1:
            bulk(1).wait_recv()
        for offset in range(1, chips):
            total = total + plane_in[offset - 1]
        whole[mine, :] = total

    piece = rank // plane

    def summed(slots, n):
        value = slots[0]
        for i in range(1, n):
            value = value + slots[i]
        return value

    def gram_sends(turn, stage, n, find, source, target):
        for k in range(1, n):
            other, device = find(k)
            remote(source(other), target, gram_send.at[turn, stage], gram_recv.at[turn, stage], device).start()

    def gram_wait(turn, stage, n, find, slots):
        if n > 1:
            part = slots.at[turn, pl.ds(0, n - 1)]
            remote(part, part, gram_send.at[turn, stage], gram_recv.at[turn, stage], find(1)[1]).wait()

    def gram_steps(turn, gram):
        for i in range(plane):
            pieces[turn, i] = gram[i * piece : (i + 1) * piece]
        piece_in[turn, me] = pieces[turn, me]
        gram_sends(turn, 0, plane, peer, lambda i: pieces.at[turn, i], piece_in.at[turn, me])
        yield
        gram_wait(turn, 0, plane, peer, piece_in)
        piece_z[turn, s] = summed(piece_in.at[turn], plane)
        mine_z = piece_z.at[turn, s]
        gram_sends(turn, 1, depth, across, lambda i: mine_z, mine_z)
        yield
        gram_wait(turn, 1, depth, across, piece_z)
        piece_all[turn, me] = summed(piece_z.at[turn], depth)
        mine_all = piece_all.at[turn, me]
        gram_sends(turn, 2, plane, peer, lambda i: mine_all, mine_all)
        yield

    def gram_whole(turn):
        gram_wait(turn, 2, plane, peer, piece_all)
        return jnp.concatenate([piece_all[turn, i] for i in range(plane)], axis=0)

    with jax.named_scope("p4_gram"):
        steps = gram_steps(0, dot(total, total, ROWS, HIGHEST))
        next(steps)
    for offset in range(1, chips):
        remote(whole.at[mine], whole.at[mine], once.at[3], once.at[4], chip(offset)[1]).start()
    with jax.named_scope("p5_gram1"):
        next(steps)
    with jax.named_scope("p6_gram2"):
        next(steps)
    with jax.named_scope("p7_agwait"):
        if chips > 1:
            bulk(1).wait_send()
            bulk(3).wait()
        if cores == 2:
            at = pl.ds(pl.multiple_of(core * (rows // 2), 8), rows // 2)
            remote(left.at[at], left.at[at], once.at[0], once.at[0], partner).wait_send()
            half_copy = remote(whole.at[at], whole.at[at], once.at[5], once.at[6], partner)
            half_copy.start()
    with jax.named_scope("p8_gram3"):
        gram = gram_whole(0)
    with jax.named_scope("p9_inv1"):
        inverse = lower(inverse_steps(gram, 0, rank // 8))
    with jax.named_scope("q0_value"):
        if cores == 2:
            half_copy.wait()
        w_high, w_middle, w_low = split3(inverse)
        ends = jnp.concatenate(
            [jnp.concatenate([w_high, w_middle], axis=1), jnp.concatenate([w_middle, w_high], axis=1)], axis=0
        )
        tail = jnp.concatenate([w_low, w_high], axis=1)
        for i in range(STEPS):
            block = rows // STEPS
            at = slice(i * block, (i + 1) * block)
            high, middle_part, low = split3(whole[at, :])
            both = dot(ends, jnp.concatenate([high, middle_part], axis=1), TURNED)
            value = both[:rank] + (both[rank:] + dot(tail, jnp.concatenate([high, low], axis=1), TURNED))
            value_t[:, at] = value
            high, low = split(value)
            turned[:rank, at] = high
            turned[rank:, at] = low
    with jax.named_scope("q1_gram"):
        begin = pl.multiple_of((core * chips + x * dp + y) * own, 128 if own % 128 == 0 else 8)
        if own % 128 == 0:
            part = value_t[:, pl.ds(begin, own)]
            gram = dot(part, part, TURNED, HIGHEST)
        else:
            part = dot(whole[mine, :], inverse, TURNED, HIGHEST)
            gram = dot(part, part, ROWS, HIGHEST)
        steps = gram_steps(1, gram)
        next(steps)

    parts = 2 if rank % 16 == 0 else 1
    tall = rank // parts
    units = count * parts

    def unit(ref, u):
        return ref.at[u // parts, pl.ds((u % parts) * tall, tall)]

    def inward(u):
        slot = jnp.where(middle, 1, 0)
        return remote(unit(sums, u), unit(arrive.at[slot], u), chain_send.at[0], chain_recv.at[slot, u],
                      {"shard": s + step_in})

    def outward(u):
        return remote(unit(totals, u), unit(arrive.at[1], u), chain_send.at[1], chain_recv.at[1, u],
                      {"shard": s - step_in})

    def landed(slot, u):
        remote(unit(sums, u), unit(arrive.at[slot], u), chain_send.at[0], chain_recv.at[slot, u],
               {"shard": s + step_in}).wait_recv()

    def near(u):
        if depth > 1:

            @pl.when(outer)
            def _():
                landed(0, u)
                unit(sums, u)[...] = unit(sums, u)[...] + unit(arrive.at[0], u)[...]
                inward(u).start()

    def far(u):
        if depth > 1:
            landed(1, u)
            got = unit(arrive.at[1], u)[...]
            unit(totals, u)[...] = jnp.where(middle, unit(sums, u)[...] + got, got)

            @pl.when(outer)
            def _():
                outward(u).start()
        else:
            unit(totals, u)[...] = unit(sums, u)[...]

    per = group // chunk
    groups = cols // group
    with jax.named_scope("q2_right"):
        for g in range(groups):
            at = slice(g * group, (g + 1) * group)
            both = dot(turned[...], wide_high[:, at], NORMAL)
            value = both[:rank] + both[rank:] + dot(turned[:rank], wide_low[:, at], NORMAL)
            for i in range(per):
                sums[g * per + i] = value[:, i * chunk : (i + 1) * chunk]
            if g == min(1, groups - 1):
                with jax.named_scope("q2_gram1"):
                    next(steps)
            if depth > 1:

                @pl.when(jnp.logical_not(outer))
                def _():
                    for u in range(g * per * parts, (g + 1) * per * parts):
                        inward(u).start()

    lag = min(LAG, units)
    for u in range(lag):
        if u == max(lag - 2, 0):
            with jax.named_scope("q4_gram2"):
                next(steps)
        with jax.named_scope("q3_near"):
            near(u)

    blocks = rank // 8

    def invert(start, stop):
        with jax.named_scope("q5_inv2"):
            work[...] = inverse_steps(work[...], start, stop)

    def basis():
        with jax.named_scope("q6_basis"):
            work[...] = lower(work[...])
            high, low = split(work[...])
            left_pair = jnp.concatenate([high, low], axis=1)
            for i in range(STEPS):
                block = rows // STEPS
                at = slice(i * block, (i + 1) * block)
                value = dot(
                    left_pair, jnp.concatenate([turned[:rank, at], turned[:rank, at]], axis=0), NORMAL
                ) + dot(high, turned[rank:, at], NORMAL)
                high_t, low_t = split(value.T)
                pair_ref[at, :rank] = high_t
                pair_ref[at, rank:] = low_t

    def correct(c):
        with jax.named_scope("q7_right"):
            value = dot(totals[c], work[...], ((0,), (1,)), HIGHEST)
            right_ref[c * chunk : (c + 1) * chunk, :] = value
            column = jnp.sum(value * value, axis=0, keepdims=True)
            squares[me] = squares[me] + jnp.broadcast_to(column, (8, rank))

    squares[me] = jnp.zeros((8, rank), jnp.float32)

    @pl.when(outer)
    def _():
        third = min(THIRD, units - 1)
        at = 0
        for u in range(units):
            with jax.named_scope("q3_far"):
                far(u)
            if u + lag < units:
                with jax.named_scope("q3_near2"):
                    near(u + lag)
            if u == third:
                with jax.named_scope("q4_gram3"):
                    work[...] = gram_whole(1)
            if u >= third and at < blocks:
                stop = blocks if u == units - 1 else min(at + SHARE, blocks)
                invert(at, stop)
                at = stop
        basis()
        for c in range(count):
            correct(c)

    @pl.when(jnp.logical_not(outer))
    def _():
        with jax.named_scope("q4_gram3"):
            work[...] = gram_whole(1)
        invert(0, blocks)
        basis()
        for u in range(units):
            with jax.named_scope(f"q3_end{u}"):
                far(u)
            if (u + 1) % parts == 0:
                correct(u // parts)

    with jax.named_scope("q8_squares"):
        for k in range(1, plane):
            remote(squares.at[me], squares.at[me], once.at[7], once.at[8], peer(k)[1]).start()
    with jax.named_scope("q9_momentum"):
        scaled = (right_ref[...] * (decay_rate - 1.0)).astype(jnp.bfloat16)

        def update(i, carry):
            block = rows // STEPS
            at = pl.ds(pl.multiple_of(i * block, 8), block)
            mixed[at, :] = mixed[at, :] + dot(pair_ref[at, :rank], scaled, TURNED)
            return carry

        lax.fori_loop(0, STEPS, update, 0)
    with jax.named_scope("r0_follow"):
        if plane > 1:
            part = squares.at[pl.ds(0, plane - 1)]
            remote(part, part, once.at[7], once.at[8], peer(1)[1]).wait()
        mean = summed(squares, plane)[:1] / (cols * plane)
        following_ref[...] = right_ref[...] / jnp.sqrt(mean + epsilon)
        if depth > 1:
            remote(sums, sums, chain_send.at[0], chain_recv.at[0, 0], {"shard": s + step_in}).wait_send()

            @pl.when(outer)
            def _():
                remote(totals, totals, chain_send.at[1], chain_recv.at[0, 0], {"shard": s - step_in}).wait_send()


def finish(scale, mixed_ref, pair_ref, following_ref, next_ref, direction_ref, out_ref, direction_vmem, sems):
    rows = mixed_ref.shape[0]
    rank = following_ref.shape[1]
    block = rows // STEPS
    moves = (
        pltpu.make_async_copy(mixed_ref, next_ref, sems.at[0]),
        pltpu.make_async_copy(following_ref, out_ref, sems.at[1]),
    )
    for copy in moves:
        copy.start()
    high, low = split(following_ref[...] * scale)
    follow = jnp.concatenate([high, high], axis=1)
    for i in range(STEPS):
        at = pl.ds(i * block, block)
        value = dot(pair_ref[at, :], follow, TURNED) + dot(pair_ref[at, :rank], low, TURNED)
        direction_vmem[at, :] = value.astype(jnp.bfloat16)
        pltpu.make_async_copy(direction_vmem.at[at], direction_ref.at[at], sems.at[2]).start()
    for copy in moves:
        copy.wait()
    pltpu.make_async_copy(direction_vmem, direction_ref, sems.at[2]).wait()


def shards(shape, gradient, momentum, prior_right_factor):
    gradient, momentum, prior = gradient[0], momentum[0], prior_right_factor[0]
    rows, cols = momentum.shape
    rank = prior.shape[1]
    z = shape["shard"]
    plane = shape["tensor"] * shape["dp"]
    cores = 2 if shape["tensor"] % 2 == 0 else 1
    chips = plane // cores
    own = rows // plane
    group, chunk = widths(cols)
    count = cols // chunk
    dma = pltpu.SemaphoreType.DMA
    vmem = pl.BlockSpec(memory_space=pltpu.VMEM)
    hbm = pl.BlockSpec(memory_space=pltpu.HBM)
    f32, bf16 = jnp.float32, jnp.bfloat16
    others = max(chips - 1, 1)
    mixed, pair, right, following = pl.pallas_call(
        functools.partial(factors, shape),
        out_shape=[
            pltpu.VMEM((rows, cols), f32),
            pltpu.VMEM((rows, 2 * rank), bf16),
            pltpu.VMEM((cols, rank), f32),
            pltpu.VMEM((cols, rank), f32),
        ],
        in_specs=[hbm, hbm, hbm],
        out_specs=[vmem, vmem, vmem, vmem],
        scratch_shapes=[
            pltpu.VMEM((rows, cols), bf16),
            pltpu.VMEM((rows, cols), bf16),
            pltpu.VMEM((rows, cols), bf16),
            pltpu.VMEM((cols, rank), f32),
            pltpu.VMEM((cols, 2 * rank), bf16),
            pltpu.VMEM((rows, rank), f32),
            pltpu.VMEM((chips, own, rank), f32),
            pltpu.VMEM((others, own, rank), f32),
            pltpu.VMEM((rows, rank), f32),
            pltpu.VMEM((2 * rank, rows), bf16),
            pltpu.VMEM((rank, rows), f32),
            pltpu.VMEM((count, rank, chunk), f32),
            pltpu.VMEM((count, rank, chunk), f32),
            pltpu.VMEM((2, count, rank, chunk), f32),
            pltpu.VMEM((2, plane, rank // plane, rank), f32),
            pltpu.VMEM((2, plane, rank // plane, rank), f32),
            pltpu.VMEM((2, z, rank // plane, rank), f32),
            pltpu.VMEM((2, plane, rank // plane, rank), f32),
            pltpu.VMEM((plane, 8, rank), f32),
            pltpu.VMEM((rank, rank), f32),
            dma((2, AHEAD)),
            dma,
            dma((chips,)),
            dma((9,)),
            dma((2, 3)),
            dma((2, 3)),
            dma((2,)),
            dma((2, 2 * count)),
        ],
        compiler_params=pltpu.CompilerParams(
            collective_id=0, has_side_effects=True, vmem_limit_bytes=36 * MiB
        ),
        name="factors",
    )(*(pltpu.with_memory_space_constraint(x, pltpu.HBM) for x in (momentum, gradient, prior)))

    scale = float((rows * z / rank) ** 0.5)
    momentum_next, direction, following = pl.pallas_call(
        functools.partial(finish, scale),
        out_shape=[
            jax.ShapeDtypeStruct((rows, cols), f32),
            jax.ShapeDtypeStruct((rows, cols), bf16),
            jax.ShapeDtypeStruct((cols, rank), f32),
        ],
        in_specs=[vmem, vmem, vmem],
        out_specs=[hbm, hbm, hbm],
        scratch_shapes=[pltpu.VMEM((rows, cols), bf16), dma((3,))],
        compiler_params=pltpu.CompilerParams(vmem_limit_bytes=24 * MiB),
        name="finish",
    )(mixed, pair, following)
    return momentum_next[None], following[None], direction[None]


def solution(mesh):
    return jax.shard_map(
        functools.partial(shards, dict(mesh.shape)),
        mesh=mesh,
        in_specs=(
            P(None, "shard", ("tensor", "dp")),
            P(None, "shard", ("tensor", "dp")),
            P(None, ("tensor", "dp"), None),
        ),
        out_specs=(
            P(None, "shard", ("tensor", "dp")),
            P(None, ("tensor", "dp"), None),
            P(None, "shard", ("tensor", "dp")),
        ),
        check_vma=False,
    )
```

```python
import functools

import jax
import jax.numpy as jnp
from jax import lax
from jax.experimental import pallas as pl
from jax.experimental.pallas import tpu as pltpu
from jax.sharding import PartitionSpec as P

MESH = pl.DeviceIdType.MESH
HIGHEST = lax.Precision.HIGHEST
decay_rate = 0.95
epsilon = 1e-06
STEPS = 8
AHEAD = 3
GAP = 5.3
THIRD = 12
SHARE = 2
MOVES = (1, 1, 1, 2, 2, 3)
MiB = 1024 * 1024
ROWS, NORMAL, TURNED = ((0,), (0,)), ((1,), (0,)), ((1,), (1,))


def dot(a, b, dims, precision=None):
    return lax.dot_general(
        a, b, (dims, ((), ())), precision=precision, preferred_element_type=jnp.float32
    )


def split(value):
    high = value.astype(jnp.bfloat16)
    low = (value - high.astype(jnp.float32)).astype(jnp.bfloat16)
    return high, low


def split3(value):
    high = value.astype(jnp.bfloat16)
    rest = value - high.astype(jnp.float32)
    middle = rest.astype(jnp.bfloat16)
    return high, middle, (rest - middle.astype(jnp.float32)).astype(jnp.bfloat16)


def inverse_steps(a, start, stop):
    size = a.shape[0]
    sub = lax.broadcasted_iota(jnp.int32, (8, size), 0)
    lane = lax.broadcasted_iota(jnp.int32, (8, size), 1)
    rows = lax.broadcasted_iota(jnp.int32, (size, size), 0)
    lanes = lax.broadcasted_iota(jnp.int32, (size, size), 1)

    def row(value, index):
        return jnp.broadcast_to(value[index : index + 1], value.shape)

    def block(step, a):
        top = a[:8]
        columns = [jnp.broadcast_to(top[:, c : c + 1], (8, size)) for c in range(8)]
        panel = jnp.where(lane < 8, jnp.where(lane == sub, 1.0, 0.0), top)
        scale = jnp.zeros((8, size), jnp.float32)
        for c in range(8):
            inverse_root = lax.rsqrt(row(columns[c], c))
            scale = jnp.where(sub == c, inverse_root, scale)
            factor = jnp.where(sub > c, columns[c] * (inverse_root * inverse_root), 0.0)
            panel = panel - factor * row(panel, c)
            for j in range(c + 1, 8):
                columns[j] = columns[j] - factor * row(columns[j], c)
        square = scale * scale
        solved = panel * square
        for c in range(7, 0, -1):
            solved = solved - jnp.where(sub < c, columns[c] * square, 0.0) * row(solved, c)
        active = rows < size - 8 * step
        source = jnp.where(active, a, 0.0)[8:]
        rest = jnp.where(active & (lanes < 8), 0.0, a)[8:]
        for c in range(8):
            rest = rest - jnp.broadcast_to(source[:, c : c + 1], rest.shape) * jnp.broadcast_to(
                solved[c : c + 1], rest.shape
            )
        return pltpu.roll(jnp.concatenate([rest, panel * scale], axis=0), size - 8, 1)

    return lax.fori_loop(start, stop, block, a)


def unit_diagonal(gram):
    rows = lax.broadcasted_iota(jnp.int32, gram.shape, 0)
    lanes = lax.broadcasted_iota(jnp.int32, gram.shape, 1)
    diagonal = jnp.where(rows == lanes, gram, 0.0)
    across = lax.rsqrt(jnp.sum(diagonal, axis=0, keepdims=True))
    down = lax.rsqrt(jnp.sum(diagonal, axis=1, keepdims=True))
    return gram * across * down, across

def eliminate(blocks, k):
    size = blocks[0].shape[1]
    sub = lax.broadcasted_iota(jnp.int32, (8, size), 0)
    lane = lax.broadcasted_iota(jnp.int32, (8, size), 1) - 8 * k
    here = (lane >= 0) & (lane < 8)

    def row(value, index):
        return jnp.broadcast_to(value[index : index + 1], value.shape)

    def column(value, index):
        return jnp.broadcast_to(value[:, 8 * k + index : 8 * k + index + 1], value.shape)

    top = blocks[k]
    columns = [column(top, c) for c in range(8)]
    e = {(i, j): row(columns[j], i) for j in range(8) for i in range(j, 8)}
    panel = jnp.where(here, jnp.where(lane == sub, 1.0, 0.0), top)
    x = [row(panel, i) for i in range(8)]
    y, z, f = [None] * 8, [None] * 8, {}
    for p in range(0, 8, 2):
        a, b, c = e[p, p], e[p + 1, p], e[p + 1, p + 1]
        root = lax.rsqrt(a * c - b * b)
        inverse = root * root
        g = {}
        for i in range(p + 2, 8):
            g[i] = (e[i, p] * c - e[i, p + 1] * b, e[i, p + 1] * a - e[i, p] * b)
        for i in range(p + 2, 8):
            for j in range(p + 2, i + 1):
                e[i, j] = e[i, j] - (g[i][0] * e[j, p] + g[i][1] * e[j, p + 1]) * inverse
        for i in range(p + 2, 8):
            f[i, p], f[i, p + 1] = g[i][0] * inverse, g[i][1] * inverse
            x[i] = x[i] - (f[i, p] * x[p] + f[i, p + 1] * x[p + 1])
        first = lax.rsqrt(a)
        y[p] = x[p] * first
        y[p + 1] = (x[p + 1] * a - b * x[p]) * (first * root)
        z[p] = (c * x[p] - b * x[p + 1]) * inverse
        z[p + 1] = (a * x[p + 1] - b * x[p]) * inverse
    for p in (4, 2, 0):
        for i in range(p + 2, 8):
            z[p] = z[p] - f[i, p] * z[i]
            z[p + 1] = z[p + 1] - f[i, p + 1] * z[i]
    done = y[0]
    for i in range(1, 8):
        done = jnp.where(sub == i, y[i], done)
    out = list(blocks)
    out[k] = done
    for r in range(k + 1, len(blocks)):
        rest = jnp.where(here, 0.0, blocks[r])
        for c in range(8):
            rest = rest - column(blocks[r], c) * z[c]
        out[r] = rest
    return out


def lower(a, start=0):
    rows = lax.broadcasted_iota(jnp.int32, a.shape, 0) + start
    lanes = lax.broadcasted_iota(jnp.int32, a.shape, 1)
    return jnp.where(rows >= lanes, a, 0.0)


def remote(src, dst, send_sem, recv_sem, device):
    return pltpu.make_async_remote_copy(
        src_ref=src, dst_ref=dst, send_sem=send_sem, recv_sem=recv_sem, device_id=device, device_id_type=MESH
    )


def widths(cols):
    group = 256 if cols % 256 == 0 else cols
    chunk = 128 if group % 128 == 0 else group
    return group, chunk


def factors(shape, momentum_ref, gradient_ref, prior_ref, mixed, pair_ref, right_ref, following_ref,
            raw, wide_high, wide_low, prior_vmem, prior_pair, left, core_in, plane_in, whole, fine, turned, sums, totals,
            arrive, pieces, piece_in, piece_z, piece_all, squares, work, load_sem, prior_sem, core_recv, once,
            gram_send, gram_recv, chain_send, chain_recv):
    rows, cols = mixed.shape
    rank = prior_ref.shape[1]
    depth, dp = shape["shard"], shape["dp"]
    cores = 2 if shape["tensor"] % 2 == 0 else 1
    nx = shape["tensor"] // cores
    chips = nx * dp
    plane = chips * cores
    own = rows // plane
    s, t, y = lax.axis_index("shard"), lax.axis_index("tensor"), lax.axis_index("dp")
    core, x = lax.rem(t, cores), lax.div(t, cores)
    me = t * dp + y

    def chip(offset):
        px = lax.rem(x + lax.div(offset, dp), nx)
        py = lax.rem(y + lax.rem(offset, dp), dp)
        return px * dp + py, {"tensor": px * cores + core, "dp": py}

    def place(half, index):
        return pl.ds(pl.multiple_of((half * chips + index) * own, 8), own)

    def peer(k):
        other = lax.rem(me + k, plane)
        return other, {"tensor": lax.div(other, dp), "dp": lax.rem(other, dp)}

    def across(k):
        other = lax.rem(s + k, depth)
        return other, {"shard": other}

    partner = {"tensor": x * cores + cores - 1 - core}

    def load(slot, at):
        return (
            pltpu.make_async_copy(momentum_ref.at[at], mixed.at[at], load_sem.at[0, lax.rem(slot, AHEAD)]),
            pltpu.make_async_copy(gradient_ref.at[at], raw.at[at], load_sem.at[1, lax.rem(slot, AHEAD)]),
        )

    loads = chips * cores

    def spot(slot):
        i = lax.div(slot, cores)
        half = lax.rem(core + 1 + lax.rem(slot, cores), cores)
        return place(half, chip(chips - 1 - i)[0])

    prior_copy = pltpu.make_async_copy(prior_ref, prior_vmem, prior_sem)
    prior_copy.start()
    for slot in range(min(AHEAD, loads)):
        for copy in load(slot, spot(slot)):
            copy.start()

    barrier = pltpu.get_barrier_semaphore()
    for k in range(1, plane):
        pl.semaphore_signal(barrier, inc=1, device_id=peer(k)[1], device_id_type=MESH)
    for k in range(1, depth):
        pl.semaphore_signal(barrier, inc=1, device_id=across(k)[1], device_id_type=MESH)

    half_depth = max(depth // 2, 1)
    first = s < half_depth
    level = jnp.where(first, s, depth - 1 - s)
    outer = level > 0
    middle = level == half_depth - 1
    step_in = jnp.where(first, 1, -1)
    group, chunk = widths(cols)
    count = cols // chunk

    prior_copy.wait()
    high, low = split(prior_vmem[...])
    prior_pair[:, :rank] = high
    prior_pair[:, rank:] = low
    pl.semaphore_wait(barrier, plane + depth - 2)

    def product(slot, at):
        for copy in load(slot, at):
            copy.wait()
        ahead = slot + AHEAD

        @pl.when(ahead < loads)
        def _():
            for copy in load(ahead, spot(ahead)):
                copy.start()

        value = mixed[at, :] + raw[at, :].astype(jnp.float32)
        mixed[at, :] = value
        high, low = split(value)
        wide_high[at, :] = high
        wide_low[at, :] = low
        both = dot(high, prior_pair[...], NORMAL) + dot(low, prior_pair[...], NORMAL)
        return both[:, :rank] + both[:, rank:]

    def core_copy(i):
        at = place(cores - 1 - core, chip(chips - 1 - i)[0])
        return remote(left.at[at], core_in.at[i], once.at[0], core_recv.at[i], partner)

    def plane_copy(offset):
        index, device = chip(offset)
        slot = offset - 1
        return remote(left.at[place(core, index)], plane_in.at[slot], once.at[1], once.at[2], device)

    def bulk(first):
        return remote(plane_in, plane_in, once.at[first], once.at[first + 1], chip(1)[1])

    def settle(i):
        offset = chips - 1 - i
        at = place(core, chip(offset)[0])
        if cores == 2:
            core_copy(i).wait_recv()
            left[at, :] = left[at, :] + core_in[i]
        return offset

    def partial(slot, carry):
        i = lax.div(slot, cores)
        at = spot(slot)
        left[at, :] = product(slot, at)
        if cores == 2:

            @pl.when(lax.rem(slot, cores) == 0)
            def _():
                core_copy(i).start()

        @pl.when(jnp.logical_and(lax.rem(slot, cores) == 0, slot > 0))
        def _():
            plane_copy(settle(i - 1)).start()

        return carry

    with jax.named_scope("p1_left"):
        lax.fori_loop(0, loads, partial, 0)

    mine = place(core, x * dp + y)
    with jax.named_scope("p3_rswait"):
        settle(chips - 1)
        total = left[mine, :]
        if chips > 1:
            bulk(1).wait_recv()
        for offset in range(1, chips):
            total = total + plane_in[offset - 1]
        whole[mine, :] = total

    piece = rank // plane

    def summed(slots, n):
        value = slots[0]
        for i in range(1, n):
            value = value + slots[i]
        return value

    def gram_sends(turn, stage, n, find, source, target):
        for k in range(1, n):
            other, device = find(k)
            remote(source(other), target, gram_send.at[turn, stage], gram_recv.at[turn, stage], device).start()

    def gram_wait(turn, stage, n, find, slots):
        if n > 1:
            part = slots.at[turn, pl.ds(0, n - 1)]
            remote(part, part, gram_send.at[turn, stage], gram_recv.at[turn, stage], find(1)[1]).wait()

    def gram_start(turn, gram):
        for i in range(plane):
            pieces[turn, i] = gram[i * piece : (i + 1) * piece]
        piece_in[turn, me] = pieces[turn, me]
        gram_sends(turn, 0, plane, peer, lambda i: pieces.at[turn, i], piece_in.at[turn, me])

    def gram_across(turn):
        gram_wait(turn, 0, plane, peer, piece_in)
        piece_z[turn, s] = summed(piece_in.at[turn], plane)
        mine_z = piece_z.at[turn, s]
        gram_sends(turn, 1, depth, across, lambda i: mine_z, mine_z)

    def gram_spread(turn):
        gram_wait(turn, 1, depth, across, piece_z)
        piece_all[turn, me] = summed(piece_z.at[turn], depth)
        mine_all = piece_all.at[turn, me]
        gram_sends(turn, 2, plane, peer, lambda i: mine_all, mine_all)

    def gram_whole(turn):
        gram_wait(turn, 2, plane, peer, piece_all)
        return jnp.concatenate([piece_all[turn, i] for i in range(plane)], axis=0)

    with jax.named_scope("p4_gram"):
        gram_start(0, dot(total, total, ROWS, HIGHEST))
    for offset in range(1, chips):
        remote(whole.at[mine], whole.at[mine], once.at[3], once.at[4], chip(offset)[1]).start()
    with jax.named_scope("p5_gram1"):
        gram_across(0)
    with jax.named_scope("p6_gram2"):
        gram_spread(0)
    with jax.named_scope("p7_agwait"):
        if chips > 1:
            bulk(1).wait_send()
            bulk(3).wait()
        if cores == 2:
            at = pl.ds(pl.multiple_of(core * (rows // 2), 8), rows // 2)
            remote(left.at[at], left.at[at], once.at[0], once.at[0], partner).wait_send()
            half_copy = remote(whole.at[at], whole.at[at], once.at[5], once.at[6], partner)
            half_copy.start()
    with jax.named_scope("p8_gram3"):
        gram = gram_whole(0)
    parts = 2 if rank % 16 == 0 else 1
    tall = rank // parts
    units = count * parts
    blocks = rank // 8
    per = group // chunk
    groups = cols // group

    def unit(ref, u):
        return ref.at[u % count, pl.ds((u // count) * tall, tall)]

    def inward(u):
        slot = jnp.where(middle, 1, 0)
        return remote(unit(sums, u), unit(arrive.at[slot], u), chain_send.at[0], chain_recv.at[slot, u],
                      {"shard": s + step_in})

    def outward(u):
        return remote(unit(totals, u), unit(arrive.at[1], u), chain_send.at[1], chain_recv.at[1, u],
                      {"shard": s - step_in})

    def landed(slot, u):
        remote(unit(sums, u), unit(arrive.at[slot], u), chain_send.at[0], chain_recv.at[slot, u],
               {"shard": s + step_in}).wait_recv()

    def near(u):
        landed(0, u)
        unit(sums, u)[...] = unit(sums, u)[...] + unit(arrive.at[0], u)[...]
        inward(u).start()

    def far(u, forward):
        if depth > 1:
            landed(1, u)
            got = unit(arrive.at[1], u)[...]
            unit(totals, u)[...] = jnp.where(middle, unit(sums, u)[...] + got, got)
            if forward:
                outward(u).start()
        else:
            unit(totals, u)[...] = unit(sums, u)[...]

    def due(step, u):
        late = 0.0 if u < count else 1.7 if 2 * u < 3 * count else 2.4
        return u + late + (GAP if step is far else 0.0)

    queue = sorted(((step, u) for u in range(units) for step in (near, far)), key=lambda item: due(*item))

    def take(n, computed):
        steps = []
        while len(steps) < n and len(queue) > 1 and queue[0][1] < computed:
            steps.append(queue.pop(0))
        if depth > 2 and steps:

            @pl.when(outer)
            def _():
                for step, u in steps:
                    with jax.named_scope(f"q3_{step.__name__}{u}"):
                        step(u, True) if step is far else step(u)

    def basis_half(r, w):
        for i in range(STEPS):
            block = rows // STEPS
            at = slice(i * block, (i + 1) * block)
            if r == 0:
                high, middle_part, low = split3(whole[at, :])
                fine[0, at, :rank] = high
                fine[0, at, rank:] = middle_part
                fine[1, at, :rank] = high
                fine[1, at, rank:] = low
            value = value_of(w, fine[0, at, :], fine[1, at, :])
            high, low = split(value)
            turned[r, :tall, at] = high
            turned[r, tall:, at] = low

    def value_of(w, block, tail_block):
        w_high, w_middle, w_low = split3(w)
        ends = jnp.concatenate(
            [jnp.concatenate([w_high, w_middle], axis=1), jnp.concatenate([w_middle, w_high], axis=1)], axis=0
        )
        both = dot(ends, block, TURNED)
        return both[:tall] + (both[tall:] + dot(jnp.concatenate([w_low, w_high], axis=1), tail_block, TURNED))

    def right_group(r, g):
        at = slice(g * group, (g + 1) * group)
        both = dot(turned[r], wide_high[:, at], NORMAL)
        value = both[:tall] + both[tall:] + dot(turned[r, :tall, :], wide_low[:, at], NORMAL)
        for i in range(per):
            sums[g * per + i, r * tall : (r + 1) * tall, :] = value[:, i * chunk : (i + 1) * chunk]

    def right_send(r, g):
        if depth > 1:

            @pl.when(jnp.logical_not(outer))
            def _():
                for i in range(per):
                    inward(r * count + g * per + i).start()

    with jax.named_scope("p9_inv1"):
        scaled, lanes = unit_diagonal(gram)
        rest = [scaled[8 * i : 8 * i + 8] for i in range(blocks)]
        weights = []
    for r in range(parts):
        with jax.named_scope(f"p9_half{r}"):
            first_block, stop = r * blocks // parts, (r + 1) * blocks // parts
            for k in range(first_block, stop):
                rest = eliminate(rest, k)
                if r > 0 and k == first_block + 5:
                    take(1, r * count)
            weights.append(lower(jnp.concatenate(rest[first_block:stop], axis=0), 8 * first_block) * lanes)
        last_part = r == parts - 1
        if last_part:
            take(1, r * count)
            with jax.named_scope("q1_gram"):
                if r == 0 and cores == 2:
                    half_copy.wait()
                high, middle_part, low = split3(whole[mine, :])
                block = jnp.concatenate([high, middle_part], axis=1)
                tail_block = jnp.concatenate([high, low], axis=1)
                part = jnp.concatenate([value_of(w, block, tail_block) for w in weights], axis=0)
                gram_start(1, dot(part, part, TURNED, HIGHEST))
            take(MOVES[0], r * count)
        with jax.named_scope(f"q0_value{r}"):
            if cores == 2 and r == 0 and not last_part:
                half_copy.wait()
            basis_half(r, weights[r])
        if last_part:
            take(MOVES[1], r * count)
        for g in range(groups):
            with jax.named_scope(f"q2_right{r}{g}"):
                right_group(r, g)
            if last_part and g == min(2, groups - 1):
                with jax.named_scope("q2_gram1"):
                    gram_across(1)
            right_send(r, g)
            if last_part:
                take(MOVES[2 + min(g, 3)], r * count + (g + 1) * per)

    def second():
        with jax.named_scope("q4_gram3"):
            scaled, across_lanes = unit_diagonal(gram_whole(1))
        return [scaled[8 * i : 8 * i + 8] for i in range(blocks)], across_lanes

    def invert(rest, start, stop):
        with jax.named_scope("q5_inv2"):
            for k in range(start, stop):
                rest = eliminate(rest, k)
        return rest

    def keep(rest, across_lanes):
        work[...] = lower(jnp.concatenate(rest, axis=0)) * across_lanes

    def basis():
        with jax.named_scope("q6_basis"):
            high, low = split(work[...])
            pair = jnp.concatenate([high, low], axis=1)
            for i in range(STEPS):
                block = rows // STEPS
                at = slice(i * block, (i + 1) * block)
                top = jnp.concatenate([turned[r, :tall, at] for r in range(parts)], axis=0)
                bottom = jnp.concatenate([turned[r, tall:, at] for r in range(parts)], axis=0)
                value = dot(pair, jnp.concatenate([top, top], axis=0), NORMAL) + dot(high, bottom, NORMAL)
                high_t, low_t = split(value.T)
                pair_ref[at, :rank] = high_t
                pair_ref[at, rank:] = low_t

    def correct(start, stop):
        with jax.named_scope("q7_right"):
            wide = jnp.concatenate([totals[c] for c in range(start, stop)], axis=1)
            value = dot(wide, work[...], ((0,), (1,)), HIGHEST)
            right_ref[start * chunk : stop * chunk, :] = value
            column = jnp.sum(value * value, axis=0, keepdims=True)
            squares[me] = squares[me] + jnp.broadcast_to(column, (8, rank))

    squares[me] = jnp.zeros((8, rank), jnp.float32)

    @pl.when(outer)
    def _():
        plan = list(queue)
        second_at = next((i for i, (step, u) in enumerate(plan) if step is near and 2 * u >= 3 * count), 0)
        third_at = next((i for i, (step, u) in enumerate(plan) if step is far and u >= THIRD), len(plan) - 1)
        third_at = max(third_at, second_at)
        at = 0
        for i, (step, u) in enumerate(plan):
            if i == second_at:
                with jax.named_scope("q4_gram2"):
                    gram_spread(1)
            with jax.named_scope(f"q3_{step.__name__}{u}"):
                far(u, True) if step is far else near(u)
            if i == third_at:
                rest, across_lanes = second()
            if i >= third_at and step is far:
                stop = blocks if i == len(plan) - 1 else min(at + SHARE, blocks)
                rest = invert(rest, at, stop)
                at = stop
        keep(rest, across_lanes)
        for c in range(0, count, 2):
            correct(c, min(c + 2, count))

    @pl.when(jnp.logical_not(outer))
    def _():
        with jax.named_scope("q4_gram2"):
            gram_spread(1)
        rest, across_lanes = second()
        keep(invert(rest, 0, blocks), across_lanes)
        for u in range(units):
            with jax.named_scope(f"q3_end{u}"):
                far(u, False)
            if u == units - 1 - 2 * per:
                for c in range(0, count - 2 * per, 2):
                    correct(c, c + 2)
        for c in range(max(count - 2 * per, 0) if count > 2 * per else 0, count, 2):
            correct(c, min(c + 2, count))

    with jax.named_scope("q8_squares"):
        for k in range(1, plane):
            remote(squares.at[me], squares.at[me], once.at[7], once.at[8], peer(k)[1]).start()
    basis()
    with jax.named_scope("q9_momentum"):
        scaled = (right_ref[...] * (decay_rate - 1.0)).astype(jnp.bfloat16)

        def update(i, carry):
            block = rows // STEPS
            at = pl.ds(pl.multiple_of(i * block, 8), block)
            mixed[at, :] = mixed[at, :] + dot(pair_ref[at, :rank], scaled, TURNED)
            return carry

        lax.fori_loop(0, STEPS, update, 0)
    with jax.named_scope("r0_follow"):
        if plane > 1:
            part = squares.at[pl.ds(0, plane - 1)]
            remote(part, part, once.at[7], once.at[8], peer(1)[1]).wait()
        mean = summed(squares, plane)[:1] / (cols * plane)
        following_ref[...] = right_ref[...] / jnp.sqrt(mean + epsilon)
        if depth > 1:
            remote(sums, sums, chain_send.at[0], chain_recv.at[0, 0], {"shard": s + step_in}).wait_send()

            @pl.when(outer)
            def _():
                remote(totals, totals, chain_send.at[1], chain_recv.at[0, 0], {"shard": s - step_in}).wait_send()


def finish(scale, mixed_ref, pair_ref, following_ref, next_ref, direction_ref, out_ref, direction_vmem, sems):
    rows = mixed_ref.shape[0]
    rank = following_ref.shape[1]
    block = rows // STEPS
    moves = (
        pltpu.make_async_copy(mixed_ref, next_ref, sems.at[0]),
        pltpu.make_async_copy(following_ref, out_ref, sems.at[1]),
    )
    for copy in moves:
        copy.start()
    high, low = split(following_ref[...] * scale)
    follow = jnp.concatenate([high, high], axis=1)
    for i in range(STEPS):
        at = pl.ds(i * block, block)
        value = dot(pair_ref[at, :], follow, TURNED) + dot(pair_ref[at, :rank], low, TURNED)
        direction_vmem[at, :] = value.astype(jnp.bfloat16)
        pltpu.make_async_copy(direction_vmem.at[at], direction_ref.at[at], sems.at[2]).start()
    for copy in moves:
        copy.wait()
    pltpu.make_async_copy(direction_vmem, direction_ref, sems.at[2]).wait()


def shards(shape, gradient, momentum, prior_right_factor):
    gradient, momentum, prior = gradient[0], momentum[0], prior_right_factor[0]
    rows, cols = momentum.shape
    rank = prior.shape[1]
    z = shape["shard"]
    plane = shape["tensor"] * shape["dp"]
    cores = 2 if shape["tensor"] % 2 == 0 else 1
    chips = plane // cores
    own = rows // plane
    group, chunk = widths(cols)
    count = cols // chunk
    parts = 2 if rank % 16 == 0 else 1
    dma = pltpu.SemaphoreType.DMA
    vmem = pl.BlockSpec(memory_space=pltpu.VMEM)
    hbm = pl.BlockSpec(memory_space=pltpu.HBM)
    f32, bf16 = jnp.float32, jnp.bfloat16
    others = max(chips - 1, 1)
    mixed, pair, right, following = pl.pallas_call(
        functools.partial(factors, shape),
        out_shape=[
            pltpu.VMEM((rows, cols), f32),
            pltpu.VMEM((rows, 2 * rank), bf16),
            pltpu.VMEM((cols, rank), f32),
            pltpu.VMEM((cols, rank), f32),
        ],
        in_specs=[hbm, hbm, hbm],
        out_specs=[vmem, vmem, vmem, vmem],
        scratch_shapes=[
            pltpu.VMEM((rows, cols), bf16),
            pltpu.VMEM((rows, cols), bf16),
            pltpu.VMEM((rows, cols), bf16),
            pltpu.VMEM((cols, rank), f32),
            pltpu.VMEM((cols, 2 * rank), bf16),
            pltpu.VMEM((rows, rank), f32),
            pltpu.VMEM((chips, own, rank), f32),
            pltpu.VMEM((others, own, rank), f32),
            pltpu.VMEM((rows, rank), f32),
            pltpu.VMEM((2, rows, 2 * rank), bf16),
            pltpu.VMEM((parts, 2 * rank // parts, rows), bf16),
            pltpu.VMEM((count, rank, chunk), f32),
            pltpu.VMEM((count, rank, chunk), f32),
            pltpu.VMEM((2, count, rank, chunk), f32),
            pltpu.VMEM((2, plane, rank // plane, rank), f32),
            pltpu.VMEM((2, plane, rank // plane, rank), f32),
            pltpu.VMEM((2, z, rank // plane, rank), f32),
            pltpu.VMEM((2, plane, rank // plane, rank), f32),
            pltpu.VMEM((plane, 8, rank), f32),
            pltpu.VMEM((rank, rank), f32),
            dma((2, AHEAD)),
            dma,
            dma((chips,)),
            dma((9,)),
            dma((2, 3)),
            dma((2, 3)),
            dma((2,)),
            dma((2, 2 * count)),
        ],
        compiler_params=pltpu.CompilerParams(
            collective_id=0, has_side_effects=True, vmem_limit_bytes=36 * MiB
        ),
        name="factors",
    )(*(pltpu.with_memory_space_constraint(x, pltpu.HBM) for x in (momentum, gradient, prior)))

    scale = float((rows * z / rank) ** 0.5)
    momentum_next, direction, following = pl.pallas_call(
        functools.partial(finish, scale),
        out_shape=[
            jax.ShapeDtypeStruct((rows, cols), f32),
            jax.ShapeDtypeStruct((rows, cols), bf16),
            jax.ShapeDtypeStruct((cols, rank), f32),
        ],
        in_specs=[vmem, vmem, vmem],
        out_specs=[hbm, hbm, hbm],
        scratch_shapes=[pltpu.VMEM((rows, cols), bf16), dma((3,))],
        compiler_params=pltpu.CompilerParams(vmem_limit_bytes=24 * MiB),
        name="finish",
    )(mixed, pair, following)
    return momentum_next[None], following[None], direction[None]


def solution(mesh):
    return jax.shard_map(
        functools.partial(shards, dict(mesh.shape)),
        mesh=mesh,
        in_specs=(
            P(None, "shard", ("tensor", "dp")),
            P(None, "shard", ("tensor", "dp")),
            P(None, ("tensor", "dp"), None),
        ),
        out_specs=(
            P(None, "shard", ("tensor", "dp")),
            P(None, ("tensor", "dp"), None),
            P(None, "shard", ("tensor", "dp")),
        ),
        check_vma=False,
    )
```

```python
import functools

import jax
import jax.numpy as jnp
from jax import lax
from jax.experimental import pallas as pl
from jax.experimental.pallas import tpu as pltpu
from jax.sharding import PartitionSpec as P

MESH = pl.DeviceIdType.MESH
HIGHEST = lax.Precision.HIGHEST
decay_rate = 0.95
epsilon = 1e-06
STEPS = 8
AHEAD = 3
GAP = 5.3
THIRD = 12
SHARE = 2
MOVES = (1, 1, 1, 2, 2, 3)
MiB = 1024 * 1024
ROWS, NORMAL, TURNED = ((0,), (0,)), ((1,), (0,)), ((1,), (1,))


def dot(a, b, dims, precision=None):
    return lax.dot_general(
        a, b, (dims, ((), ())), precision=precision, preferred_element_type=jnp.float32
    )


def split(value):
    high = value.astype(jnp.bfloat16)
    low = (value - high.astype(jnp.float32)).astype(jnp.bfloat16)
    return high, low


def split3(value):
    high = value.astype(jnp.bfloat16)
    rest = value - high.astype(jnp.float32)
    middle = rest.astype(jnp.bfloat16)
    return high, middle, (rest - middle.astype(jnp.float32)).astype(jnp.bfloat16)


def inverse_steps(a, start, stop):
    size = a.shape[0]
    sub = lax.broadcasted_iota(jnp.int32, (8, size), 0)
    lane = lax.broadcasted_iota(jnp.int32, (8, size), 1)
    rows = lax.broadcasted_iota(jnp.int32, (size, size), 0)
    lanes = lax.broadcasted_iota(jnp.int32, (size, size), 1)

    def row(value, index):
        return jnp.broadcast_to(value[index : index + 1], value.shape)

    def block(step, a):
        top = a[:8]
        columns = [jnp.broadcast_to(top[:, c : c + 1], (8, size)) for c in range(8)]
        panel = jnp.where(lane < 8, jnp.where(lane == sub, 1.0, 0.0), top)
        scale = jnp.zeros((8, size), jnp.float32)
        for c in range(8):
            inverse_root = lax.rsqrt(row(columns[c], c))
            scale = jnp.where(sub == c, inverse_root, scale)
            factor = jnp.where(sub > c, columns[c] * (inverse_root * inverse_root), 0.0)
            panel = panel - factor * row(panel, c)
            for j in range(c + 1, 8):
                columns[j] = columns[j] - factor * row(columns[j], c)
        square = scale * scale
        solved = panel * square
        for c in range(7, 0, -1):
            solved = solved - jnp.where(sub < c, columns[c] * square, 0.0) * row(solved, c)
        active = rows < size - 8 * step
        source = jnp.where(active, a, 0.0)[8:]
        rest = jnp.where(active & (lanes < 8), 0.0, a)[8:]
        for c in range(8):
            rest = rest - jnp.broadcast_to(source[:, c : c + 1], rest.shape) * jnp.broadcast_to(
                solved[c : c + 1], rest.shape
            )
        return pltpu.roll(jnp.concatenate([rest, panel * scale], axis=0), size - 8, 1)

    return lax.fori_loop(start, stop, block, a)


def unit_diagonal(gram):
    rows = lax.broadcasted_iota(jnp.int32, gram.shape, 0)
    lanes = lax.broadcasted_iota(jnp.int32, gram.shape, 1)
    diagonal = jnp.where(rows == lanes, gram, 0.0)
    across = lax.rsqrt(jnp.sum(diagonal, axis=0, keepdims=True))
    down = lax.rsqrt(jnp.sum(diagonal, axis=1, keepdims=True))
    return gram * across * down, across

def eliminate(blocks, k):
    size = blocks[0].shape[1]
    sub = lax.broadcasted_iota(jnp.int32, (8, size), 0)
    lane = lax.broadcasted_iota(jnp.int32, (8, size), 1) - 8 * k
    here = (lane >= 0) & (lane < 8)

    def row(value, index):
        return jnp.broadcast_to(value[index : index + 1], value.shape)

    def column(value, index):
        return jnp.broadcast_to(value[:, 8 * k + index : 8 * k + index + 1], value.shape)

    top = blocks[k]
    columns = [column(top, c) for c in range(8)]
    e = {(i, j): row(columns[j], i) for j in range(8) for i in range(j, 8)}
    panel = jnp.where(here, jnp.where(lane == sub, 1.0, 0.0), top)
    x = [row(panel, i) for i in range(8)]
    y, z, f = [None] * 8, [None] * 8, {}
    for p in range(0, 8, 2):
        a, b, c = e[p, p], e[p + 1, p], e[p + 1, p + 1]
        root = lax.rsqrt(a * c - b * b)
        inverse = root * root
        g = {}
        for i in range(p + 2, 8):
            g[i] = (e[i, p] * c - e[i, p + 1] * b, e[i, p + 1] * a - e[i, p] * b)
        for i in range(p + 2, 8):
            for j in range(p + 2, i + 1):
                e[i, j] = e[i, j] - (g[i][0] * e[j, p] + g[i][1] * e[j, p + 1]) * inverse
        for i in range(p + 2, 8):
            f[i, p], f[i, p + 1] = g[i][0] * inverse, g[i][1] * inverse
            x[i] = x[i] - (f[i, p] * x[p] + f[i, p + 1] * x[p + 1])
        first = lax.rsqrt(a)
        y[p] = x[p] * first
        y[p + 1] = (x[p + 1] * a - b * x[p]) * (first * root)
        z[p] = (c * x[p] - b * x[p + 1]) * inverse
        z[p + 1] = (a * x[p + 1] - b * x[p]) * inverse
    for p in (4, 2, 0):
        for i in range(p + 2, 8):
            z[p] = z[p] - f[i, p] * z[i]
            z[p + 1] = z[p + 1] - f[i, p + 1] * z[i]
    done = y[0]
    for i in range(1, 8):
        done = jnp.where(sub == i, y[i], done)
    out = list(blocks)
    out[k] = done
    for r in range(k + 1, len(blocks)):
        rest = jnp.where(here, 0.0, blocks[r])
        for c in range(8):
            rest = rest - column(blocks[r], c) * z[c]
        out[r] = rest
    return out


def lower(a, start=0):
    rows = lax.broadcasted_iota(jnp.int32, a.shape, 0) + start
    lanes = lax.broadcasted_iota(jnp.int32, a.shape, 1)
    return jnp.where(rows >= lanes, a, 0.0)


def remote(src, dst, send_sem, recv_sem, device):
    return pltpu.make_async_remote_copy(
        src_ref=src, dst_ref=dst, send_sem=send_sem, recv_sem=recv_sem, device_id=device, device_id_type=MESH
    )


def widths(cols):
    group = 256 if cols % 256 == 0 else cols
    chunk = 128 if group % 128 == 0 else group
    return group, chunk


def factors(shape, momentum_ref, gradient_ref, prior_ref, mixed, pair_ref, following_ref, right_ref, raw, wide_high, wide_low, prior_vmem, prior_pair, left, core_in, plane_in, whole, fine, turned, sums, totals,
            arrive, pieces, piece_in, piece_z, piece_all, squares, work, load_sem, prior_sem, core_recv, once,
            gram_send, gram_recv, chain_send, chain_recv):
    rows, cols = mixed.shape
    rank = prior_ref.shape[1]
    depth, dp = shape["shard"], shape["dp"]
    cores = 2 if shape["tensor"] % 2 == 0 else 1
    nx = shape["tensor"] // cores
    chips = nx * dp
    plane = chips * cores
    own = rows // plane
    s, t, y = lax.axis_index("shard"), lax.axis_index("tensor"), lax.axis_index("dp")
    core, x = lax.rem(t, cores), lax.div(t, cores)
    me = t * dp + y

    def chip(offset):
        px = lax.rem(x + lax.div(offset, dp), nx)
        py = lax.rem(y + lax.rem(offset, dp), dp)
        return px * dp + py, {"tensor": px * cores + core, "dp": py}

    def place(half, index):
        return pl.ds(pl.multiple_of((half * chips + index) * own, 8), own)

    def peer(k):
        other = lax.rem(me + k, plane)
        return other, {"tensor": lax.div(other, dp), "dp": lax.rem(other, dp)}

    def across(k):
        other = lax.rem(s + k, depth)
        return other, {"shard": other}

    partner = {"tensor": x * cores + cores - 1 - core}

    def load(slot, at):
        return (
            pltpu.make_async_copy(momentum_ref.at[at], mixed.at[at], load_sem.at[0, lax.rem(slot, AHEAD)]),
            pltpu.make_async_copy(gradient_ref.at[at], raw.at[at], load_sem.at[1, lax.rem(slot, AHEAD)]),
        )

    loads = chips * cores

    def spot(slot):
        i = lax.div(slot, cores)
        half = lax.rem(core + 1 + lax.rem(slot, cores), cores)
        return place(half, chip(chips - 1 - i)[0])

    prior_copy = pltpu.make_async_copy(prior_ref, prior_vmem, prior_sem)
    prior_copy.start()
    for slot in range(min(AHEAD, loads)):
        for copy in load(slot, spot(slot)):
            copy.start()

    barrier = pltpu.get_barrier_semaphore()
    for k in range(1, plane):
        pl.semaphore_signal(barrier, inc=1, device_id=peer(k)[1], device_id_type=MESH)
    for k in range(1, depth):
        pl.semaphore_signal(barrier, inc=1, device_id=across(k)[1], device_id_type=MESH)

    half_depth = max(depth // 2, 1)
    first = s < half_depth
    level = jnp.where(first, s, depth - 1 - s)
    outer = level > 0
    middle = level == half_depth - 1
    step_in = jnp.where(first, 1, -1)
    group, chunk = widths(cols)
    count = cols // chunk

    prior_copy.wait()
    high, low = split(prior_vmem[...])
    prior_pair[:, :rank] = high
    prior_pair[:, rank:] = low
    pl.semaphore_wait(barrier, plane + depth - 2)

    def product(slot, at):
        for copy in load(slot, at):
            copy.wait()
        ahead = slot + AHEAD

        @pl.when(ahead < loads)
        def _():
            for copy in load(ahead, spot(ahead)):
                copy.start()

        value = mixed[at, :] + raw[at, :].astype(jnp.float32)
        mixed[at, :] = value
        high, low = split(value)
        wide_high[at, :] = high
        wide_low[at, :] = low
        both = dot(high, prior_pair[...], NORMAL) + dot(low, prior_pair[...], NORMAL)
        return both[:, :rank] + both[:, rank:]

    def core_copy(i):
        at = place(cores - 1 - core, chip(chips - 1 - i)[0])
        return remote(left.at[at], core_in.at[i], once.at[0], core_recv.at[i], partner)

    def plane_copy(offset):
        index, device = chip(offset)
        slot = offset - 1
        return remote(left.at[place(core, index)], plane_in.at[slot], once.at[1], once.at[2], device)

    def bulk(first):
        return remote(plane_in, plane_in, once.at[first], once.at[first + 1], chip(1)[1])

    def settle(i):
        offset = chips - 1 - i
        at = place(core, chip(offset)[0])
        if cores == 2:
            core_copy(i).wait_recv()
            left[at, :] = left[at, :] + core_in[i]
        return offset

    def partial(slot, carry):
        i = lax.div(slot, cores)
        at = spot(slot)
        left[at, :] = product(slot, at)
        if cores == 2:

            @pl.when(lax.rem(slot, cores) == 0)
            def _():
                core_copy(i).start()

        @pl.when(jnp.logical_and(lax.rem(slot, cores) == 0, slot > 0))
        def _():
            plane_copy(settle(i - 1)).start()

        return carry

    with jax.named_scope("p1_left"):
        lax.fori_loop(0, loads, partial, 0)

    mine = place(core, x * dp + y)
    with jax.named_scope("p3_rswait"):
        settle(chips - 1)
        total = left[mine, :]
        if chips > 1:
            bulk(1).wait_recv()
        for offset in range(1, chips):
            total = total + plane_in[offset - 1]
        whole[mine, :] = total

    piece = rank // plane

    def summed(slots, n):
        value = slots[0]
        for i in range(1, n):
            value = value + slots[i]
        return value

    def gram_sends(turn, stage, n, find, source, target):
        for k in range(1, n):
            other, device = find(k)
            remote(source(other), target, gram_send.at[turn, stage], gram_recv.at[turn, stage], device).start()

    def gram_wait(turn, stage, n, find, slots):
        if n > 1:
            part = slots.at[turn, pl.ds(0, n - 1)]
            remote(part, part, gram_send.at[turn, stage], gram_recv.at[turn, stage], find(1)[1]).wait()

    def gram_start(turn, gram):
        for i in range(plane):
            pieces[turn, i] = gram[i * piece : (i + 1) * piece]
        piece_in[turn, me] = pieces[turn, me]
        gram_sends(turn, 0, plane, peer, lambda i: pieces.at[turn, i], piece_in.at[turn, me])

    def gram_across(turn):
        gram_wait(turn, 0, plane, peer, piece_in)
        piece_z[turn, s] = summed(piece_in.at[turn], plane)
        mine_z = piece_z.at[turn, s]
        gram_sends(turn, 1, depth, across, lambda i: mine_z, mine_z)

    def gram_spread(turn):
        gram_wait(turn, 1, depth, across, piece_z)
        piece_all[turn, me] = summed(piece_z.at[turn], depth)
        mine_all = piece_all.at[turn, me]
        gram_sends(turn, 2, plane, peer, lambda i: mine_all, mine_all)

    def gram_whole(turn):
        gram_wait(turn, 2, plane, peer, piece_all)
        return jnp.concatenate([piece_all[turn, i] for i in range(plane)], axis=0)

    with jax.named_scope("p4_gram"):
        gram_start(0, dot(total, total, ROWS, HIGHEST))
    for offset in range(1, chips):
        remote(whole.at[mine], whole.at[mine], once.at[3], once.at[4], chip(offset)[1]).start()
    with jax.named_scope("p5_gram1"):
        gram_across(0)
    with jax.named_scope("p6_gram2"):
        gram_spread(0)
    with jax.named_scope("p7_agwait"):
        if chips > 1:
            bulk(1).wait_send()
            bulk(3).wait()
        if cores == 2:
            at = pl.ds(pl.multiple_of(core * (rows // 2), 8), rows // 2)
            remote(left.at[at], left.at[at], once.at[0], once.at[0], partner).wait_send()
            half_copy = remote(whole.at[at], whole.at[at], once.at[5], once.at[6], partner)
            half_copy.start()
    with jax.named_scope("p8_gram3"):
        gram = gram_whole(0)
    parts = 2 if rank % 16 == 0 else 1
    tall = rank // parts
    units = count * parts
    blocks = rank // 8
    per = group // chunk
    groups = cols // group

    def unit(ref, u):
        return ref.at[u % count, pl.ds((u // count) * tall, tall)]

    def inward(u):
        slot = jnp.where(middle, 1, 0)
        return remote(unit(sums, u), unit(arrive.at[slot], u), chain_send.at[0], chain_recv.at[slot, u],
                      {"shard": s + step_in})

    def outward(u):
        return remote(unit(totals, u), unit(arrive.at[1], u), chain_send.at[1], chain_recv.at[1, u],
                      {"shard": s - step_in})

    def landed(slot, u):
        remote(unit(sums, u), unit(arrive.at[slot], u), chain_send.at[0], chain_recv.at[slot, u],
               {"shard": s + step_in}).wait_recv()

    def near(u):
        landed(0, u)
        unit(sums, u)[...] = unit(sums, u)[...] + unit(arrive.at[0], u)[...]
        inward(u).start()

    def far(u, forward):
        if depth > 1:
            landed(1, u)
            got = unit(arrive.at[1], u)[...]
            unit(totals, u)[...] = jnp.where(middle, unit(sums, u)[...] + got, got)
            if forward:
                outward(u).start()
        else:
            unit(totals, u)[...] = unit(sums, u)[...]

    def due(step, u):
        late = 0.0 if u < count else 1.7 if 2 * u < 3 * count else 2.4
        return u + late + (GAP if step is far else 0.0)

    queue = sorted(((step, u) for u in range(units) for step in (near, far)), key=lambda item: due(*item))

    def take(n, computed):
        steps = []
        while len(steps) < n and len(queue) > 1 and queue[0][1] < computed:
            steps.append(queue.pop(0))
        if depth > 2 and steps:

            @pl.when(outer)
            def _():
                for step, u in steps:
                    with jax.named_scope(f"q3_{step.__name__}{u}"):
                        step(u, True) if step is far else step(u)

    def basis_half(r, w):
        for i in range(STEPS):
            block = rows // STEPS
            at = slice(i * block, (i + 1) * block)
            if r == 0:
                high, middle_part, low = split3(whole[at, :])
                fine[0, at, :rank] = high
                fine[0, at, rank:] = middle_part
                fine[1, at, :rank] = high
                fine[1, at, rank:] = low
            value = value_of(w, fine[0, at, :], fine[1, at, :])
            high, low = split(value)
            turned[r, :tall, at] = high
            turned[r, tall:, at] = low

    def value_of(w, block, tail_block):
        w_high, w_middle, w_low = split3(w)
        ends = jnp.concatenate(
            [jnp.concatenate([w_high, w_middle], axis=1), jnp.concatenate([w_middle, w_high], axis=1)], axis=0
        )
        both = dot(ends, block, TURNED)
        return both[:tall] + (both[tall:] + dot(jnp.concatenate([w_low, w_high], axis=1), tail_block, TURNED))

    def right_group(r, g):
        at = slice(g * group, (g + 1) * group)
        both = dot(turned[r], wide_high[:, at], NORMAL)
        value = both[:tall] + both[tall:] + dot(turned[r, :tall, :], wide_low[:, at], NORMAL)
        for i in range(per):
            sums[g * per + i, r * tall : (r + 1) * tall, :] = value[:, i * chunk : (i + 1) * chunk]

    def right_send(r, g):
        if depth > 1:

            @pl.when(jnp.logical_not(outer))
            def _():
                for i in range(per):
                    inward(r * count + g * per + i).start()

    with jax.named_scope("p9_inv1"):
        scaled, lanes = unit_diagonal(gram)
        rest = [scaled[8 * i : 8 * i + 8] for i in range(blocks)]
        weights = []
    for r in range(parts):
        with jax.named_scope(f"p9_half{r}"):
            first_block, stop = r * blocks // parts, (r + 1) * blocks // parts
            for k in range(first_block, stop):
                rest = eliminate(rest, k)
                if r > 0 and k == first_block + 5:
                    take(1, r * count)
            weights.append(lower(jnp.concatenate(rest[first_block:stop], axis=0), 8 * first_block) * lanes)
        last_part = r == parts - 1
        if last_part:
            take(1, r * count)
            with jax.named_scope("q1_gram"):
                if r == 0 and cores == 2:
                    half_copy.wait()
                high, middle_part, low = split3(whole[mine, :])
                block = jnp.concatenate([high, middle_part], axis=1)
                tail_block = jnp.concatenate([high, low], axis=1)
                part = jnp.concatenate([value_of(w, block, tail_block) for w in weights], axis=0)
                gram_start(1, dot(part, part, TURNED, HIGHEST))
            take(MOVES[0], r * count)
        with jax.named_scope(f"q0_value{r}"):
            if cores == 2 and r == 0 and not last_part:
                half_copy.wait()
            basis_half(r, weights[r])
        if last_part:
            take(MOVES[1], r * count)
        for g in range(groups):
            with jax.named_scope(f"q2_right{r}{g}"):
                right_group(r, g)
            if last_part and g == min(2, groups - 1):
                with jax.named_scope("q2_gram1"):
                    gram_across(1)
            right_send(r, g)
            if last_part:
                take(MOVES[2 + min(g, 3)], r * count + (g + 1) * per)

    def second():
        with jax.named_scope("q4_gram3"):
            scaled, across_lanes = unit_diagonal(gram_whole(1))
        return [scaled[8 * i : 8 * i + 8] for i in range(blocks)], across_lanes

    def invert(rest, start, stop):
        with jax.named_scope("q5_inv2"):
            for k in range(start, stop):
                rest = eliminate(rest, k)
        return rest

    def keep(rest, across_lanes):
        work[...] = lower(jnp.concatenate(rest, axis=0)) * across_lanes

    def basis():
        with jax.named_scope("q6_basis"):
            high, low = split(work[...])
            pair = jnp.concatenate([high, low], axis=1)
            for i in range(STEPS):
                block = rows // STEPS
                at = slice(i * block, (i + 1) * block)
                top = jnp.concatenate([turned[r, :tall, at] for r in range(parts)], axis=0)
                bottom = jnp.concatenate([turned[r, tall:, at] for r in range(parts)], axis=0)
                value = dot(pair, jnp.concatenate([top, top], axis=0), NORMAL) + dot(high, bottom, NORMAL)
                high_t, low_t = split(value.T)
                pair_ref[at, :rank] = high_t
                pair_ref[at, rank:] = low_t

    def correct(start, stop):
        with jax.named_scope("q7_right"):
            wide = jnp.concatenate([totals[c] for c in range(start, stop)], axis=1)
            value = dot(wide, work[...], ((0,), (1,)), HIGHEST)
            right_ref[start * chunk : stop * chunk, :] = value
            column = jnp.sum(value * value, axis=0, keepdims=True)
            squares[me] = squares[me] + jnp.broadcast_to(column, (8, rank))

    squares[me] = jnp.zeros((8, rank), jnp.float32)

    @pl.when(outer)
    def _():
        plan = list(queue)
        second_at = next((i for i, (step, u) in enumerate(plan) if step is near and 2 * u >= 3 * count), 0)
        third_at = next((i for i, (step, u) in enumerate(plan) if step is far and u >= THIRD), len(plan) - 1)
        third_at = max(third_at, second_at)
        at = 0
        for i, (step, u) in enumerate(plan):
            if i == second_at:
                with jax.named_scope("q4_gram2"):
                    gram_spread(1)
            with jax.named_scope(f"q3_{step.__name__}{u}"):
                far(u, True) if step is far else near(u)
            if i == third_at:
                rest, across_lanes = second()
            if i >= third_at and step is far:
                stop = blocks if i == len(plan) - 1 else min(at + SHARE, blocks)
                rest = invert(rest, at, stop)
                at = stop
        keep(rest, across_lanes)
        for c in range(0, count, 2):
            correct(c, min(c + 2, count))

    @pl.when(jnp.logical_not(outer))
    def _():
        with jax.named_scope("q4_gram2"):
            gram_spread(1)
        rest, across_lanes = second()
        keep(invert(rest, 0, blocks), across_lanes)
        for u in range(units):
            with jax.named_scope(f"q3_end{u}"):
                far(u, False)
            if u == units - 1 - 2 * per:
                for c in range(0, count - 2 * per, 2):
                    correct(c, c + 2)
        for c in range(max(count - 2 * per, 0) if count > 2 * per else 0, count, 2):
            correct(c, min(c + 2, count))

    with jax.named_scope("q8_squares"):
        for k in range(1, plane):
            remote(squares.at[me], squares.at[me], once.at[7], once.at[8], peer(k)[1]).start()
    basis()
    with jax.named_scope("q9_momentum"):
        scaled = (right_ref[...] * (decay_rate - 1.0)).astype(jnp.bfloat16)

        def update(i, carry):
            block = rows // STEPS
            at = pl.ds(pl.multiple_of(i * block, 8), block)
            mixed[at, :] = mixed[at, :] + dot(pair_ref[at, :rank], scaled, TURNED)
            return carry

        lax.fori_loop(0, STEPS, update, 0)
    with jax.named_scope("r0_follow"):
        if plane > 1:
            part = squares.at[pl.ds(0, plane - 1)]
            remote(part, part, once.at[7], once.at[8], peer(1)[1]).wait()
        mean = summed(squares, plane)[:1] / (cols * plane)
        following_ref[...] = right_ref[...] / jnp.sqrt(mean + epsilon)
        if depth > 1:
            remote(sums, sums, chain_send.at[0], chain_recv.at[0, 0], {"shard": s + step_in}).wait_send()

            @pl.when(outer)
            def _():
                remote(totals, totals, chain_send.at[1], chain_recv.at[0, 0], {"shard": s - step_in}).wait_send()


def finish(scale, mixed_ref, pair_ref, following_ref, next_ref, direction_ref, out_ref, direction_vmem, sems):
    rows = mixed_ref.shape[0]
    rank = following_ref.shape[1]
    block = rows // STEPS
    moves = (
        pltpu.make_async_copy(mixed_ref, next_ref, sems.at[0]),
        pltpu.make_async_copy(following_ref, out_ref, sems.at[1]),
    )
    for copy in moves:
        copy.start()
    high, low = split(following_ref[...] * scale)
    follow = jnp.concatenate([high, high], axis=1)
    for i in range(STEPS):
        at = pl.ds(i * block, block)
        value = dot(pair_ref[at, :], follow, TURNED) + dot(pair_ref[at, :rank], low, TURNED)
        direction_vmem[at, :] = value.astype(jnp.bfloat16)
        pltpu.make_async_copy(direction_vmem.at[at], direction_ref.at[at], sems.at[2]).start()
    for copy in moves:
        copy.wait()
    pltpu.make_async_copy(direction_vmem, direction_ref, sems.at[2]).wait()


def shards(shape, gradient, momentum, prior_right_factor):
    gradient, momentum, prior = gradient[0], momentum[0], prior_right_factor[0]
    rows, cols = momentum.shape
    rank = prior.shape[1]
    z = shape["shard"]
    plane = shape["tensor"] * shape["dp"]
    cores = 2 if shape["tensor"] % 2 == 0 else 1
    chips = plane // cores
    own = rows // plane
    group, chunk = widths(cols)
    count = cols // chunk
    parts = 2 if rank % 16 == 0 else 1
    dma = pltpu.SemaphoreType.DMA
    vmem = pl.BlockSpec(memory_space=pltpu.VMEM)
    hbm = pl.BlockSpec(memory_space=pltpu.HBM)
    f32, bf16 = jnp.float32, jnp.bfloat16
    others = max(chips - 1, 1)
    mixed, pair, following = pl.pallas_call(
        functools.partial(factors, shape),
        out_shape=[
            pltpu.VMEM((rows, cols), f32),
            pltpu.VMEM((rows, 2 * rank), bf16),
            pltpu.VMEM((cols, rank), f32),
        ],
        in_specs=[hbm, hbm, hbm],
        out_specs=[vmem, vmem, vmem],
        scratch_shapes=[
            pltpu.VMEM((cols, rank), f32),
            pltpu.VMEM((rows, cols), bf16),
            pltpu.VMEM((rows, cols), bf16),
            pltpu.VMEM((rows, cols), bf16),
            pltpu.VMEM((cols, rank), f32),
            pltpu.VMEM((cols, 2 * rank), bf16),
            pltpu.VMEM((rows, rank), f32),
            pltpu.VMEM((chips, own, rank), f32),
            pltpu.VMEM((others, own, rank), f32),
            pltpu.VMEM((rows, rank), f32),
            pltpu.VMEM((2, rows, 2 * rank), bf16),
            pltpu.VMEM((parts, 2 * rank // parts, rows), bf16),
            pltpu.VMEM((count, rank, chunk), f32),
            pltpu.VMEM((count, rank, chunk), f32),
            pltpu.VMEM((2, count, rank, chunk), f32),
            pltpu.VMEM((2, plane, rank // plane, rank), f32),
            pltpu.VMEM((2, plane, rank // plane, rank), f32),
            pltpu.VMEM((2, z, rank // plane, rank), f32),
            pltpu.VMEM((2, plane, rank // plane, rank), f32),
            pltpu.VMEM((plane, 8, rank), f32),
            pltpu.VMEM((rank, rank), f32),
            dma((2, AHEAD)),
            dma,
            dma((chips,)),
            dma((9,)),
            dma((2, 3)),
            dma((2, 3)),
            dma((2,)),
            dma((2, 2 * count)),
        ],
        compiler_params=pltpu.CompilerParams(
            collective_id=0, has_side_effects=True, vmem_limit_bytes=36 * MiB
        ),
        name="factors",
    )(*(pltpu.with_memory_space_constraint(x, pltpu.HBM) for x in (momentum, gradient, prior)))

    scale = float((rows * z / rank) ** 0.5)
    momentum_next, direction, following = pl.pallas_call(
        functools.partial(finish, scale),
        out_shape=[
            jax.ShapeDtypeStruct((rows, cols), f32),
            jax.ShapeDtypeStruct((rows, cols), bf16),
            jax.ShapeDtypeStruct((cols, rank), f32),
        ],
        in_specs=[vmem, vmem, vmem],
        out_specs=[hbm, hbm, hbm],
        scratch_shapes=[pltpu.VMEM((rows, cols), bf16), dma((3,))],
        compiler_params=pltpu.CompilerParams(vmem_limit_bytes=24 * MiB),
        name="finish",
    )(mixed, pair, following)
    return momentum_next[None], following[None], direction[None]


def solution(mesh):
    return jax.shard_map(
        functools.partial(shards, dict(mesh.shape)),
        mesh=mesh,
        in_specs=(
            P(None, "shard", ("tensor", "dp")),
            P(None, "shard", ("tensor", "dp")),
            P(None, ("tensor", "dp"), None),
        ),
        out_specs=(
            P(None, "shard", ("tensor", "dp")),
            P(None, ("tensor", "dp"), None),
            P(None, "shard", ("tensor", "dp")),
        ),
        check_vma=False,
    )
```

```python
import functools

import jax
import jax.numpy as jnp
from jax import lax
from jax.experimental import pallas as pl
from jax.experimental.pallas import tpu as pltpu
from jax.sharding import PartitionSpec as P

MESH = pl.DeviceIdType.MESH
HIGHEST = lax.Precision.HIGHEST
decay_rate = 0.95
epsilon = 1e-06
STEPS = 8
AHEAD = 3
GAP = 5.3
THIRD = 12
SHARE = 2
MOVES = (1, 1, 1, 2, 2, 3)
MiB = 1024 * 1024
ROWS, NORMAL, TURNED = ((0,), (0,)), ((1,), (0,)), ((1,), (1,))


def dot(a, b, dims, precision=None):
    return lax.dot_general(
        a, b, (dims, ((), ())), precision=precision, preferred_element_type=jnp.float32
    )


def split(value):
    high = value.astype(jnp.bfloat16)
    low = (value - high.astype(jnp.float32)).astype(jnp.bfloat16)
    return high, low


def split3(value):
    high = value.astype(jnp.bfloat16)
    rest = value - high.astype(jnp.float32)
    middle = rest.astype(jnp.bfloat16)
    return high, middle, (rest - middle.astype(jnp.float32)).astype(jnp.bfloat16)


def inverse_steps(a, start, stop):
    size = a.shape[0]
    sub = lax.broadcasted_iota(jnp.int32, (8, size), 0)
    lane = lax.broadcasted_iota(jnp.int32, (8, size), 1)
    rows = lax.broadcasted_iota(jnp.int32, (size, size), 0)
    lanes = lax.broadcasted_iota(jnp.int32, (size, size), 1)

    def row(value, index):
        return jnp.broadcast_to(value[index : index + 1], value.shape)

    def block(step, a):
        top = a[:8]
        columns = [jnp.broadcast_to(top[:, c : c + 1], (8, size)) for c in range(8)]
        panel = jnp.where(lane < 8, jnp.where(lane == sub, 1.0, 0.0), top)
        scale = jnp.zeros((8, size), jnp.float32)
        for c in range(8):
            inverse_root = lax.rsqrt(row(columns[c], c))
            scale = jnp.where(sub == c, inverse_root, scale)
            factor = jnp.where(sub > c, columns[c] * (inverse_root * inverse_root), 0.0)
            panel = panel - factor * row(panel, c)
            for j in range(c + 1, 8):
                columns[j] = columns[j] - factor * row(columns[j], c)
        square = scale * scale
        solved = panel * square
        for c in range(7, 0, -1):
            solved = solved - jnp.where(sub < c, columns[c] * square, 0.0) * row(solved, c)
        active = rows < size - 8 * step
        source = jnp.where(active, a, 0.0)[8:]
        rest = jnp.where(active & (lanes < 8), 0.0, a)[8:]
        for c in range(8):
            rest = rest - jnp.broadcast_to(source[:, c : c + 1], rest.shape) * jnp.broadcast_to(
                solved[c : c + 1], rest.shape
            )
        return pltpu.roll(jnp.concatenate([rest, panel * scale], axis=0), size - 8, 1)

    return lax.fori_loop(start, stop, block, a)


def unit_diagonal(gram):
    rows = lax.broadcasted_iota(jnp.int32, gram.shape, 0)
    lanes = lax.broadcasted_iota(jnp.int32, gram.shape, 1)
    diagonal = jnp.where(rows == lanes, gram, 0.0)
    across = lax.rsqrt(jnp.sum(diagonal, axis=0, keepdims=True))
    down = lax.rsqrt(jnp.sum(diagonal, axis=1, keepdims=True))
    return gram * across * down, across

def eliminate(blocks, k):
    size = blocks[0].shape[1]
    sub = lax.broadcasted_iota(jnp.int32, (8, size), 0)
    lane = lax.broadcasted_iota(jnp.int32, (8, size), 1) - 8 * k
    here = (lane >= 0) & (lane < 8)

    def row(value, index):
        return jnp.broadcast_to(value[index : index + 1], value.shape)

    def column(value, index):
        return jnp.broadcast_to(value[:, 8 * k + index : 8 * k + index + 1], value.shape)

    top = blocks[k]
    columns = [column(top, c) for c in range(8)]
    e = {(i, j): row(columns[j], i) for j in range(8) for i in range(j, 8)}
    panel = jnp.where(here, jnp.where(lane == sub, 1.0, 0.0), top)
    x = [row(panel, i) for i in range(8)]
    y, z, f = [None] * 8, [None] * 8, {}
    for p in range(0, 8, 2):
        a, b, c = e[p, p], e[p + 1, p], e[p + 1, p + 1]
        root = lax.rsqrt(a * c - b * b)
        inverse = root * root
        g = {}
        for i in range(p + 2, 8):
            g[i] = (e[i, p] * c - e[i, p + 1] * b, e[i, p + 1] * a - e[i, p] * b)
        for i in range(p + 2, 8):
            for j in range(p + 2, i + 1):
                e[i, j] = e[i, j] - (g[i][0] * e[j, p] + g[i][1] * e[j, p + 1]) * inverse
        for i in range(p + 2, 8):
            f[i, p], f[i, p + 1] = g[i][0] * inverse, g[i][1] * inverse
            x[i] = x[i] - (f[i, p] * x[p] + f[i, p + 1] * x[p + 1])
        first = lax.rsqrt(a)
        y[p] = x[p] * first
        y[p + 1] = (x[p + 1] * a - b * x[p]) * (first * root)
        z[p] = (c * x[p] - b * x[p + 1]) * inverse
        z[p + 1] = (a * x[p + 1] - b * x[p]) * inverse
    for p in (4, 2, 0):
        for i in range(p + 2, 8):
            z[p] = z[p] - f[i, p] * z[i]
            z[p + 1] = z[p + 1] - f[i, p + 1] * z[i]
    done = y[0]
    for i in range(1, 8):
        done = jnp.where(sub == i, y[i], done)
    out = list(blocks)
    out[k] = done
    for r in range(k + 1, len(blocks)):
        rest = jnp.where(here, 0.0, blocks[r])
        for c in range(8):
            rest = rest - column(blocks[r], c) * z[c]
        out[r] = rest
    return out


def lower(a, start=0):
    rows = lax.broadcasted_iota(jnp.int32, a.shape, 0) + start
    lanes = lax.broadcasted_iota(jnp.int32, a.shape, 1)
    return jnp.where(rows >= lanes, a, 0.0)


def remote(src, dst, send_sem, recv_sem, device):
    return pltpu.make_async_remote_copy(
        src_ref=src, dst_ref=dst, send_sem=send_sem, recv_sem=recv_sem, device_id=device, device_id_type=MESH
    )


def widths(cols):
    group = 256 if cols % 256 == 0 else cols
    chunk = 128 if group % 128 == 0 else group
    return group, chunk


def factors(shape, momentum_ref, gradient_ref, prior_ref, mixed, pair_ref, following_ref, right_ref, raw, wide_high, wide_low, prior_vmem, prior_pair, left, core_in, plane_in, whole, fine, turned, sums, totals,
            arrive, pieces, piece_in, piece_z, piece_all, squares, work, load_sem, prior_sem, core_recv, once,
            gram_send, gram_recv, chain_send, chain_recv):
    rows, cols = mixed.shape
    rank = prior_ref.shape[1]
    depth, dp = shape["shard"], shape["dp"]
    cores = 2 if shape["tensor"] % 2 == 0 else 1
    nx = shape["tensor"] // cores
    chips = nx * dp
    plane = chips * cores
    own = rows // plane
    s, t, y = lax.axis_index("shard"), lax.axis_index("tensor"), lax.axis_index("dp")
    core, x = lax.rem(t, cores), lax.div(t, cores)
    me = t * dp + y

    def chip(offset):
        px = lax.rem(x + lax.div(offset, dp), nx)
        py = lax.rem(y + lax.rem(offset, dp), dp)
        return px * dp + py, {"tensor": px * cores + core, "dp": py}

    def place(half, index):
        return pl.ds(pl.multiple_of((half * chips + index) * own, 8), own)

    def peer(k):
        other = lax.rem(me + k, plane)
        return other, {"tensor": lax.div(other, dp), "dp": lax.rem(other, dp)}

    def across(k):
        other = lax.rem(s + k, depth)
        return other, {"shard": other}

    partner = {"tensor": x * cores + cores - 1 - core}

    def load(slot, at):
        return (
            pltpu.make_async_copy(momentum_ref.at[at], mixed.at[at], load_sem.at[0, lax.rem(slot, AHEAD)]),
            pltpu.make_async_copy(gradient_ref.at[at], raw.at[at], load_sem.at[1, lax.rem(slot, AHEAD)]),
        )

    loads = chips * cores

    def spot(slot):
        i = lax.div(slot, cores)
        half = lax.rem(core + 1 + lax.rem(slot, cores), cores)
        return place(half, chip(chips - 1 - i)[0])

    prior_copy = pltpu.make_async_copy(prior_ref, prior_vmem, prior_sem)
    for slot in range(min(AHEAD, loads)):
        for copy in load(slot, spot(slot)):
            copy.start()
        if slot == 0:
            prior_copy.start()

    barrier = pltpu.get_barrier_semaphore()
    for k in range(1, plane):
        pl.semaphore_signal(barrier, inc=1, device_id=peer(k)[1], device_id_type=MESH)
    for k in range(1, depth):
        pl.semaphore_signal(barrier, inc=1, device_id=across(k)[1], device_id_type=MESH)

    half_depth = max(depth // 2, 1)
    first = s < half_depth
    level = jnp.where(first, s, depth - 1 - s)
    outer = level > 0
    middle = level == half_depth - 1
    step_in = jnp.where(first, 1, -1)
    group, chunk = widths(cols)
    count = cols // chunk

    prior_copy.wait()
    high, low = split(prior_vmem[...])
    prior_pair[:, :rank] = high
    prior_pair[:, rank:] = low
    pl.semaphore_wait(barrier, plane + depth - 2)

    def product(slot, at):
        for copy in load(slot, at):
            copy.wait()
        ahead = slot + AHEAD

        @pl.when(ahead < loads)
        def _():
            for copy in load(ahead, spot(ahead)):
                copy.start()

        value = mixed[at, :] + raw[at, :].astype(jnp.float32)
        mixed[at, :] = value
        high, low = split(value)
        wide_high[at, :] = high
        wide_low[at, :] = low
        both = dot(high, prior_pair[...], NORMAL) + dot(low, prior_pair[...], NORMAL)
        return both[:, :rank] + both[:, rank:]

    def core_copy(i):
        at = place(cores - 1 - core, chip(chips - 1 - i)[0])
        return remote(left.at[at], core_in.at[i], once.at[0], core_recv.at[i], partner)

    def plane_copy(offset):
        index, device = chip(offset)
        slot = offset - 1
        return remote(left.at[place(core, index)], plane_in.at[slot], once.at[1], once.at[2], device)

    def bulk(first):
        return remote(plane_in, plane_in, once.at[first], once.at[first + 1], chip(1)[1])

    def settle(i):
        offset = chips - 1 - i
        at = place(core, chip(offset)[0])
        if cores == 2:
            core_copy(i).wait_recv()
            left[at, :] = left[at, :] + core_in[i]
        return offset

    def partial(slot, carry):
        i = lax.div(slot, cores)
        at = spot(slot)
        left[at, :] = product(slot, at)
        if cores == 2:

            @pl.when(lax.rem(slot, cores) == 0)
            def _():
                core_copy(i).start()

        @pl.when(jnp.logical_and(lax.rem(slot, cores) == 0, slot > 0))
        def _():
            plane_copy(settle(i - 1)).start()

        return carry

    with jax.named_scope("p1_left"):
        lax.fori_loop(0, loads, partial, 0)

    mine = place(core, x * dp + y)
    with jax.named_scope("p3_rswait"):
        settle(chips - 1)
        total = left[mine, :]
        if chips > 1:
            bulk(1).wait_recv()
        for offset in range(1, chips):
            total = total + plane_in[offset - 1]
        whole[mine, :] = total

    piece = rank // plane

    def summed(slots, n):
        value = slots[0]
        for i in range(1, n):
            value = value + slots[i]
        return value

    def gram_sends(turn, stage, n, find, source, target):
        for k in range(1, n):
            other, device = find(k)
            remote(source(other), target, gram_send.at[turn, stage], gram_recv.at[turn, stage], device).start()

    def gram_wait(turn, stage, n, find, slots):
        if n > 1:
            part = slots.at[turn, pl.ds(0, n - 1)]
            remote(part, part, gram_send.at[turn, stage], gram_recv.at[turn, stage], find(1)[1]).wait()

    def gram_start(turn, gram):
        for i in range(plane):
            pieces[turn, i] = gram[i * piece : (i + 1) * piece]
        piece_in[turn, me] = pieces[turn, me]
        gram_sends(turn, 0, plane, peer, lambda i: pieces.at[turn, i], piece_in.at[turn, me])

    def gram_across(turn):
        gram_wait(turn, 0, plane, peer, piece_in)
        piece_z[turn, s] = summed(piece_in.at[turn], plane)
        mine_z = piece_z.at[turn, s]
        gram_sends(turn, 1, depth, across, lambda i: mine_z, mine_z)

    def gram_spread(turn):
        gram_wait(turn, 1, depth, across, piece_z)
        piece_all[turn, me] = summed(piece_z.at[turn], depth)
        mine_all = piece_all.at[turn, me]
        gram_sends(turn, 2, plane, peer, lambda i: mine_all, mine_all)

    def gram_whole(turn):
        gram_wait(turn, 2, plane, peer, piece_all)
        return jnp.concatenate([piece_all[turn, i] for i in range(plane)], axis=0)

    with jax.named_scope("p4_gram"):
        gram_start(0, dot(total, total, ROWS, HIGHEST))
    for offset in range(1, chips):
        remote(whole.at[mine], whole.at[mine], once.at[3], once.at[4], chip(offset)[1]).start()
    with jax.named_scope("p5_gram1"):
        gram_across(0)
    with jax.named_scope("p6_gram2"):
        gram_spread(0)
    def refine(half):
        block = rows // STEPS
        for i in range(STEPS // cores):
            at = pl.ds(pl.multiple_of(half * (rows // cores) + i * block, 8), block)
            high, middle_part, low = split3(whole[at, :])
            fine[0, at, :rank] = high
            fine[0, at, rank:] = middle_part
            fine[1, at, :rank] = high
            fine[1, at, rank:] = low

    with jax.named_scope("p7_agwait"):
        if chips > 1:
            bulk(1).wait_send()
            bulk(3).wait()
        if cores == 2:
            at = pl.ds(pl.multiple_of(core * (rows // 2), 8), rows // 2)
            remote(left.at[at], left.at[at], once.at[0], once.at[0], partner).wait_send()
            half_copy = remote(whole.at[at], whole.at[at], once.at[5], once.at[6], partner)
            half_copy.start()
            refine(core)
    with jax.named_scope("p8_gram3"):
        gram = gram_whole(0)
    parts = 2 if rank % 16 == 0 else 1
    tall = rank // parts
    units = count * parts
    blocks = rank // 8
    per = group // chunk
    groups = cols // group

    def unit(ref, u):
        return ref.at[u % count, pl.ds((u // count) * tall, tall)]

    def inward(u):
        slot = jnp.where(middle, 1, 0)
        return remote(unit(sums, u), unit(arrive.at[slot], u), chain_send.at[0], chain_recv.at[slot, u],
                      {"shard": s + step_in})

    def outward(u):
        return remote(unit(totals, u), unit(arrive.at[1], u), chain_send.at[1], chain_recv.at[1, u],
                      {"shard": s - step_in})

    def landed(slot, u):
        remote(unit(sums, u), unit(arrive.at[slot], u), chain_send.at[0], chain_recv.at[slot, u],
               {"shard": s + step_in}).wait_recv()

    def near(u):
        landed(0, u)
        unit(sums, u)[...] = unit(sums, u)[...] + unit(arrive.at[0], u)[...]
        inward(u).start()

    def far(u, forward):
        if depth > 1:
            landed(1, u)
            got = unit(arrive.at[1], u)[...]
            unit(totals, u)[...] = jnp.where(middle, unit(sums, u)[...] + got, got)
            if forward:
                outward(u).start()
        else:
            unit(totals, u)[...] = unit(sums, u)[...]

    def due(step, u):
        late = 0.0 if u < count else 1.7 if 2 * u < 3 * count else 2.4
        return u + late + (GAP if step is far else 0.0)

    queue = sorted(((step, u) for u in range(units) for step in (near, far)), key=lambda item: due(*item))

    def take(n, computed):
        steps = []
        while len(steps) < n and len(queue) > 1 and queue[0][1] < computed:
            steps.append(queue.pop(0))
        if depth > 2 and steps:

            @pl.when(outer)
            def _():
                for step, u in steps:
                    with jax.named_scope(f"q3_{step.__name__}{u}"):
                        step(u, True) if step is far else step(u)

    def basis_half(r, w):
        if r == 0:
            refine(cores - 1 - core)
        for i in range(STEPS):
            block = rows // STEPS
            at = slice(i * block, (i + 1) * block)
            value = value_of(w, fine[0, at, :], fine[1, at, :])
            high, low = split(value)
            turned[r, :tall, at] = high
            turned[r, tall:, at] = low

    def value_of(w, block, tail_block):
        w_high, w_middle, w_low = split3(w)
        ends = jnp.concatenate(
            [jnp.concatenate([w_high, w_middle], axis=1), jnp.concatenate([w_middle, w_high], axis=1)], axis=0
        )
        both = dot(ends, block, TURNED)
        return both[:tall] + (both[tall:] + dot(jnp.concatenate([w_low, w_high], axis=1), tail_block, TURNED))

    def right_group(r, g):
        at = slice(g * group, (g + 1) * group)
        both = dot(turned[r], wide_high[:, at], NORMAL)
        value = both[:tall] + both[tall:] + dot(turned[r, :tall, :], wide_low[:, at], NORMAL)
        for i in range(per):
            sums[g * per + i, r * tall : (r + 1) * tall, :] = value[:, i * chunk : (i + 1) * chunk]

    def right_send(r, g):
        if depth > 1:

            @pl.when(jnp.logical_not(outer))
            def _():
                for i in range(per):
                    inward(r * count + g * per + i).start()

    with jax.named_scope("p9_inv1"):
        scaled, lanes = unit_diagonal(gram)
        rest = [scaled[8 * i : 8 * i + 8] for i in range(blocks)]
        weights = []
    for r in range(parts):
        with jax.named_scope(f"p9_half{r}"):
            first_block, stop = r * blocks // parts, (r + 1) * blocks // parts
            for k in range(first_block, stop):
                rest = eliminate(rest, k)
                if r > 0 and k == first_block + 5:
                    take(1, r * count)
            weights.append(lower(jnp.concatenate(rest[first_block:stop], axis=0), 8 * first_block) * lanes)
        last_part = r == parts - 1
        if last_part:
            take(1, r * count)
            with jax.named_scope("q1_gram"):
                if r == 0 and cores == 2:
                    half_copy.wait()
                high, middle_part, low = split3(whole[mine, :])
                block = jnp.concatenate([high, middle_part], axis=1)
                tail_block = jnp.concatenate([high, low], axis=1)
                part = jnp.concatenate([value_of(w, block, tail_block) for w in weights], axis=0)
                gram_start(1, dot(part, part, TURNED, HIGHEST))
            take(MOVES[0], r * count)
        with jax.named_scope(f"q0_value{r}"):
            if cores == 2 and r == 0 and not last_part:
                half_copy.wait()
            basis_half(r, weights[r])
        if last_part:
            take(MOVES[1], r * count)
        for g in range(groups):
            with jax.named_scope(f"q2_right{r}{g}"):
                right_group(r, g)
            if last_part and g == min(2, groups - 1):
                with jax.named_scope("q2_gram1"):
                    gram_across(1)
            right_send(r, g)
            if last_part:
                take(MOVES[2 + min(g, 3)], r * count + (g + 1) * per)

    def second():
        with jax.named_scope("q4_gram3"):
            scaled, across_lanes = unit_diagonal(gram_whole(1))
        return [scaled[8 * i : 8 * i + 8] for i in range(blocks)], across_lanes

    def invert(rest, start, stop):
        with jax.named_scope("q5_inv2"):
            for k in range(start, stop):
                rest = eliminate(rest, k)
        return rest

    def keep(rest, across_lanes):
        work[...] = lower(jnp.concatenate(rest, axis=0)) * across_lanes

    def basis():
        with jax.named_scope("q6_basis"):
            high, low = split(work[...])
            pair = jnp.concatenate([high, low], axis=1)
            for i in range(STEPS):
                block = rows // STEPS
                at = slice(i * block, (i + 1) * block)
                top = jnp.concatenate([turned[r, :tall, at] for r in range(parts)], axis=0)
                bottom = jnp.concatenate([turned[r, tall:, at] for r in range(parts)], axis=0)
                value = dot(pair, jnp.concatenate([top, top], axis=0), NORMAL) + dot(high, bottom, NORMAL)
                high_t, low_t = split(value.T)
                pair_ref[at, :rank] = high_t
                pair_ref[at, rank:] = low_t

    def correct(start, stop):
        with jax.named_scope("q7_right"):
            wide = jnp.concatenate([totals[c] for c in range(start, stop)], axis=1)
            value = dot(wide, work[...], ((0,), (1,)), HIGHEST)
            right_ref[start * chunk : stop * chunk, :] = value
            column = jnp.sum(value * value, axis=0, keepdims=True)
            squares[me] = squares[me] + jnp.broadcast_to(column, (8, rank))

    squares[me] = jnp.zeros((8, rank), jnp.float32)

    @pl.when(outer)
    def _():
        plan = list(queue)
        second_at = next((i for i, (step, u) in enumerate(plan) if step is near and 2 * u >= 3 * count), 0)
        third_at = next((i for i, (step, u) in enumerate(plan) if step is far and u >= THIRD), len(plan) - 1)
        third_at = max(third_at, second_at)
        at = 0
        for i, (step, u) in enumerate(plan):
            if i == second_at:
                with jax.named_scope("q4_gram2"):
                    gram_spread(1)
            with jax.named_scope(f"q3_{step.__name__}{u}"):
                far(u, True) if step is far else near(u)
            if i == third_at:
                rest, across_lanes = second()
            if i >= third_at and step is far:
                stop = blocks if i == len(plan) - 1 else min(at + SHARE, blocks)
                rest = invert(rest, at, stop)
                at = stop
        keep(rest, across_lanes)
        for c in range(0, count, 2):
            correct(c, min(c + 2, count))

    @pl.when(jnp.logical_not(outer))
    def _():
        with jax.named_scope("q4_gram2"):
            gram_spread(1)
        rest, across_lanes = second()
        keep(invert(rest, 0, blocks), across_lanes)
        for u in range(units):
            with jax.named_scope(f"q3_end{u}"):
                far(u, False)
            if u == units - 1 - 2 * per:
                for c in range(0, count - 2 * per, 2):
                    correct(c, c + 2)
        for c in range(max(count - 2 * per, 0) if count > 2 * per else 0, count, 2):
            correct(c, min(c + 2, count))

    with jax.named_scope("q8_squares"):
        for k in range(1, plane):
            remote(squares.at[me], squares.at[me], once.at[7], once.at[8], peer(k)[1]).start()
    basis()
    with jax.named_scope("q9_momentum"):
        scaled = (right_ref[...] * (decay_rate - 1.0)).astype(jnp.bfloat16)

        def update(i, carry):
            block = rows // STEPS
            at = pl.ds(pl.multiple_of(i * block, 8), block)
            mixed[at, :] = mixed[at, :] + dot(pair_ref[at, :rank], scaled, TURNED)
            return carry

        lax.fori_loop(0, STEPS, update, 0)
    with jax.named_scope("r0_follow"):
        if plane > 1:
            part = squares.at[pl.ds(0, plane - 1)]
            remote(part, part, once.at[7], once.at[8], peer(1)[1]).wait()
        mean = summed(squares, plane)[:1] / (cols * plane)
        following_ref[...] = right_ref[...] / jnp.sqrt(mean + epsilon)
        if depth > 1:
            remote(sums, sums, chain_send.at[0], chain_recv.at[0, 0], {"shard": s + step_in}).wait_send()

            @pl.when(outer)
            def _():
                remote(totals, totals, chain_send.at[1], chain_recv.at[0, 0], {"shard": s - step_in}).wait_send()


def finish(scale, mixed_ref, pair_ref, following_ref, next_ref, direction_ref, out_ref, direction_vmem, sems):
    rows = mixed_ref.shape[0]
    rank = following_ref.shape[1]
    block = rows // STEPS
    moves = (
        pltpu.make_async_copy(mixed_ref, next_ref, sems.at[0]),
        pltpu.make_async_copy(following_ref, out_ref, sems.at[1]),
    )
    for copy in moves:
        copy.start()
    high, low = split(following_ref[...] * scale)
    follow = jnp.concatenate([high, high], axis=1)
    for i in range(STEPS):
        at = pl.ds(i * block, block)
        value = dot(pair_ref[at, :], follow, TURNED) + dot(pair_ref[at, :rank], low, TURNED)
        direction_vmem[at, :] = value.astype(jnp.bfloat16)
        pltpu.make_async_copy(direction_vmem.at[at], direction_ref.at[at], sems.at[2]).start()
    for copy in moves:
        copy.wait()
    pltpu.make_async_copy(direction_vmem, direction_ref, sems.at[2]).wait()


def shards(shape, gradient, momentum, prior_right_factor):
    gradient, momentum, prior = gradient[0], momentum[0], prior_right_factor[0]
    rows, cols = momentum.shape
    rank = prior.shape[1]
    z = shape["shard"]
    plane = shape["tensor"] * shape["dp"]
    cores = 2 if shape["tensor"] % 2 == 0 else 1
    chips = plane // cores
    own = rows // plane
    group, chunk = widths(cols)
    count = cols // chunk
    parts = 2 if rank % 16 == 0 else 1
    dma = pltpu.SemaphoreType.DMA
    vmem = pl.BlockSpec(memory_space=pltpu.VMEM)
    hbm = pl.BlockSpec(memory_space=pltpu.HBM)
    f32, bf16 = jnp.float32, jnp.bfloat16
    others = max(chips - 1, 1)
    mixed, pair, following = pl.pallas_call(
        functools.partial(factors, shape),
        out_shape=[
            pltpu.VMEM((rows, cols), f32),
            pltpu.VMEM((rows, 2 * rank), bf16),
            pltpu.VMEM((cols, rank), f32),
        ],
        in_specs=[hbm, hbm, hbm],
        out_specs=[vmem, vmem, vmem],
        scratch_shapes=[
            pltpu.VMEM((cols, rank), f32),
            pltpu.VMEM((rows, cols), bf16),
            pltpu.VMEM((rows, cols), bf16),
            pltpu.VMEM((rows, cols), bf16),
            pltpu.VMEM((cols, rank), f32),
            pltpu.VMEM((cols, 2 * rank), bf16),
            pltpu.VMEM((rows, rank), f32),
            pltpu.VMEM((chips, own, rank), f32),
            pltpu.VMEM((others, own, rank), f32),
            pltpu.VMEM((rows, rank), f32),
            pltpu.VMEM((2, rows, 2 * rank), bf16),
            pltpu.VMEM((parts, 2 * rank // parts, rows), bf16),
            pltpu.VMEM((count, rank, chunk), f32),
            pltpu.VMEM((count, rank, chunk), f32),
            pltpu.VMEM((2, count, rank, chunk), f32),
            pltpu.VMEM((2, plane, rank // plane, rank), f32),
            pltpu.VMEM((2, plane, rank // plane, rank), f32),
            pltpu.VMEM((2, z, rank // plane, rank), f32),
            pltpu.VMEM((2, plane, rank // plane, rank), f32),
            pltpu.VMEM((plane, 8, rank), f32),
            pltpu.VMEM((rank, rank), f32),
            dma((2, AHEAD)),
            dma,
            dma((chips,)),
            dma((9,)),
            dma((2, 3)),
            dma((2, 3)),
            dma((2,)),
            dma((2, 2 * count)),
        ],
        compiler_params=pltpu.CompilerParams(
            collective_id=0, has_side_effects=True, vmem_limit_bytes=36 * MiB
        ),
        name="factors",
    )(*(pltpu.with_memory_space_constraint(x, pltpu.HBM) for x in (momentum, gradient, prior)))

    scale = float((rows * z / rank) ** 0.5)
    momentum_next, direction, following = pl.pallas_call(
        functools.partial(finish, scale),
        out_shape=[
            jax.ShapeDtypeStruct((rows, cols), f32),
            jax.ShapeDtypeStruct((rows, cols), bf16),
            jax.ShapeDtypeStruct((cols, rank), f32),
        ],
        in_specs=[vmem, vmem, vmem],
        out_specs=[hbm, hbm, hbm],
        scratch_shapes=[pltpu.VMEM((rows, cols), bf16), dma((3,))],
        compiler_params=pltpu.CompilerParams(vmem_limit_bytes=24 * MiB),
        name="finish",
    )(mixed, pair, following)
    return momentum_next[None], following[None], direction[None]


def solution(mesh):
    return jax.shard_map(
        functools.partial(shards, dict(mesh.shape)),
        mesh=mesh,
        in_specs=(
            P(None, "shard", ("tensor", "dp")),
            P(None, "shard", ("tensor", "dp")),
            P(None, ("tensor", "dp"), None),
        ),
        out_specs=(
            P(None, "shard", ("tensor", "dp")),
            P(None, ("tensor", "dp"), None),
            P(None, "shard", ("tensor", "dp")),
        ),
        check_vma=False,
    )
```

```python
import functools

import jax
import jax.numpy as jnp
from jax import lax
from jax.experimental import pallas as pl
from jax.experimental.pallas import tpu as pltpu
from jax.sharding import PartitionSpec as P

MESH = pl.DeviceIdType.MESH
HIGHEST = lax.Precision.HIGHEST
decay_rate = 0.95
epsilon = 1e-06
STEPS = 8
AHEAD = 3
GAP = 5.3
THIRD = 12
SHARE = 2
MOVES = (1, 1, 1, 2, 2, 3)
MiB = 1024 * 1024
ROWS, NORMAL, TURNED = ((0,), (0,)), ((1,), (0,)), ((1,), (1,))


def dot(a, b, dims, precision=None):
    return lax.dot_general(
        a, b, (dims, ((), ())), precision=precision, preferred_element_type=jnp.float32
    )


def split(value):
    high = value.astype(jnp.bfloat16)
    low = (value - high.astype(jnp.float32)).astype(jnp.bfloat16)
    return high, low


def split3(value):
    high = value.astype(jnp.bfloat16)
    rest = value - high.astype(jnp.float32)
    middle = rest.astype(jnp.bfloat16)
    return high, middle, (rest - middle.astype(jnp.float32)).astype(jnp.bfloat16)


def inverse_steps(a, start, stop):
    size = a.shape[0]
    sub = lax.broadcasted_iota(jnp.int32, (8, size), 0)
    lane = lax.broadcasted_iota(jnp.int32, (8, size), 1)
    rows = lax.broadcasted_iota(jnp.int32, (size, size), 0)
    lanes = lax.broadcasted_iota(jnp.int32, (size, size), 1)

    def row(value, index):
        return jnp.broadcast_to(value[index : index + 1], value.shape)

    def block(step, a):
        top = a[:8]
        columns = [jnp.broadcast_to(top[:, c : c + 1], (8, size)) for c in range(8)]
        panel = jnp.where(lane < 8, jnp.where(lane == sub, 1.0, 0.0), top)
        scale = jnp.zeros((8, size), jnp.float32)
        for c in range(8):
            inverse_root = lax.rsqrt(row(columns[c], c))
            scale = jnp.where(sub == c, inverse_root, scale)
            factor = jnp.where(sub > c, columns[c] * (inverse_root * inverse_root), 0.0)
            panel = panel - factor * row(panel, c)
            for j in range(c + 1, 8):
                columns[j] = columns[j] - factor * row(columns[j], c)
        square = scale * scale
        solved = panel * square
        for c in range(7, 0, -1):
            solved = solved - jnp.where(sub < c, columns[c] * square, 0.0) * row(solved, c)
        active = rows < size - 8 * step
        source = jnp.where(active, a, 0.0)[8:]
        rest = jnp.where(active & (lanes < 8), 0.0, a)[8:]
        for c in range(8):
            rest = rest - jnp.broadcast_to(source[:, c : c + 1], rest.shape) * jnp.broadcast_to(
                solved[c : c + 1], rest.shape
            )
        return pltpu.roll(jnp.concatenate([rest, panel * scale], axis=0), size - 8, 1)

    return lax.fori_loop(start, stop, block, a)


def unit_diagonal(gram):
    rows = lax.broadcasted_iota(jnp.int32, gram.shape, 0)
    lanes = lax.broadcasted_iota(jnp.int32, gram.shape, 1)
    diagonal = jnp.where(rows == lanes, gram, 0.0)
    across = lax.rsqrt(jnp.sum(diagonal, axis=0, keepdims=True))
    down = lax.rsqrt(jnp.sum(diagonal, axis=1, keepdims=True))
    return gram * across * down, across

def eliminate(blocks, k):
    size = blocks[0].shape[1]
    sub = lax.broadcasted_iota(jnp.int32, (8, size), 0)
    lane = lax.broadcasted_iota(jnp.int32, (8, size), 1) - 8 * k
    here = (lane >= 0) & (lane < 8)

    def row(value, index):
        return jnp.broadcast_to(value[index : index + 1], value.shape)

    def column(value, index):
        return jnp.broadcast_to(value[:, 8 * k + index : 8 * k + index + 1], value.shape)

    top = blocks[k]
    columns = [column(top, c) for c in range(8)]
    e = {(i, j): row(columns[j], i) for j in range(8) for i in range(j, 8)}
    panel = jnp.where(here, jnp.where(lane == sub, 1.0, 0.0), top)
    x = [row(panel, i) for i in range(8)]
    y, z, f = [None] * 8, [None] * 8, {}
    for p in range(0, 8, 2):
        a, b, c = e[p, p], e[p + 1, p], e[p + 1, p + 1]
        root = lax.rsqrt(a * c - b * b)
        inverse = root * root
        g = {}
        for i in range(p + 2, 8):
            g[i] = (e[i, p] * c - e[i, p + 1] * b, e[i, p + 1] * a - e[i, p] * b)
        for i in range(p + 2, 8):
            for j in range(p + 2, i + 1):
                e[i, j] = e[i, j] - (g[i][0] * e[j, p] + g[i][1] * e[j, p + 1]) * inverse
        for i in range(p + 2, 8):
            f[i, p], f[i, p + 1] = g[i][0] * inverse, g[i][1] * inverse
            x[i] = x[i] - (f[i, p] * x[p] + f[i, p + 1] * x[p + 1])
        first = lax.rsqrt(a)
        y[p] = x[p] * first
        y[p + 1] = (x[p + 1] * a - b * x[p]) * (first * root)
        z[p] = (c * x[p] - b * x[p + 1]) * inverse
        z[p + 1] = (a * x[p + 1] - b * x[p]) * inverse
    for p in (4, 2, 0):
        for i in range(p + 2, 8):
            z[p] = z[p] - f[i, p] * z[i]
            z[p + 1] = z[p + 1] - f[i, p + 1] * z[i]
    done = y[0]
    for i in range(1, 8):
        done = jnp.where(sub == i, y[i], done)
    out = list(blocks)
    out[k] = done
    for r in range(k + 1, len(blocks)):
        rest = jnp.where(here, 0.0, blocks[r])
        for c in range(8):
            rest = rest - column(blocks[r], c) * z[c]
        out[r] = rest
    return out


def lower(a, start=0):
    rows = lax.broadcasted_iota(jnp.int32, a.shape, 0) + start
    lanes = lax.broadcasted_iota(jnp.int32, a.shape, 1)
    return jnp.where(rows >= lanes, a, 0.0)


def remote(src, dst, send_sem, recv_sem, device):
    return pltpu.make_async_remote_copy(
        src_ref=src, dst_ref=dst, send_sem=send_sem, recv_sem=recv_sem, device_id=device, device_id_type=MESH
    )


def widths(cols):
    group = 256 if cols % 256 == 0 else cols
    chunk = 128 if group % 128 == 0 else group
    return group, chunk


def factors(shape, momentum_ref, gradient_ref, prior_ref, mixed, pair_ref, following_ref, right_ref, raw, wide_high, wide_low, prior_vmem, prior_pair, left, core_in, plane_in, whole, fine, turned, sums, totals,
            arrive, pieces, piece_in, piece_z, piece_all, squares, work, load_sem, prior_sem, core_recv, once,
            gram_send, gram_recv, chain_send, chain_recv):
    rows, cols = mixed.shape
    rank = prior_ref.shape[1]
    depth, dp = shape["shard"], shape["dp"]
    cores = 2 if shape["tensor"] % 2 == 0 else 1
    nx = shape["tensor"] // cores
    chips = nx * dp
    plane = chips * cores
    own = rows // plane
    s, t, y = lax.axis_index("shard"), lax.axis_index("tensor"), lax.axis_index("dp")
    core, x = lax.rem(t, cores), lax.div(t, cores)
    me = t * dp + y

    def chip(offset):
        px = lax.rem(x + lax.div(offset, dp), nx)
        py = lax.rem(y + lax.rem(offset, dp), dp)
        return px * dp + py, {"tensor": px * cores + core, "dp": py}

    def place(half, index):
        return pl.ds(pl.multiple_of((half * chips + index) * own, 8), own)

    def peer(k):
        other = lax.rem(me + k, plane)
        return other, {"tensor": lax.div(other, dp), "dp": lax.rem(other, dp)}

    def across(k):
        other = lax.rem(s + k, depth)
        return other, {"shard": other}

    partner = {"tensor": x * cores + cores - 1 - core}

    def load(slot, at):
        return (
            pltpu.make_async_copy(momentum_ref.at[at], mixed.at[at], load_sem.at[0, lax.rem(slot, AHEAD)]),
            pltpu.make_async_copy(gradient_ref.at[at], raw.at[at], load_sem.at[1, lax.rem(slot, AHEAD)]),
        )

    loads = chips * cores

    def spot(slot):
        i = lax.div(slot, cores)
        half = lax.rem(core + 1 + lax.rem(slot, cores), cores)
        return place(half, chip(chips - 1 - i)[0])

    prior_copy = pltpu.make_async_copy(prior_ref, prior_vmem, prior_sem)
    for slot in range(min(AHEAD, loads)):
        for copy in load(slot, spot(slot)):
            copy.start()
        if slot == 0:
            prior_copy.start()

    barrier = pltpu.get_barrier_semaphore()
    for k in range(1, plane):
        pl.semaphore_signal(barrier, inc=1, device_id=peer(k)[1], device_id_type=MESH)
    for k in range(1, depth):
        pl.semaphore_signal(barrier, inc=1, device_id=across(k)[1], device_id_type=MESH)

    half_depth = max(depth // 2, 1)
    first = s < half_depth
    level = jnp.where(first, s, depth - 1 - s)
    outer = level > 0
    middle = level == half_depth - 1
    step_in = jnp.where(first, 1, -1)
    group, chunk = widths(cols)
    count = cols // chunk

    prior_copy.wait()
    high, low = split(prior_vmem[...])
    prior_pair[:, :rank] = high
    prior_pair[:, rank:] = low
    pl.semaphore_wait(barrier, plane + depth - 2)

    def product(slot, at):
        for copy in load(slot, at):
            copy.wait()
        ahead = slot + AHEAD

        @pl.when(ahead < loads)
        def _():
            for copy in load(ahead, spot(ahead)):
                copy.start()

        value = mixed[at, :] + raw[at, :].astype(jnp.float32)
        mixed[at, :] = value
        high, low = split(value)
        wide_high[at, :] = high
        wide_low[at, :] = low
        both = dot(high, prior_pair[...], NORMAL) + dot(low, prior_pair[...], NORMAL)
        return both[:, :rank] + both[:, rank:]

    def core_copy(i):
        at = place(cores - 1 - core, chip(chips - 1 - i)[0])
        return remote(left.at[at], core_in.at[i], once.at[0], core_recv.at[i], partner)

    def plane_copy(offset):
        index, device = chip(offset)
        slot = offset - 1
        return remote(left.at[place(core, index)], plane_in.at[slot], once.at[1], once.at[2], device)

    def bulk(first):
        return remote(plane_in, plane_in, once.at[first], once.at[first + 1], chip(1)[1])

    def settle(i):
        offset = chips - 1 - i
        at = place(core, chip(offset)[0])
        if cores == 2:
            core_copy(i).wait_recv()
            left[at, :] = left[at, :] + core_in[i]
        return offset

    def partial(slot, carry):
        i = lax.div(slot, cores)
        at = spot(slot)
        left[at, :] = product(slot, at)
        if cores == 2:

            @pl.when(lax.rem(slot, cores) == 0)
            def _():
                core_copy(i).start()

        @pl.when(jnp.logical_and(lax.rem(slot, cores) == 0, slot > 0))
        def _():
            plane_copy(settle(i - 1)).start()

        return carry

    with jax.named_scope("p1_left"):
        lax.fori_loop(0, loads, partial, 0)

    mine = place(core, x * dp + y)
    with jax.named_scope("p3_rswait"):
        settle(chips - 1)
        total = left[mine, :]
        if chips > 1:
            bulk(1).wait_recv()
        for offset in range(1, chips):
            total = total + plane_in[offset - 1]
        whole[mine, :] = total

    piece = rank // plane

    def summed(slots, n):
        value = slots[0]
        for i in range(1, n):
            value = value + slots[i]
        return value

    def gram_sends(turn, stage, n, find, source, target):
        for k in range(1, n):
            other, device = find(k)
            remote(source(other), target, gram_send.at[turn, stage], gram_recv.at[turn, stage], device).start()

    def gram_wait(turn, stage, n, find, slots):
        if n > 1:
            part = slots.at[turn, pl.ds(0, n - 1)]
            remote(part, part, gram_send.at[turn, stage], gram_recv.at[turn, stage], find(1)[1]).wait()

    def gram_start(turn, gram):
        for i in range(plane):
            pieces[turn, i] = gram[i * piece : (i + 1) * piece]
        piece_in[turn, me] = pieces[turn, me]
        gram_sends(turn, 0, plane, peer, lambda i: pieces.at[turn, i], piece_in.at[turn, me])

    def gram_across(turn):
        gram_wait(turn, 0, plane, peer, piece_in)
        piece_z[turn, s] = summed(piece_in.at[turn], plane)
        mine_z = piece_z.at[turn, s]
        gram_sends(turn, 1, depth, across, lambda i: mine_z, mine_z)

    def gram_spread(turn):
        gram_wait(turn, 1, depth, across, piece_z)
        piece_all[turn, me] = summed(piece_z.at[turn], depth)
        mine_all = piece_all.at[turn, me]
        gram_sends(turn, 2, plane, peer, lambda i: mine_all, mine_all)

    def gram_whole(turn):
        gram_wait(turn, 2, plane, peer, piece_all)
        return jnp.concatenate([piece_all[turn, i] for i in range(plane)], axis=0)

    with jax.named_scope("p4_gram"):
        gram_start(0, dot(total, total, ROWS, HIGHEST))
    for offset in range(1, chips):
        remote(whole.at[mine], whole.at[mine], once.at[3], once.at[4], chip(offset)[1]).start()
    with jax.named_scope("p5_gram1"):
        gram_across(0)
    with jax.named_scope("p6_gram2"):
        gram_spread(0)
    with jax.named_scope("p7_agwait"):
        if chips > 1:
            bulk(1).wait_send()
            bulk(3).wait()
        if cores == 2:
            at = pl.ds(pl.multiple_of(core * (rows // 2), 8), rows // 2)
            remote(left.at[at], left.at[at], once.at[0], once.at[0], partner).wait_send()
            half_copy = remote(whole.at[at], whole.at[at], once.at[5], once.at[6], partner)
            half_copy.start()
    with jax.named_scope("p8_gram3"):
        gram = gram_whole(0)
    parts = 2 if rank % 16 == 0 else 1
    tall = rank // parts
    units = count * parts
    blocks = rank // 8
    per = group // chunk
    groups = cols // group

    def unit(ref, u):
        return ref.at[u % count, pl.ds((u // count) * tall, tall)]

    def inward(u):
        slot = jnp.where(middle, 1, 0)
        return remote(unit(sums, u), unit(arrive.at[slot], u), chain_send.at[0], chain_recv.at[slot, u],
                      {"shard": s + step_in})

    def outward(u):
        return remote(unit(totals, u), unit(arrive.at[1], u), chain_send.at[1], chain_recv.at[1, u],
                      {"shard": s - step_in})

    def landed(slot, u):
        remote(unit(sums, u), unit(arrive.at[slot], u), chain_send.at[0], chain_recv.at[slot, u],
               {"shard": s + step_in}).wait_recv()

    def near(u):
        landed(0, u)
        unit(sums, u)[...] = unit(sums, u)[...] + unit(arrive.at[0], u)[...]
        inward(u).start()

    def far(u, forward):
        if depth > 1:
            landed(1, u)
            got = unit(arrive.at[1], u)[...]
            unit(totals, u)[...] = jnp.where(middle, unit(sums, u)[...] + got, got)
            if forward:
                outward(u).start()
        else:
            unit(totals, u)[...] = unit(sums, u)[...]

    def due(step, u):
        late = 0.0 if u < count else 1.7 if 2 * u < 3 * count else 2.4
        return u + late + (GAP if step is far else 0.0)

    queue = sorted(((step, u) for u in range(units) for step in (near, far)), key=lambda item: due(*item))

    def take(n, computed):
        steps = []
        while len(steps) < n and len(queue) > 1 and queue[0][1] < computed:
            steps.append(queue.pop(0))
        if depth > 2 and steps:

            @pl.when(outer)
            def _():
                for step, u in steps:
                    with jax.named_scope(f"q3_{step.__name__}{u}"):
                        step(u, True) if step is far else step(u)

    def basis_half(r, w):
        for i in range(STEPS):
            block = rows // STEPS
            at = slice(i * block, (i + 1) * block)
            if r == 0:
                high, middle_part, low = split3(whole[at, :])
                fine[0, at, :rank] = high
                fine[0, at, rank:] = middle_part
                fine[1, at, :rank] = high
                fine[1, at, rank:] = low
            value = value_of(w, fine[0, at, :], fine[1, at, :])
            high, low = split(value)
            turned[r, :tall, at] = high
            turned[r, tall:, at] = low

    def value_of(w, block, tail_block):
        w_high, w_middle, w_low = split3(w)
        ends = jnp.concatenate(
            [jnp.concatenate([w_high, w_middle], axis=1), jnp.concatenate([w_middle, w_high], axis=1)], axis=0
        )
        both = dot(ends, block, TURNED)
        return both[:tall] + (both[tall:] + dot(jnp.concatenate([w_low, w_high], axis=1), tail_block, TURNED))

    def right_group(r, g):
        at = slice(g * group, (g + 1) * group)
        both = dot(turned[r], wide_high[:, at], NORMAL)
        value = both[:tall] + both[tall:] + dot(turned[r, :tall, :], wide_low[:, at], NORMAL)
        for i in range(per):
            sums[g * per + i, r * tall : (r + 1) * tall, :] = value[:, i * chunk : (i + 1) * chunk]

    def right_send(r, g):
        if depth > 1:

            @pl.when(jnp.logical_not(outer))
            def _():
                for i in range(per):
                    inward(r * count + g * per + i).start()

    with jax.named_scope("p9_inv1"):
        scaled, lanes = unit_diagonal(gram)
        rest = [scaled[8 * i : 8 * i + 8] for i in range(blocks)]
        weights = []
    for r in range(parts):
        with jax.named_scope(f"p9_half{r}"):
            first_block, stop = r * blocks // parts, (r + 1) * blocks // parts
            for k in range(first_block, stop):
                rest = eliminate(rest, k)
                if r > 0 and k == first_block + 5:
                    take(1, r * count)
            weights.append(lower(jnp.concatenate(rest[first_block:stop], axis=0), 8 * first_block) * lanes)
        last_part = r == parts - 1
        if last_part:
            take(1, r * count)
            with jax.named_scope("q1_gram"):
                if r == 0 and cores == 2:
                    half_copy.wait()
                high, middle_part, low = split3(whole[mine, :])
                block = jnp.concatenate([high, middle_part], axis=1)
                tail_block = jnp.concatenate([high, low], axis=1)
                part = jnp.concatenate([value_of(w, block, tail_block) for w in weights], axis=0)
                gram_start(1, dot(part, part, TURNED, HIGHEST))
            take(MOVES[0], r * count)
        with jax.named_scope(f"q0_value{r}"):
            if cores == 2 and r == 0 and not last_part:
                half_copy.wait()
            basis_half(r, weights[r])
        if last_part:
            take(MOVES[1], r * count)
        for g in range(groups):
            with jax.named_scope(f"q2_right{r}{g}"):
                right_group(r, g)
            if last_part and g == min(2, groups - 1):
                with jax.named_scope("q2_gram1"):
                    gram_across(1)
            right_send(r, g)
            if last_part:
                take(MOVES[2 + min(g, 3)], r * count + (g + 1) * per)

    def second():
        with jax.named_scope("q4_gram3"):
            scaled, across_lanes = unit_diagonal(gram_whole(1))
        return [scaled[8 * i : 8 * i + 8] for i in range(blocks)], across_lanes

    def invert(rest, start, stop):
        with jax.named_scope("q5_inv2"):
            for k in range(start, stop):
                rest = eliminate(rest, k)
        return rest

    def keep(rest, across_lanes):
        work[...] = lower(jnp.concatenate(rest, axis=0)) * across_lanes

    def basis():
        with jax.named_scope("q6_basis"):
            high, low = split(work[...])
            pair = jnp.concatenate([high, low], axis=1)
            for i in range(STEPS):
                block = rows // STEPS
                at = slice(i * block, (i + 1) * block)
                top = jnp.concatenate([turned[r, :tall, at] for r in range(parts)], axis=0)
                bottom = jnp.concatenate([turned[r, tall:, at] for r in range(parts)], axis=0)
                value = dot(pair, jnp.concatenate([top, top], axis=0), NORMAL) + dot(high, bottom, NORMAL)
                high_t, low_t = split(value.T)
                pair_ref[at, :rank] = high_t
                pair_ref[at, rank:] = low_t

    def correct(start, stop):
        with jax.named_scope("q7_right"):
            wide = jnp.concatenate([totals[c] for c in range(start, stop)], axis=1)
            value = dot(wide, work[...], ((0,), (1,)), HIGHEST)
            right_ref[start * chunk : stop * chunk, :] = value
            column = jnp.sum(value * value, axis=0, keepdims=True)
            squares[me] = squares[me] + jnp.broadcast_to(column, (8, rank))

    squares[me] = jnp.zeros((8, rank), jnp.float32)

    @pl.when(outer)
    def _():
        plan = list(queue)
        second_at = next((i for i, (step, u) in enumerate(plan) if step is near and 2 * u >= 3 * count), 0)
        third_at = next((i for i, (step, u) in enumerate(plan) if step is far and u >= THIRD), len(plan) - 1)
        third_at = max(third_at, second_at)
        at = 0
        for i, (step, u) in enumerate(plan):
            if i == second_at:
                with jax.named_scope("q4_gram2"):
                    gram_spread(1)
            with jax.named_scope(f"q3_{step.__name__}{u}"):
                far(u, True) if step is far else near(u)
            if i == third_at:
                rest, across_lanes = second()
            if i >= third_at and step is far:
                stop = blocks if i == len(plan) - 1 else min(at + SHARE, blocks)
                rest = invert(rest, at, stop)
                at = stop
        keep(rest, across_lanes)
        for c in range(0, count, 2):
            correct(c, min(c + 2, count))

    @pl.when(jnp.logical_not(outer))
    def _():
        with jax.named_scope("q4_gram2"):
            gram_spread(1)
        rest, across_lanes = second()
        keep(invert(rest, 0, blocks), across_lanes)
        for u in range(units):
            with jax.named_scope(f"q3_end{u}"):
                far(u, False)
            if u == units - 1 - 2 * per:
                for c in range(0, count - 2 * per, 2):
                    correct(c, c + 2)
        for c in range(max(count - 2 * per, 0) if count > 2 * per else 0, count, 2):
            correct(c, min(c + 2, count))

    with jax.named_scope("q8_squares"):
        for k in range(1, plane):
            remote(squares.at[me], squares.at[me], once.at[7], once.at[8], peer(k)[1]).start()
    basis()
    with jax.named_scope("q9_momentum"):
        scaled = (right_ref[...] * (decay_rate - 1.0)).astype(jnp.bfloat16)

        def update(i, carry):
            block = rows // STEPS
            at = pl.ds(pl.multiple_of(i * block, 8), block)
            mixed[at, :] = mixed[at, :] + dot(pair_ref[at, :rank], scaled, TURNED)
            return carry

        lax.fori_loop(0, STEPS, update, 0)
    with jax.named_scope("r0_follow"):
        if plane > 1:
            part = squares.at[pl.ds(0, plane - 1)]
            remote(part, part, once.at[7], once.at[8], peer(1)[1]).wait()
        mean = summed(squares, plane)[:1] / (cols * plane)
        following_ref[...] = right_ref[...] / jnp.sqrt(mean + epsilon)
        if depth > 1:
            remote(sums, sums, chain_send.at[0], chain_recv.at[0, 0], {"shard": s + step_in}).wait_send()

            @pl.when(outer)
            def _():
                remote(totals, totals, chain_send.at[1], chain_recv.at[0, 0], {"shard": s - step_in}).wait_send()


def finish(scale, mixed_ref, pair_ref, following_ref, next_ref, direction_ref, out_ref, direction_vmem, sems):
    rows = mixed_ref.shape[0]
    rank = following_ref.shape[1]
    block = rows // STEPS
    moves = (
        pltpu.make_async_copy(mixed_ref, next_ref, sems.at[0]),
        pltpu.make_async_copy(following_ref, out_ref, sems.at[1]),
    )
    for copy in moves:
        copy.start()
    high, low = split(following_ref[...] * scale)
    follow = jnp.concatenate([high, high], axis=1)
    for i in range(STEPS):
        at = pl.ds(i * block, block)
        value = dot(pair_ref[at, :], follow, TURNED) + dot(pair_ref[at, :rank], low, TURNED)
        direction_vmem[at, :] = value.astype(jnp.bfloat16)
        pltpu.make_async_copy(direction_vmem.at[at], direction_ref.at[at], sems.at[2]).start()
    for copy in moves:
        copy.wait()
    pltpu.make_async_copy(direction_vmem, direction_ref, sems.at[2]).wait()


def shards(shape, gradient, momentum, prior_right_factor):
    gradient, momentum, prior = gradient[0], momentum[0], prior_right_factor[0]
    rows, cols = momentum.shape
    rank = prior.shape[1]
    z = shape["shard"]
    plane = shape["tensor"] * shape["dp"]
    cores = 2 if shape["tensor"] % 2 == 0 else 1
    chips = plane // cores
    own = rows // plane
    group, chunk = widths(cols)
    count = cols // chunk
    parts = 2 if rank % 16 == 0 else 1
    dma = pltpu.SemaphoreType.DMA
    vmem = pl.BlockSpec(memory_space=pltpu.VMEM)
    hbm = pl.BlockSpec(memory_space=pltpu.HBM)
    f32, bf16 = jnp.float32, jnp.bfloat16
    others = max(chips - 1, 1)
    mixed, pair, following = pl.pallas_call(
        functools.partial(factors, shape),
        out_shape=[
            pltpu.VMEM((rows, cols), f32),
            pltpu.VMEM((rows, 2 * rank), bf16),
            pltpu.VMEM((cols, rank), f32),
        ],
        in_specs=[hbm, hbm, hbm],
        out_specs=[vmem, vmem, vmem],
        scratch_shapes=[
            pltpu.VMEM((cols, rank), f32),
            pltpu.VMEM((rows, cols), bf16),
            pltpu.VMEM((rows, cols), bf16),
            pltpu.VMEM((rows, cols), bf16),
            pltpu.VMEM((cols, rank), f32),
            pltpu.VMEM((cols, 2 * rank), bf16),
            pltpu.VMEM((rows, rank), f32),
            pltpu.VMEM((chips, own, rank), f32),
            pltpu.VMEM((others, own, rank), f32),
            pltpu.VMEM((rows, rank), f32),
            pltpu.VMEM((2, rows, 2 * rank), bf16),
            pltpu.VMEM((parts, 2 * rank // parts, rows), bf16),
            pltpu.VMEM((count, rank, chunk), f32),
            pltpu.VMEM((count, rank, chunk), f32),
            pltpu.VMEM((2, count, rank, chunk), f32),
            pltpu.VMEM((2, plane, rank // plane, rank), f32),
            pltpu.VMEM((2, plane, rank // plane, rank), f32),
            pltpu.VMEM((2, z, rank // plane, rank), f32),
            pltpu.VMEM((2, plane, rank // plane, rank), f32),
            pltpu.VMEM((plane, 8, rank), f32),
            pltpu.VMEM((rank, rank), f32),
            dma((2, AHEAD)),
            dma,
            dma((chips,)),
            dma((9,)),
            dma((2, 3)),
            dma((2, 3)),
            dma((2,)),
            dma((2, 2 * count)),
        ],
        compiler_params=pltpu.CompilerParams(
            collective_id=0, has_side_effects=True, vmem_limit_bytes=36 * MiB
        ),
        name="factors",
    )(*(pltpu.with_memory_space_constraint(x, pltpu.HBM) for x in (momentum, gradient, prior)))

    scale = float((rows * z / rank) ** 0.5)
    momentum_next, direction, following = pl.pallas_call(
        functools.partial(finish, scale),
        out_shape=[
            jax.ShapeDtypeStruct((rows, cols), f32),
            jax.ShapeDtypeStruct((rows, cols), bf16),
            jax.ShapeDtypeStruct((cols, rank), f32),
        ],
        in_specs=[vmem, vmem, vmem],
        out_specs=[hbm, hbm, hbm],
        scratch_shapes=[pltpu.VMEM((rows, cols), bf16), dma((3,))],
        compiler_params=pltpu.CompilerParams(vmem_limit_bytes=24 * MiB),
        name="finish",
    )(mixed, pair, following)
    return momentum_next[None], following[None], direction[None]


def solution(mesh):
    return jax.shard_map(
        functools.partial(shards, dict(mesh.shape)),
        mesh=mesh,
        in_specs=(
            P(None, "shard", ("tensor", "dp")),
            P(None, "shard", ("tensor", "dp")),
            P(None, ("tensor", "dp"), None),
        ),
        out_specs=(
            P(None, "shard", ("tensor", "dp")),
            P(None, ("tensor", "dp"), None),
            P(None, "shard", ("tensor", "dp")),
        ),
        check_vma=False,
    )
```
